32 devices in a mesh: qx: 8 (over z, y), qy: 4 (over x, core).
Axes of the slice: x: 2, y: 2, z: 4, core: 2. Of those that a mesh axis runs over, the one named last changes fastest.
Arguments:
- vectors: bfloat16 [64, 256, 512], P(None, 'qx', 'qy'), may hold values from -6 to 6
- near_tiles: bfloat16 [16, 32, 3, 256, 256], P('qx', 'qy'), may hold values from -0.21875 to 0.21875
- near_offset: int32 [16, 32, 3], P('qx', 'qy'), may hold values from 0 to 8, as said below
- col_basis: bfloat16 [16, 32, 64, 256], P('qx', 'qy'), may hold values from -0.375 to 0.375
- row_basis: bfloat16 [16, 32, 64, 256], P('qx', 'qy'), may hold values from -0.375 to 0.375
- up_transfer: float32 [16, 32, 64, 64], P('qx', 'qy'), may hold values from -0.375 to 0.375
- down_transfer: float32 [16, 32, 64, 64], P('qx', 'qy'), may hold values from -0.75 to 0.75
- coupling: float32 [32, 128, 64, 64], P(('qx', 'qy')), may hold values from -0.75 to 0.75
- couple_dest: int32 [32, 128], replicated, may hold values from -1 to 31, as said below
- couple_target: int32 [32, 128], replicated, may hold values from 0 to 19, as said below
Outputs:
- product: float32 [64, 256, 512], P(None, 'qx', 'qy')
The draws below stay inside these ranges and needn't reach their ends.
Inputs may be any that keep to these rules, and one draw needn't show every extreme that they name: `couple_dest`: in each row (source device) no destination device appears more than 4 times; in every draw one destination device appears exactly 4 times in every row; -1 marks a padded slot. `couple_target`: slots below 96 name a leaf cluster (0 to 15), the others a parent cluster (16 to 19) of the target device. `near_offset`: the 3 codes of a leaf are distinct; code o reads the leaf at offset (o // 3 - 1, o % 3 - 1).
All inputs are finite; a program needn't handle non-finite values.
Results may differ from the reference program's by a relative error of at most 0.0003.
Values may be sent and summed in bfloat16 or wider, within the bound.
A program may use at most 64 MiB of HBM per device.

```python
import jax
import jax.numpy as jnp
from jax import lax

R = 64
VECS = 64
LS = 16
NEAR = 3
K0 = 6
K1 = 8
CY = 128
LP = 256
LEAVES_DEV = 16
L1_DEV = 4
CLUSTERS = 20
SLOTS = 128
CAP = 4
NX = 256
NY = 512
GX = 16
GY = 32
N_QX = 8
N_QY = 4
DEVICES = 32


def draw_couple_dest(key, part):
    key = jax.random.fold_in(key, 101)
    key_hot, key_order, key_shuffle, key_live = jax.random.split(key, 4)
    total = DEVICES * CAP
    hot_device = jax.random.randint(key_hot, (), 0, DEVICES)
    ident = jnp.arange(total, dtype=jnp.int32)
    owner = ident // CAP
    scores = jax.random.randint(key_order, (DEVICES, total), 0, 1 << 20) * total + ident[None, :]
    scores = jnp.where(owner[None, :] == hot_device, ident[None, :] - total, scores)
    chosen = jnp.argsort(scores, axis=1)[:, :SLOTS].astype(jnp.int32)
    dest = chosen // CAP
    slot_ident = jnp.arange(SLOTS, dtype=jnp.int32)
    shuffle = jnp.argsort(jax.random.randint(key_shuffle, (DEVICES, SLOTS), 0, 1 << 20) * SLOTS + slot_ident[None, :], axis=1).astype(jnp.int32)
    dest = jnp.take_along_axis(dest, shuffle, axis=1)
    live = (jax.random.randint(key_live, (DEVICES, SLOTS), 0, 20) >= 3) | (dest == hot_device)
    return jnp.where(live, dest, -1).astype(jnp.int32)


def draw_couple_target(key, part):
    key = jax.random.fold_in(key, 202)
    drawn = jax.random.randint(key, (DEVICES, SLOTS), 0, 1 << 20)
    column = jnp.arange(SLOTS, dtype=jnp.int32)[None, :]
    leaf_part = column < LEAVES_DEV * K0
    return jnp.where(leaf_part, drawn % LEAVES_DEV, LEAVES_DEV + drawn % L1_DEV).astype(jnp.int32)


def draw_near_offset(key, part):
    key = jax.random.fold_in(key, 303)
    scores = jax.random.randint(key, (GX, GY, 9), 0, 1 << 20) * 9 + jnp.arange(9, dtype=jnp.int32)
    return jnp.argsort(scores, axis=2)[:, :, :NEAR].astype(jnp.int32)


def levels(own_key, extent, cuts, low, largest):
    gain = 1.0
    for position, blocks in cuts:
        draws = jax.random.uniform(jax.random.fold_in(jax.random.fold_in(own_key, 6), position), (blocks,), jnp.float32, low / len(cuts), largest / len(cuts))
        gain = gain * jnp.repeat(jnp.exp(draws), extent[position] // blocks).reshape((-1,) + (1,) * (len(extent) - 1 - position))
    return gain


def bell_draw(own_key, dims, deviation, bound, cuts=(), kind=jnp.bfloat16):
    values = jax.random.normal(own_key, dims, jnp.float32) * deviation
    if len(cuts) > 0:
        values = levels(own_key, dims, cuts, -0.22, 0.18) * values
    return jnp.clip(values, min=-bound, max=bound).astype(kind)


def setup_inputs(seed: int = 0) -> dict:
    key_list = jax.random.split(jax.random.key(seed), 11)
    vectors = bell_draw(key_list[0], (VECS, NX, NY), 1.0, 6.0, ((1, 8), (2, 4)))
    near_tiles = bell_draw(key_list[1], (GX, GY, NEAR, LP, LP), (NEAR * LP) ** -0.5, 0.21875, ((0, 8), (1, 4)))
    near_offset = draw_near_offset(jax.random.fold_in(key_list[10], 71), 0)
    col_basis = bell_draw(key_list[3], (GX, GY, R, LP), LP ** -0.5, 0.375, ((0, 8), (1, 4)))
    row_basis = bell_draw(key_list[4], (GX, GY, R, LP), LP ** -0.5, 0.375, ((0, 8), (1, 4)))
    up_transfer = bell_draw(key_list[5], (GX, GY, R, R), (4 * R) ** -0.5, 0.375, ((0, 8), (1, 4)), jnp.float32)
    down_transfer = bell_draw(key_list[6], (GX, GY, R, R), R ** -0.5, 0.75, ((0, 8), (1, 4)), jnp.float32)
    coupling = bell_draw(key_list[7], (DEVICES, SLOTS, R, R), R ** -0.5, 0.75, ((0, 32),), jnp.float32)
    couple_dest = draw_couple_dest(jax.random.fold_in(key_list[10], 71), 0)
    couple_target = draw_couple_target(jax.random.fold_in(key_list[10], 71), 0)
    return dict(vectors=vectors, near_tiles=near_tiles, near_offset=near_offset, col_basis=col_basis, row_basis=row_basis, up_transfer=up_transfer, down_transfer=down_transfer, coupling=coupling, couple_dest=couple_dest, couple_target=couple_target)


def reference(vectors, near_tiles, near_offset, col_basis, row_basis, up_transfer, down_transfer, coupling, couple_dest, couple_target):
    precise = lax.Precision.HIGHEST
    grid_x = NX // LS
    grid_y = NY // LS
    leaf_y = CY // LS
    devices = N_QX * N_QY
    blocks = vectors.reshape(VECS, grid_x, LS, grid_y, LS).transpose(1, 3, 0, 2, 4).reshape(grid_x, grid_y, VECS, LP)
    leaf_coef = jnp.einsum('ijrp,ijvp->ijrv', col_basis.astype(jnp.float32), blocks.astype(jnp.float32), precision=precise)
    lifted = jnp.einsum('ijrs,ijsv->ijrv', up_transfer, leaf_coef, precision=precise)
    upper_coef = lifted.reshape(grid_x // 2, 2, grid_y // 2, 2, R, VECS).sum(axis=(1, 3))
    leaf_dev = leaf_coef.reshape(N_QX, 2, N_QY, leaf_y, R, VECS).transpose(0, 2, 1, 3, 4, 5).reshape(devices, LEAVES_DEV, R, VECS)
    upper_dev = upper_coef.reshape(N_QX, N_QY, L1_DEV, R, VECS).reshape(devices, L1_DEV, R, VECS)

    def send_step(totals, device_item):
        leaf_part, upper_part, couple_block, dest_row, target_row = device_item
        source_coef = jnp.concatenate([jnp.repeat(leaf_part, K0, axis=0), jnp.repeat(upper_part, K1, axis=0)], axis=0)
        contrib = jnp.einsum('srt,stv->srv', couple_block, source_coef, precision=precise).reshape(SLOTS, R * VECS)
        segment_ids = jnp.where(dest_row >= 0, dest_row * CLUSTERS + target_row, devices * CLUSTERS).astype(jnp.int32)
        return totals.at[segment_ids].add(contrib), None

    totals = jnp.zeros((devices * CLUSTERS + 1, R * VECS), jnp.float32)
    totals, _ = lax.scan(send_step, totals, (leaf_dev, upper_dev, coupling, couple_dest, couple_target))
    gathered = totals[:devices * CLUSTERS].reshape(devices, CLUSTERS, R, VECS)
    down_leaf = gathered[:, :LEAVES_DEV].reshape(N_QX, N_QY, 2, leaf_y, R, VECS).transpose(0, 2, 1, 3, 4, 5).reshape(grid_x, grid_y, R, VECS)
    down_upper = gathered[:, LEAVES_DEV:].reshape(N_QX, N_QY * L1_DEV, R, VECS)
    expanded = jnp.repeat(jnp.repeat(down_upper, 2, axis=0), 2, axis=1)
    down_leaf = down_leaf + jnp.einsum('ijrs,ijsv->ijrv', down_transfer, expanded, precision=precise)
    far_out = jnp.einsum('ijrp,ijrv->ijvp', row_basis.astype(jnp.float32), down_leaf, precision=precise)

    padded = jnp.pad(vectors, ((0, 0), (LS, LS), (LS, LS)))
    padded_blocks = padded.reshape(VECS, grid_x + 2, LS, grid_y + 2, LS).transpose(1, 3, 0, 2, 4).reshape((grid_x + 2) * (grid_y + 2), VECS, LP)
    along_x = jnp.arange(grid_x, dtype=jnp.int32)[:, None, None]
    along_y = jnp.arange(grid_y, dtype=jnp.int32)[None, :, None]
    tile_index = ((along_x + near_offset // 3) * (grid_y + 2) + along_y + near_offset % 3).astype(jnp.int32)

    def near_row(leaf_row):
        tiles = near_tiles[leaf_row].astype(jnp.float32)
        picked = padded_blocks[tile_index[leaf_row]].astype(jnp.float32)
        return jnp.einsum('jkps,jkvs->jvp', tiles, picked, precision=precise)

    near_out = lax.map(near_row, jnp.arange(grid_x, dtype=jnp.int32))
    total_out = near_out + far_out
    return total_out.reshape(grid_x, grid_y, VECS, LS, LS).transpose(2, 0, 3, 1, 4).reshape(VECS, NX, NY)
```

```python
import jax
import jax.numpy as jnp
from jax import lax
from jax.experimental import pallas as pl
from jax.experimental.pallas import tpu as pltpu
from jax.sharding import PartitionSpec as P

LS = 16
K0 = 6
K1 = 8
KEYS = 32
STEP = 32767.0

ANY = pl.BlockSpec(memory_space=pl.ANY)
VM = pl.BlockSpec(memory_space=pltpu.VMEM)
SM = pl.BlockSpec(memory_space=pltpu.SMEM)
F32 = jnp.float32
BF16 = jnp.bfloat16
I32 = jnp.int32


def halves(value):
    high = value.astype(BF16)
    return high, (value - high.astype(F32)).astype(BF16)


def left_of(value):
    high, low = halves(value)
    return jnp.concatenate([high, low, high], axis=1)


def right_of(value):
    high, low = halves(value)
    return jnp.concatenate([high, high, low], axis=0)


def dot(left, right):
    return jnp.dot(left, right, preferred_element_type=F32)


def swapped(value):
    half = value.shape[-1] // 2
    return jnp.concatenate([value[..., half:], value[..., :half]], axis=-1)


def spread(first, second):
    low = lax.broadcasted_iota(I32, first.shape, 1) < first.shape[1] // 2
    return jnp.concatenate(
        [
            jnp.where(low, first, 0.0),
            jnp.where(low, swapped(first), 0.0),
            jnp.where(low, 0.0, swapped(second)),
            jnp.where(low, 0.0, second),
        ],
        axis=0,
    )


def twice(value):
    low = lax.broadcasted_iota(I32, value.shape, 1) < value.shape[1] // 2
    return jnp.concatenate([jnp.where(low, value, 0.0), jnp.where(low, 0.0, value)], axis=0)


def coded(blocks):
    peak = jnp.max(jnp.abs(blocks), axis=1)
    scale = (jnp.maximum(peak, 1e-30) * 1.004).astype(BF16).astype(F32)
    inverse = STEP / scale
    whole = jnp.round(blocks * inverse[:, None, :]).astype(I32).astype(jnp.int16)
    return whole, scale


def decoded(value):
    return value.astype(I32).astype(F32)


class Plan:
    def __init__(self, width_x, width_y, slots):
        part = max(1, width_y // 2)
        if width_x % part:
            part = 1
        self.width_x, self.width_y = width_x, width_y
        self.part = part
        self.group = part * width_y
        self.lines = width_x // part
        devices = width_x * width_y
        self.cap = (slots + devices - 1) // devices
        self.total = devices * self.cap
        self.each = self.group * self.cap
        self.scale_rows = -(-(self.lines * self.cap) // 16) * 16
        self.xor_line = self.lines & (self.lines - 1) == 0
        self.xor_group = self.group & (self.group - 1) == 0
        far = self.lines // 2
        self.order = [t for t in range(far, self.lines)] + [t for t in range(far - 1, 0, -1)] + [0]

    def line(self, z, t):
        return z ^ t if self.xor_line else lax.rem(z + t, self.lines)

    def line_step(self, z, other):
        return other ^ z if self.xor_line else lax.rem(other - z + self.lines, self.lines)

    def peer(self, j, u):
        return j ^ u if self.xor_group else lax.rem(j + u, self.group)


def tables(plan, clusters, dest_ref, target_ref, tab_ref):
    here_x = lax.axis_index("qx")
    me_z = lax.div(here_x, plan.part)
    me_j = lax.rem(here_x, plan.part) * plan.width_y + lax.axis_index("qy")
    slots = dest_ref.shape[1]
    cap, group, lines = plan.cap, plan.group, plan.lines
    own = dest_ref[pl.ds(me_z * group + me_j, 1), :]
    across = jnp.broadcast_to(own.astype(F32), (slots, slots))
    down = across.T
    row = lax.broadcasted_iota(I32, (slots, slots), 0)
    col = lax.broadcasted_iota(I32, (slots, slots), 1)
    order = jnp.sum(jnp.where((across == down) & (col < row), 1.0, 0.0), axis=1, keepdims=True)
    dest = down[:, :1].astype(I32)
    whole = jnp.maximum(dest, 0)
    step = plan.line_step(me_z, lax.div(whole, group))
    place = (step * group + lax.rem(whole, group)) * cap + order.astype(I32)
    place = jnp.where(dest >= 0, place, -1)
    lane = lax.broadcasted_iota(I32, (slots, plan.total), 1)
    slot = lax.broadcasted_iota(I32, (slots, plan.total), 0).astype(F32)
    slot_of = jnp.sum(jnp.where(place == lane, slot, 0.0), axis=0, keepdims=True)

    first = pl.multiple_of(me_z * group, group)
    dests = dest_ref[pl.ds(first, group), :]
    targets = target_ref[pl.ds(first, group), :].astype(F32)
    match = jnp.concatenate([dests == plan.line(me_z, t) * group + me_j for t in range(lines)], axis=0)
    target = jnp.concatenate([targets] * lines, axis=0)
    before = jnp.where(row < col, 1.0, 0.0).astype(BF16)
    rank_in = dot(jnp.where(match, 1.0, 0.0).astype(BF16), before)
    rows = lines * group
    step_row = lax.div(lax.broadcasted_iota(I32, (rows, 1), 0), group)
    from_row = lax.rem(lax.broadcasted_iota(I32, (rows, 1), 0), group)
    keys, blocks, scales = [], [], []
    for k in range(cap):
        landing = match & (rank_in == float(k))
        mine = clusters + jnp.sum(jnp.where(landing, target - clusters, 0.0), axis=1, keepdims=True)
        keys.append(mine + (step_row * KEYS).astype(F32))
        blocks.append((from_row * cap + k).astype(F32))
        scales.append((from_row * plan.scale_rows + step_row * cap + k).astype(F32))
    total = plan.total
    key_row = jnp.broadcast_to(jnp.concatenate(keys, axis=0), (total, total))
    key_col = key_row.T
    row = lax.broadcasted_iota(I32, (total, total), 0)
    col = lax.broadcasted_iota(I32, (total, total), 1)
    earlier = (key_row == key_col) & (col < row)
    rank = jnp.sum(jnp.where((key_col < key_row) | earlier, 1.0, 0.0), axis=1, keepdims=True)
    follows = jnp.max(jnp.where(earlier, 1.0, 0.0), axis=1, keepdims=True)
    hit = rank == col.astype(F32)

    def sorted_row(values):
        return jnp.sum(jnp.where(hit, values, 0.0), axis=0, keepdims=True)

    wide = lines * KEYS
    key = jnp.concatenate(keys, axis=0)
    place = lax.broadcasted_iota(I32, (total, wide), 1)
    code = place.astype(F32)
    last = jnp.sum(jnp.where(key <= code, 1.0, 0.0), axis=0, keepdims=True) - 1.0
    last = last - (lax.div(place[:1], KEYS) * plan.each).astype(F32)
    last = jnp.clip(last, 0.0, plan.each - 1.0)
    there = jnp.max(jnp.where(key == code, 1.0, 0.0), axis=0, keepdims=True)
    tab_ref[0:1, :total] = slot_of.astype(I32)
    tab_ref[1:2, :total] = sorted_row(jnp.concatenate(blocks, axis=0)).astype(I32)
    tab_ref[2:3, :total] = sorted_row(jnp.concatenate(scales, axis=0)).astype(I32)
    tab_ref[3:4, :total] = sorted_row(follows).astype(I32)
    tab_ref[4:5, :wide] = last.astype(I32)
    tab_ref[5:6, :wide] = there.astype(I32)


def kernel(plan, *refs):
    lines, group, cap = plan.lines, plan.group, plan.cap
    (
        vec_hbm, tiles_hbm, off_ref, col_hbm, row_hbm, up_hbm, down_hbm, coup_hbm, tab,
        out_ref,
        vec, tiles, col, row, up, down, coup,
        wide, halo, grid, strips, rim, mats, coef, held, held_scale,
        place_scale, send_scale, got_scale, scale_of, send1,
        run, own, send2, send2_scale, near, turned, lifts,
        load_sem, near_send, near_recv, scale_send, scale_recv,
        one_send, one_recv, two_send, two_recv, twos_send, twos_recv, local_sem,
        *landing,
    ) = refs
    recv1 = landing[:lines]
    recv2 = landing[lines : 2 * lines - 1]
    recv2_scale = landing[2 * lines - 1 :]

    here_x = lax.axis_index("qx")
    here_y = lax.axis_index("qy")
    me_z = lax.div(here_x, plan.part)
    me_j = lax.rem(here_x, plan.part) * plan.width_y + here_y
    vecs, rows_x, rows_y = vec.shape
    leaf_x, leaf_y = rows_x // LS, rows_y // LS
    leaves = leaf_x * leaf_y
    uppers = leaf_y // 2
    clusters = leaves + uppers
    rank = coup.shape[0]
    half = rank // 2
    lanes = 2 * vecs
    points = LS * LS
    low = lax.broadcasted_iota(I32, (1, lanes), 1) < vecs

    pairs = [(vec_hbm, vec), (col_hbm, col), (up_hbm, up), (coup_hbm, coup), (row_hbm, row), (down_hbm, down), (tiles_hbm, tiles)]
    loads = [pltpu.make_async_copy(src, dst, load_sem.at[n]) for n, (src, dst) in enumerate(pairs)]
    for load in loads:
        load.start()

    def at_line(t):
        other = plan.line(me_z, t)
        return other * plan.part + lax.div(me_j, plan.width_y), here_y

    def at_peer(u):
        other = plan.peer(me_j, u)
        return me_z * plan.part + lax.div(other, plan.width_y), lax.rem(other, plan.width_y)

    steps = [(1, 0), (-1, 0), (0, 1), (0, -1), (1, 1), (1, -1), (-1, 1), (-1, -1)]

    def present(dx, dy):
        x = here_x + dx
        y = here_y + dy
        return (x >= 0) & (x < plan.width_x) & (y >= 0) & (y < plan.width_y)

    barrier = pltpu.get_barrier_semaphore()

    def greet(device):
        pl.semaphore_signal(barrier, inc=1, device_id=device, device_id_type=pl.DeviceIdType.MESH)

    for dx, dy in steps:

        @pl.when(present(dx, dy))
        def _():
            greet((here_x + dx, here_y + dy))

    for u in range(1, group):
        greet(at_peer(u))
    for t in range(1, lines):
        greet(at_line(t))

    spans = []
    for here, width in ((here_x, plan.width_x), (here_y, plan.width_y)):
        spans.append(1 + (here > 0).astype(I32) + (here < width - 1).astype(I32))
    pl.semaphore_wait(barrier, spans[0] * spans[1] - 1 + group - 1 + lines - 1)

    def remote(src, dst, send, recv, device):
        return pltpu.make_async_remote_copy(
            src_ref=src,
            dst_ref=dst,
            send_sem=send,
            recv_sem=recv,
            device_id=device,
            device_id_type=pl.DeviceIdType.MESH,
        )

    def near_copy(n):
        dx, dy = steps[n]
        if dy == 0:
            src = vec.at[:, pl.ds(rows_x - LS if dx > 0 else 0, LS), :]
            dst = halo.at[0 if dx > 0 else 1]
        else:
            side = 1 if dy > 0 else 0
            if dx == 0:
                src = strips.at[side]
                dst = rim.at[1 - side, pl.ds(1, leaf_x)]
            else:
                src = strips.at[side, leaf_x - 1 if dx > 0 else 0]
                dst = rim.at[1 - side, 0 if dx > 0 else leaf_x + 1]
        return remote(src, dst, near_send.at[n], near_recv.at[n], (here_x + dx, here_y + dy))

    def near_start(first, end):
        for n in range(first, end):

            @pl.when(present(*steps[n]))
            def _():
                near_copy(n).start()

    loads[0].wait()
    near_start(0, 2)

    wide[...] = vec[...].astype(F32)

    def to_grid(x, carry):
        plane = wide[:, x, :]
        lines_of = jnp.concatenate([plane, plane], axis=0).T.astype(BF16).reshape(leaf_y, LS, lanes)
        at = pl.multiple_of(lax.rem(x, LS) * LS, LS)
        grid[1 + lax.div(x, LS), 1 : 1 + leaf_y, pl.ds(at, LS), :] = lines_of
        return carry

    lax.fori_loop(0, rows_x, to_grid, 0, unroll=4)
    for side in range(2):
        for i in range(leaf_x):
            block = grid[1 + i, leaf_y if side else 1].reshape(2, LS // 2, LS, lanes)
            strips[side, i] = jnp.where(low, block[0], block[1])
    near_start(2, 8)

    loads[1].wait()

    def leaf_coef(m, carry):
        i = lax.div(m, leaf_y)
        j = lax.rem(m, leaf_y)
        coef[m] = dot(col[m], grid[1 + i, 1 + j])
        return carry

    lax.fori_loop(0, leaves, leaf_coef, 0, unroll=4)
    loads[2].wait()

    def upper_coef(p, carry):
        children = [i * leaf_y + 2 * p + q for i in range(leaf_x) for q in range(2)]
        left = jnp.concatenate([up[m] for m in children], axis=1)
        right = jnp.concatenate([coef[m] for m in children], axis=0)
        coef[leaves + p] = dot(left_of(left), right_of(right))
        return carry

    lax.fori_loop(0, uppers, upper_coef, 0)

    loads[3].wait()

    def turn(r, carry):
        mats[:, r, :] = jnp.concatenate([coup[r], coup[r + half]], axis=0).T
        return carry

    lax.fori_loop(0, half, turn, 0, unroll=4)

    def contribute(first, count, m):
        left = left_of(mats[pl.ds(first, count)].reshape(count * half, lanes))
        blocks = dot(left, right_of(twice(coef[m]))).reshape(count, half, lanes)
        whole, scale = coded(blocks)
        held[pl.ds(first, count)] = whole
        for q in range(count):
            held_scale[first + q] = scale[q : q + 1]

    def leaf_slots(m, carry):
        contribute(m * K0, K0, m)
        return carry

    def upper_slots(p, carry):
        contribute(leaves * K0 + p * K1, K1, leaves + p)
        return carry

    lax.fori_loop(0, leaves, leaf_slots, 0, unroll=2)
    lax.fori_loop(0, uppers, upper_slots, 0, unroll=2)

    place_scale[...] = jnp.zeros_like(place_scale)

    def put_scale(p, carry):
        t = lax.div(p, plan.each)
        q = lax.rem(p, plan.each)
        at = lax.div(q, cap) * plan.scale_rows + t * cap + lax.rem(q, cap)
        place_scale[pl.ds(at, 1), :] = held_scale[tab[0, p]]
        return carry

    lax.fori_loop(0, plan.total, put_scale, 0, unroll=8)
    send_scale[...] = place_scale[...].astype(BF16).reshape(send_scale.shape)

    def scale_copy(u):
        return remote(
            send_scale.at[plan.peer(me_j, u)], got_scale.at[me_j], scale_send.at[u], scale_recv.at[u], at_peer(u)
        )

    def one_copy(t, u):
        return remote(
            send1.at[pl.ds((t * group + plan.peer(me_j, u)) * cap, cap)],
            recv1[t].at[pl.ds(me_j * cap, cap)],
            one_send.at[t, u],
            one_recv.at[t, u],
            at_peer(u),
        )

    def one_local(t):
        return pltpu.make_async_copy(
            send1.at[pl.ds((t * group + me_j) * cap, cap)], recv1[t].at[pl.ds(me_j * cap, cap)], local_sem.at[t]
        )

    scale_local = pltpu.make_async_copy(send_scale.at[me_j], got_scale.at[me_j], local_sem.at[lines])
    scale_local.start()
    for u in range(1, group):
        scale_copy(u).start()

    for t in plan.order:

        def put(p, carry, t=t):
            send1[t * plan.each + p] = held[tab[0, t * plan.each + p]]
            return carry

        lax.fori_loop(0, plan.each, put, 0, unroll=8)
        for u in range(1, group):
            one_copy(t, u).start()
        one_local(t).start()

    loads[4].wait()
    loads[5].wait()

    def turn_row(j, carry):
        pair = jnp.concatenate([row[j], row[leaf_y + j]], axis=0)
        basis = pair.astype(F32).T.astype(BF16)
        turned[j] = jnp.concatenate([basis, basis], axis=1)
        return carry

    lax.fori_loop(0, leaf_y, turn_row, 0)

    def lift(p, carry):
        parts = []
        for i in range(leaf_x):
            for q in range(2):
                mat = down[i * leaf_y + 2 * p + q]
                parts.append(jnp.concatenate([mat[:half], mat[half:]], axis=1))
        lifts[p] = left_of(jnp.concatenate(parts, axis=0))
        return carry

    lax.fori_loop(0, uppers, lift, 0)

    def near_field(first, count):
        def pair(j, carry):
            sums = []
            for i in range(leaf_x):
                m = i * leaf_y + j
                total = None
                for k in range(tiles.shape[1]):
                    o = off_ref[m, k]
                    term = dot(tiles[m, k], grid[i + lax.div(o, 3), j + lax.rem(o, 3)])
                    total = term if total is None else total + term
                sums.append(total)
            near[j] = jnp.where(low, sums[0], sums[1])
            return carry

        lax.fori_loop(first, first + count, pair, 0)

    def near_edges():
        for n, (dx, dy) in enumerate(steps):

            @pl.when(present(-dx, -dy))
            def _():
                near_copy(n).wait_recv()

        for side in range(2):
            keep = present(-1 if side == 0 else 1, 0)
            wide[:, side * LS : (side + 1) * LS, :] = jnp.where(keep, halo[side].astype(F32), 0.0)

        def to_rows(x, carry):
            plane = wide[:, x, :]
            lines_of = jnp.concatenate([plane, plane], axis=0).T.astype(BF16).reshape(leaf_y, LS, lanes)
            at = pl.multiple_of(lax.rem(x, LS) * LS, LS)
            grid[lax.div(x, LS) * (leaf_x + 1), 1 : 1 + leaf_y, pl.ds(at, LS), :] = lines_of
            return carry

        lax.fori_loop(0, 2 * LS, to_rows, 0, unroll=4)
        for side in range(2):
            dy = 1 if side else -1
            for i in range(leaf_x + 2):
                dx = -1 if i == 0 else (1 if i == leaf_x + 1 else 0)
                keep = present(dx, dy)
                value = jnp.where(keep, rim[side, i].astype(F32), 0.0).reshape(points // 2, lanes)
                other = swapped(value)
                y = leaf_y + 1 if side else 0
                grid[i, y, : points // 2, :] = jnp.where(low, value, other).astype(BF16)
                grid[i, y, points // 2 :, :] = jnp.where(low, other, value).astype(BF16)

    scale_local.wait()
    for u in range(1, group):
        scale_copy(u).wait_recv()
    scale_of[...] = got_scale[...].astype(F32).reshape(scale_of.shape) * (1.0 / STEP)

    def two_copy(t):
        return remote(send2.at[t - 1], recv2[t - 1], two_send.at[t], two_recv.at[t], at_line(t))

    def twos_copy(t):
        return remote(send2_scale.at[t - 1], recv2_scale[t - 1], twos_send.at[t], twos_recv.at[t], at_line(t))

    share = -(-leaf_y // lines)
    done = 0
    for step, t in enumerate(plan.order):
        one_local(t).wait()
        for u in range(1, group):
            one_copy(t, u).wait_recv()

        def collect(i, total, t=t):
            at = t * plan.each + i
            block = decoded(recv1[t][tab[1, at]]) * scale_of[tab[2, at]]
            total = total * tab[3, at].astype(F32) + block
            run[i] = total
            return total

        lax.fori_loop(0, plan.each, collect, jnp.zeros((half, lanes), F32), unroll=4)

        def pick(n, carry, t=t):
            own[n] = run[tab[4, t * KEYS + n]] * tab[5, t * KEYS + n].astype(F32)
            return carry

        lax.fori_loop(0, clusters, pick, 0, unroll=4)
        if t:
            send2_scale[t - 1] = jnp.zeros(send2_scale.shape[1:], BF16)
            group_of = 4

            def pack(g, carry, t=t):
                whole, scale = coded(own[pl.ds(g * group_of, group_of)])
                send2[t - 1, pl.ds(g * group_of, group_of)] = whole
                for q in range(group_of):
                    place_scale[pl.ds(g * group_of + q, 1), :] = scale[q : q + 1]
                return carry

            lax.fori_loop(0, clusters // group_of, pack, 0)
            send2_scale[t - 1] = place_scale[: send2_scale.shape[1], :].astype(BF16)
            two_copy(t).start()
            twos_copy(t).start()
        if step == 0:
            near_edges()
            loads[6].wait()
        count = min(share, leaf_y - done)
        if count > 0:
            near_field(done, count)
            done += count

    for t in range(1, lines):
        two_copy(t).wait_recv()
        twos_copy(t).wait_recv()

    for t in range(1, lines):
        place_scale[: send2_scale.shape[1], :] = recv2_scale[t - 1][...].astype(F32) * (1.0 / STEP)

        def gather(n, carry, t=t):
            own[n] = own[n] + decoded(recv2[t - 1][n]) * place_scale[pl.ds(n, 1), :]
            return carry

        lax.fori_loop(0, clusters, gather, 0, unroll=4)

    def descend(p, carry):
        top = own[leaves + p]
        extra = dot(lifts[p], right_of(spread(top, top))).reshape(2 * leaf_x, half, lanes)
        for i in range(leaf_x):
            for q in range(2):
                m = i * leaf_y + 2 * p + q
                own[m] = own[m] + extra[2 * i + q]
        return carry

    lax.fori_loop(0, uppers, descend, 0)

    def far(j, carry):
        high, rest = halves(spread(own[j], own[leaf_y + j]))
        near[j] = near[j] + dot(turned[j], jnp.concatenate([high, rest], axis=0))
        return carry

    lax.fori_loop(0, leaf_y, far, 0, unroll=2)

    def put_out(x, carry):
        line = near[:, pl.ds(pl.multiple_of(x * LS, LS), LS), :].reshape(rows_y, lanes).T
        out_ref[:, x, :] = line[:vecs]
        out_ref[:, LS + x, :] = line[vecs:]
        return carry

    lax.fori_loop(0, LS, put_out, 0, unroll=2)

    for n in range(8):

        @pl.when(present(*steps[n]))
        def _():
            near_copy(n).wait_send()

    for u in range(1, group):
        scale_copy(u).wait_send()
        for t in range(lines):
            one_copy(t, u).wait_send()
    for t in range(1, lines):
        two_copy(t).wait_send()
        twos_copy(t).wait_send()


def body(
    vectors,
    near_tiles,
    near_offset,
    col_basis,
    row_basis,
    up_transfer,
    down_transfer,
    coupling,
    couple_dest,
    couple_target,
):
    vecs, rows_x, rows_y = vectors.shape
    leaf_x, leaf_y = rows_x // LS, rows_y // LS
    leaves = leaf_x * leaf_y
    uppers = leaf_y // 2
    clusters = leaves + uppers
    rank = coupling.shape[2]
    half = rank // 2
    slots = coupling.shape[1]
    near_count = near_tiles.shape[2]
    points = LS * LS
    lanes = 2 * vecs
    plan = Plan(lax.axis_size("qx"), lax.axis_size("qy"), slots)
    lines, group, cap = plan.lines, plan.group, plan.cap
    scale2 = -(-clusters // 16) * 16
    width = max(plan.total, lines * KEYS)
    vmem, dma = pltpu.VMEM, pltpu.SemaphoreType.DMA
    int16 = jnp.int16
    scratch = [
        vmem((vecs, rows_x, rows_y), BF16),
        vmem((leaves, near_count, points, points), BF16),
        vmem((leaves, rank, points), BF16),
        vmem((leaves, rank, points), BF16),
        vmem((leaves, rank, rank), F32),
        vmem((leaves, rank, rank), F32),
        vmem((rank, rank, slots), F32),
        vmem((vecs, rows_x, rows_y), F32),
        vmem((2, vecs, LS, rows_y), BF16),
        vmem((leaf_x + 2, leaf_y + 2, points, lanes), BF16),
        vmem((2, leaf_x, LS // 2, LS, lanes), BF16),
        vmem((2, leaf_x + 2, LS // 2, LS, lanes), BF16),
        vmem((slots, half, lanes), F32),
        vmem((clusters, rank, lanes), F32),
        vmem((slots, half, lanes), int16),
        vmem((slots, 1, lanes), F32),
        vmem((group * plan.scale_rows, lanes), F32),
        vmem((group, plan.scale_rows, lanes), BF16),
        vmem((group, plan.scale_rows, lanes), BF16),
        vmem((group * plan.scale_rows, 1, lanes), F32),
        vmem((plan.total, half, lanes), int16),
        vmem((plan.each, half, lanes), F32),
        vmem((clusters, half, lanes), F32),
        vmem((max(lines - 1, 1), clusters, half, lanes), int16),
        vmem((max(lines - 1, 1), scale2, lanes), BF16),
        vmem((leaf_y, points, lanes), F32),
        vmem((leaf_y, points, 4 * rank), BF16),
        vmem((uppers, 2 * leaf_x * half, 6 * rank), BF16),
        dma((7,)),
        dma((8,)),
        dma((8,)),
        dma((group,)),
        dma((group,)),
        dma((lines, group)),
        dma((lines, group)),
        dma((lines,)),
        dma((lines,)),
        dma((lines,)),
        dma((lines,)),
        dma((lines + 1,)),
    ]
    scratch += [vmem((plan.each, half, lanes), int16)] * lines
    scratch += [vmem((clusters, half, lanes), int16)] * (lines - 1)
    scratch += [vmem((scale2, lanes), BF16)] * (lines - 1)
    tab = pl.pallas_call(
        lambda *refs: tables(plan, clusters, *refs),
        out_shape=jax.ShapeDtypeStruct((8, width), I32),
        in_specs=[VM, VM],
        out_specs=VM,
        name="tables",
    )(couple_dest, couple_target)
    return pl.pallas_call(
        lambda *refs: kernel(plan, *refs),
        out_shape=jax.ShapeDtypeStruct((vecs, rows_x, rows_y), F32),
        in_specs=[ANY, ANY, SM, ANY, ANY, ANY, ANY, ANY, SM],
        out_specs=VM,
        scratch_shapes=scratch,
        compiler_params=pltpu.CompilerParams(collective_id=0, has_side_effects=True, vmem_limit_bytes=48 << 20),
        name="product",
    )(
        vectors,
        near_tiles.reshape(leaves, near_count, points, points),
        near_offset.reshape(leaves, near_count),
        col_basis.reshape(leaves, rank, points),
        row_basis.reshape(leaves, rank, points),
        up_transfer.reshape(leaves, rank, rank),
        down_transfer.reshape(leaves, rank, rank),
        coupling[0].transpose(1, 2, 0),
        tab,
    )


def solution(mesh):
    return jax.shard_map(
        body,
        mesh=mesh,
        in_specs=(
            P(None, "qx", "qy"),
            P("qx", "qy", None, None, None),
            P("qx", "qy", None),
            P("qx", "qy", None, None),
            P("qx", "qy", None, None),
            P("qx", "qy", None, None),
            P("qx", "qy", None, None),
            P(("qx", "qy"), None, None, None),
            P(),
            P(),
        ),
        out_specs=P(None, "qx", "qy"),
        check_vma=False,
    )
```

```python
import jax
import jax.numpy as jnp
from jax import lax
from jax.experimental import pallas as pl
from jax.experimental.pallas import tpu as pltpu
from jax.sharding import PartitionSpec as P

LS = 16
K0 = 6
K1 = 8
KEYS = 32
STEP = 32767.0

ANY = pl.BlockSpec(memory_space=pl.ANY)
VM = pl.BlockSpec(memory_space=pltpu.VMEM)
SM = pl.BlockSpec(memory_space=pltpu.SMEM)
F32 = jnp.float32
BF16 = jnp.bfloat16
I32 = jnp.int32


def halves(value):
    high = value.astype(BF16)
    return high, (value - high.astype(F32)).astype(BF16)


def left_of(value):
    high, low = halves(value)
    return jnp.concatenate([high, low, high], axis=1)


def right_of(value):
    high, low = halves(value)
    return jnp.concatenate([high, high, low], axis=0)


def dot(left, right):
    return jnp.dot(left, right, preferred_element_type=F32)


def swapped(value):
    half = value.shape[-1] // 2
    return jnp.concatenate([value[..., half:], value[..., :half]], axis=-1)


def spread(first, second):
    low = lax.broadcasted_iota(I32, first.shape, 1) < first.shape[1] // 2
    return jnp.concatenate(
        [
            jnp.where(low, first, 0.0),
            jnp.where(low, swapped(first), 0.0),
            jnp.where(low, 0.0, swapped(second)),
            jnp.where(low, 0.0, second),
        ],
        axis=0,
    )


def twice(value):
    low = lax.broadcasted_iota(I32, value.shape, 1) < value.shape[1] // 2
    return jnp.concatenate([jnp.where(low, value, 0.0), jnp.where(low, 0.0, value)], axis=0)


def coded(blocks):
    peak = jnp.max(jnp.abs(blocks), axis=1)
    scale = (jnp.maximum(peak, 1e-30) * 1.004).astype(BF16).astype(F32)
    inverse = STEP / scale
    whole = jnp.round(blocks * inverse[:, None, :]).astype(I32).astype(jnp.int16)
    return whole, scale


def decoded(value):
    return value.astype(I32).astype(F32)


class Plan:
    def __init__(self, width_x, width_y, slots):
        part = max(1, width_y // 2)
        if width_x % part:
            part = 1
        self.width_x, self.width_y = width_x, width_y
        self.part = part
        self.group = part * width_y
        self.lines = width_x // part
        devices = width_x * width_y
        self.cap = (slots + devices - 1) // devices
        self.total = devices * self.cap
        self.each = self.group * self.cap
        self.scale_rows = -(-(self.lines * self.cap) // 16) * 16
        self.xor_line = self.lines & (self.lines - 1) == 0
        self.xor_group = self.group & (self.group - 1) == 0
        far = self.lines // 2
        self.order = [t for t in range(far, self.lines)] + [t for t in range(far - 1, 0, -1)] + [0]

    def line(self, z, t):
        return z ^ t if self.xor_line else lax.rem(z + t, self.lines)

    def line_step(self, z, other):
        return other ^ z if self.xor_line else lax.rem(other - z + self.lines, self.lines)

    def peer(self, j, u):
        return j ^ u if self.xor_group else lax.rem(j + u, self.group)


def tables(plan, clusters, me_z, me_j, dest_ref, target_ref, tab_ref):
    slots = dest_ref.shape[1]
    cap, group, lines = plan.cap, plan.group, plan.lines
    own = dest_ref[pl.ds(me_z * group + me_j, 1), :]
    across = jnp.broadcast_to(own.astype(F32), (slots, slots))
    down = across.T
    row = lax.broadcasted_iota(I32, (slots, slots), 0)
    col = lax.broadcasted_iota(I32, (slots, slots), 1)
    order = jnp.sum(jnp.where((across == down) & (col < row), 1.0, 0.0), axis=1, keepdims=True)
    dest = down[:, :1].astype(I32)
    whole = jnp.maximum(dest, 0)
    step = plan.line_step(me_z, lax.div(whole, group))
    place = (step * group + lax.rem(whole, group)) * cap + order.astype(I32)
    place = jnp.where(dest >= 0, place, -1)
    lane = lax.broadcasted_iota(I32, (slots, plan.total), 1)
    slot = lax.broadcasted_iota(I32, (slots, plan.total), 0).astype(F32)
    slot_of = jnp.sum(jnp.where(place == lane, slot, 0.0), axis=0, keepdims=True)

    first = pl.multiple_of(me_z * group, group)
    dests = dest_ref[pl.ds(first, group), :]
    targets = target_ref[pl.ds(first, group), :].astype(F32)
    match = jnp.concatenate([dests == plan.line(me_z, t) * group + me_j for t in range(lines)], axis=0)
    target = jnp.concatenate([targets] * lines, axis=0)
    before = jnp.where(row < col, 1.0, 0.0).astype(BF16)
    rank_in = dot(jnp.where(match, 1.0, 0.0).astype(BF16), before)
    rows = lines * group
    step_row = lax.div(lax.broadcasted_iota(I32, (rows, 1), 0), group)
    from_row = lax.rem(lax.broadcasted_iota(I32, (rows, 1), 0), group)
    keys, blocks, scales = [], [], []
    for k in range(cap):
        landing = match & (rank_in == float(k))
        mine = clusters + jnp.sum(jnp.where(landing, target - clusters, 0.0), axis=1, keepdims=True)
        keys.append(mine + (step_row * KEYS).astype(F32))
        blocks.append((from_row * cap + k).astype(F32))
        scales.append((from_row * plan.scale_rows + step_row * cap + k).astype(F32))
    total = plan.total
    key_row = jnp.broadcast_to(jnp.concatenate(keys, axis=0), (total, total))
    key_col = key_row.T
    row = lax.broadcasted_iota(I32, (total, total), 0)
    col = lax.broadcasted_iota(I32, (total, total), 1)
    earlier = (key_row == key_col) & (col < row)
    rank = jnp.sum(jnp.where((key_col < key_row) | earlier, 1.0, 0.0), axis=1, keepdims=True)
    follows = jnp.max(jnp.where(earlier, 1.0, 0.0), axis=1, keepdims=True)
    hit = rank == col.astype(F32)

    def sorted_row(values):
        return jnp.sum(jnp.where(hit, values, 0.0), axis=0, keepdims=True)

    wide = lines * KEYS
    key = jnp.concatenate(keys, axis=0)
    place = lax.broadcasted_iota(I32, (total, wide), 1)
    code = place.astype(F32)
    last = jnp.sum(jnp.where(key <= code, 1.0, 0.0), axis=0, keepdims=True) - 1.0
    last = last - (lax.div(place[:1], KEYS) * plan.each).astype(F32)
    there = jnp.max(jnp.where(key == code, 1.0, 0.0), axis=0, keepdims=True)

    def put(at, values, size):
        tab_ref[at : at + 1, : values.shape[1]] = jnp.clip(values.astype(I32), 0, size - 1)

    put(0, slot_of, slots)
    put(1, sorted_row(jnp.concatenate(blocks, axis=0)), plan.each)
    put(2, sorted_row(jnp.concatenate(scales, axis=0)), group * plan.scale_rows)
    put(3, sorted_row(follows), 2)
    put(4, last, plan.each)
    put(5, there, 2)


def kernel(plan, *refs):
    lines, group, cap = plan.lines, plan.group, plan.cap
    (
        vec_hbm, tiles_hbm, off_ref, col_hbm, row_hbm, up_hbm, down_hbm, coup_hbm, dest_hbm, target_hbm,
        out_ref,
        vec, tiles, col, row, up, down, coup,
        wide, halo, grid, strips, rim, mats, coef, held, held_scale,
        place_scale, send_scale, got_scale, scale_of, send1,
        dest, target, tab_v, tab, run, own, send2, send2_scale, near, turned, lifts,
        load_sem, tab_sem, near_send, near_recv, scale_send, scale_recv,
        one_send, one_recv, two_send, two_recv, twos_send, twos_recv, local_sem,
        *landing,
    ) = refs
    recv1 = landing[:lines]
    recv2 = landing[lines : 2 * lines - 1]
    recv2_scale = landing[2 * lines - 1 :]

    here_x = lax.axis_index("qx")
    here_y = lax.axis_index("qy")
    me_z = lax.div(here_x, plan.part)
    me_j = lax.rem(here_x, plan.part) * plan.width_y + here_y
    vecs, rows_x, rows_y = vec.shape
    leaf_x, leaf_y = rows_x // LS, rows_y // LS
    leaves = leaf_x * leaf_y
    uppers = leaf_y // 2
    clusters = leaves + uppers
    rank = coup.shape[0]
    half = rank // 2
    lanes = 2 * vecs
    points = LS * LS
    low = lax.broadcasted_iota(I32, (1, lanes), 1) < vecs

    pairs = [
        (vec_hbm, vec),
        (col_hbm, col),
        (up_hbm, up),
        (coup_hbm, coup),
        (row_hbm, row),
        (down_hbm, down),
        (tiles_hbm, tiles),
        (dest_hbm, dest),
        (target_hbm, target),
    ]
    loads = [pltpu.make_async_copy(src, dst, load_sem.at[n]) for n, (src, dst) in enumerate(pairs)]
    for n in (7, 8, 0, 1, 2, 3, 4, 5, 6):
        loads[n].start()

    def at_line(t):
        other = plan.line(me_z, t)
        return other * plan.part + lax.div(me_j, plan.width_y), here_y

    def at_peer(u):
        other = plan.peer(me_j, u)
        return me_z * plan.part + lax.div(other, plan.width_y), lax.rem(other, plan.width_y)

    steps = [(1, 0), (-1, 0), (0, 1), (0, -1), (1, 1), (1, -1), (-1, 1), (-1, -1)]

    def present(dx, dy):
        x = here_x + dx
        y = here_y + dy
        return (x >= 0) & (x < plan.width_x) & (y >= 0) & (y < plan.width_y)

    barrier = pltpu.get_barrier_semaphore()

    def greet(device):
        pl.semaphore_signal(barrier, inc=1, device_id=device, device_id_type=pl.DeviceIdType.MESH)

    for dx, dy in steps:

        @pl.when(present(dx, dy))
        def _():
            greet((here_x + dx, here_y + dy))

    for u in range(1, group):
        greet(at_peer(u))
    for t in range(1, lines):
        greet(at_line(t))

    loads[7].wait()
    loads[8].wait()
    tables(plan, clusters, me_z, me_j, dest, target, tab_v)
    tab_copy = pltpu.make_async_copy(tab_v, tab, tab_sem)
    tab_copy.start()

    spans = []
    for here, width in ((here_x, plan.width_x), (here_y, plan.width_y)):
        spans.append(1 + (here > 0).astype(I32) + (here < width - 1).astype(I32))
    pl.semaphore_wait(barrier, spans[0] * spans[1] - 1 + group - 1 + lines - 1)

    def remote(src, dst, send, recv, device):
        return pltpu.make_async_remote_copy(
            src_ref=src,
            dst_ref=dst,
            send_sem=send,
            recv_sem=recv,
            device_id=device,
            device_id_type=pl.DeviceIdType.MESH,
        )

    def near_copy(n):
        dx, dy = steps[n]
        if dy == 0:
            src = vec.at[:, pl.ds(rows_x - LS if dx > 0 else 0, LS), :]
            dst = halo.at[0 if dx > 0 else 1]
        else:
            side = 1 if dy > 0 else 0
            if dx == 0:
                src = strips.at[side]
                dst = rim.at[1 - side, pl.ds(1, leaf_x)]
            else:
                src = strips.at[side, leaf_x - 1 if dx > 0 else 0]
                dst = rim.at[1 - side, 0 if dx > 0 else leaf_x + 1]
        return remote(src, dst, near_send.at[n], near_recv.at[n], (here_x + dx, here_y + dy))

    def near_start(first, end):
        for n in range(first, end):

            @pl.when(present(*steps[n]))
            def _():
                near_copy(n).start()

    loads[0].wait()
    odd = lax.rem(here_x, 2) == 1
    inside = (jnp.logical_not(odd), odd)
    for n in range(2):

        @pl.when(present(*steps[n]) & jnp.logical_not(inside[n]))
        def _():
            near_copy(n).start()


    wide[...] = vec[...].astype(F32)

    def to_grid(x, carry):
        plane = wide[:, x, :]
        lines_of = jnp.concatenate([plane, plane], axis=0).T.astype(BF16).reshape(leaf_y, LS, lanes)
        at = pl.multiple_of(lax.rem(x, LS) * LS, LS)
        grid[1 + lax.div(x, LS), 1 : 1 + leaf_y, pl.ds(at, LS), :] = lines_of
        return carry

    lax.fori_loop(0, rows_x, to_grid, 0, unroll=4)
    for side in range(2):
        for i in range(leaf_x):
            block = grid[1 + i, leaf_y if side else 1].reshape(2, LS // 2, LS, lanes)
            strips[side, i] = jnp.where(low, block[0], block[1])
    near_start(2, 8)

    loads[1].wait()

    def leaf_coef(m, carry):
        i = lax.div(m, leaf_y)
        j = lax.rem(m, leaf_y)
        coef[m] = dot(col[m], grid[1 + i, 1 + j])
        return carry

    lax.fori_loop(0, leaves, leaf_coef, 0, unroll=4)
    loads[2].wait()

    def upper_coef(p, carry):
        children = [i * leaf_y + 2 * p + q for i in range(leaf_x) for q in range(2)]
        left = jnp.concatenate([up[m] for m in children], axis=1)
        right = jnp.concatenate([coef[m] for m in children], axis=0)
        coef[leaves + p] = dot(left_of(left), right_of(right))
        return carry

    lax.fori_loop(0, uppers, upper_coef, 0)

    loads[3].wait()

    def turn(r, carry):
        mats[:, r, :] = jnp.concatenate([coup[r], coup[r + half]], axis=0).T
        return carry

    lax.fori_loop(0, half, turn, 0, unroll=4)

    def contribute(first, count, m):
        left = left_of(mats[pl.ds(first, count)].reshape(count * half, lanes))
        blocks = dot(left, right_of(twice(coef[m]))).reshape(count, half, lanes)
        whole, scale = coded(blocks)
        held[pl.ds(first, count)] = whole
        for q in range(count):
            held_scale[first + q] = scale[q : q + 1]

    def leaf_slots(m, carry):
        contribute(m * K0, K0, m)
        return carry

    def upper_slots(p, carry):
        contribute(leaves * K0 + p * K1, K1, leaves + p)
        return carry

    lax.fori_loop(0, leaves, leaf_slots, 0, unroll=2)
    lax.fori_loop(0, uppers, upper_slots, 0, unroll=2)

    tab_copy.wait()
    place_scale[...] = jnp.zeros_like(place_scale)

    def put_scale(p, carry):
        t = lax.div(p, plan.each)
        q = lax.rem(p, plan.each)
        at = lax.div(q, cap) * plan.scale_rows + t * cap + lax.rem(q, cap)
        place_scale[pl.ds(at, 1), :] = held_scale[tab[0, p]]
        return carry

    lax.fori_loop(0, plan.total, put_scale, 0, unroll=8)
    send_scale[...] = place_scale[...].astype(BF16).reshape(send_scale.shape)

    def scale_copy(u):
        return remote(
            send_scale.at[plan.peer(me_j, u)], got_scale.at[me_j], scale_send.at[u], scale_recv.at[u], at_peer(u)
        )

    def one_copy(t, u):
        return remote(
            send1.at[pl.ds((t * group + plan.peer(me_j, u)) * cap, cap)],
            recv1[t].at[pl.ds(me_j * cap, cap)],
            one_send.at[t, u],
            one_recv.at[t, u],
            at_peer(u),
        )

    def one_local(t):
        return pltpu.make_async_copy(
            send1.at[pl.ds((t * group + me_j) * cap, cap)], recv1[t].at[pl.ds(me_j * cap, cap)], local_sem.at[t]
        )

    scale_local = pltpu.make_async_copy(send_scale.at[me_j], got_scale.at[me_j], local_sem.at[lines])
    scale_local.start()
    for u in range(1, group):
        scale_copy(u).start()

    for t in plan.order:

        def put(p, carry, t=t):
            send1[t * plan.each + p] = held[tab[0, t * plan.each + p]]
            return carry

        lax.fori_loop(0, plan.each, put, 0, unroll=8)
        for u in range(1, group):
            one_copy(t, u).start()
        one_local(t).start()

    loads[4].wait()
    loads[5].wait()

    def turn_row(j, carry):
        pair = jnp.concatenate([row[j], row[leaf_y + j]], axis=0)
        basis = pair.astype(F32).T.astype(BF16)
        turned[j] = jnp.concatenate([basis, basis], axis=1)
        return carry

    lax.fori_loop(0, leaf_y, turn_row, 0)

    def lift(p, carry):
        parts = []
        for i in range(leaf_x):
            for q in range(2):
                mat = down[i * leaf_y + 2 * p + q]
                parts.append(jnp.concatenate([mat[:half], mat[half:]], axis=1))
        lifts[p] = left_of(jnp.concatenate(parts, axis=0))
        return carry

    lax.fori_loop(0, uppers, lift, 0)

    def near_field(i, first, count, merge):
        mine = low if merge is None else (low & (i == 0)) | (jnp.logical_not(low) & (i != 0))

        def leaf(j, carry):
            m = i * leaf_y + j
            total = None
            for k in range(tiles.shape[1]):
                o = off_ref[k, i, j]
                term = dot(tiles[m, k], grid[i + lax.div(o, 3), j + lax.rem(o, 3)])
                total = term if total is None else total + term
            near[j] = total if merge is None else jnp.where(mine, total, near[j])
            return carry

        lax.fori_loop(first, first + count, leaf, 0)

    def near_rows(side):
        wide[:, :LS, :] = jnp.where(present(2 * side - 1, 0), halo[side].astype(F32), 0.0)

        def to_rows(x, carry):
            plane = wide[:, x, :]
            lines_of = jnp.concatenate([plane, plane], axis=0).T.astype(BF16).reshape(leaf_y, LS, lanes)
            grid[side * (leaf_x + 1), 1 : 1 + leaf_y, pl.ds(pl.multiple_of(x * LS, LS), LS), :] = lines_of
            return carry

        lax.fori_loop(0, LS, to_rows, 0, unroll=4)

    def near_edges():
        for n, (dx, dy) in enumerate(steps):
            if n >= 2:

                @pl.when(present(-dx, -dy))
                def _():
                    near_copy(n).wait_recv()

        for side in range(2):
            dy = 1 if side else -1
            for i in range(leaf_x + 2):
                dx = -1 if i == 0 else (1 if i == leaf_x + 1 else 0)
                keep = present(dx, dy)
                value = jnp.where(keep, rim[side, i].astype(F32), 0.0).reshape(points // 2, lanes)
                other = swapped(value)
                y = leaf_y + 1 if side else 0
                grid[i, y, : points // 2, :] = jnp.where(low, value, other).astype(BF16)
                grid[i, y, points // 2 :, :] = jnp.where(low, other, value).astype(BF16)

    scale_local.wait()
    for u in range(1, group):
        scale_copy(u).wait_recv()
    scale_of[...] = got_scale[...].astype(F32).reshape(scale_of.shape) * (1.0 / STEP)

    def two_copy(t):
        return remote(send2.at[t - 1], recv2[t - 1], two_send.at[t], two_recv.at[t], at_line(t))

    def twos_copy(t):
        return remote(send2_scale.at[t - 1], recv2_scale[t - 1], twos_send.at[t], twos_recv.at[t], at_line(t))

    early = lax.rem(here_x, 2)
    arrives_inside = (inside[1], inside[0])
    done = 0
    for step, t in enumerate(plan.order):
        one_local(t).wait()
        for u in range(1, group):
            one_copy(t, u).wait_recv()

        def collect(i, total, t=t):
            at = t * plan.each + i
            block = decoded(recv1[t][tab[1, at]]) * scale_of[tab[2, at]]
            total = total * tab[3, at].astype(F32) + block
            run[i] = total
            return total

        lax.fori_loop(0, plan.each, collect, jnp.zeros((half, lanes), F32), unroll=4)

        def pick(n, carry, t=t):
            own[n] = run[tab[4, t * KEYS + n]] * tab[5, t * KEYS + n].astype(F32)
            return carry

        lax.fori_loop(0, clusters, pick, 0, unroll=4)
        if t:
            send2_scale[t - 1] = jnp.zeros(send2_scale.shape[1:], BF16)
            group_of = 4

            def pack(g, carry, t=t):
                whole, scale = coded(own[pl.ds(g * group_of, group_of)])
                send2[t - 1, pl.ds(g * group_of, group_of)] = whole
                for q in range(group_of):
                    place_scale[pl.ds(g * group_of + q, 1), :] = scale[q : q + 1]
                return carry

            lax.fori_loop(0, clusters // group_of, pack, 0)
            send2_scale[t - 1] = place_scale[: send2_scale.shape[1], :].astype(BF16)
            two_copy(t).start()
            twos_copy(t).start()
        if step == 0:
            near_edges()
            loads[6].wait()
            for n in range(2):

                @pl.when(present(-steps[n][0], 0) & jnp.logical_not(arrives_inside[n]))
                def _():
                    near_copy(n).wait_recv()

            near_rows(early)
        if step == lines - 1:
            for n in range(2):

                @pl.when(present(*steps[n]) & inside[n])
                def _():
                    near_copy(n).start()

        count = leaf_y - done if step == lines - 1 else min(-(-leaf_y // lines), leaf_y - done)
        if count > 0:
            near_field(early, done, count, None)
            done += count

    for n in range(2):

        @pl.when(present(-steps[n][0], 0) & arrives_inside[n])
        def _():
            near_copy(n).wait_recv()

    near_rows(1 - early)
    near_field(1 - early, 0, leaf_y, True)

    for t in range(1, lines):
        two_copy(t).wait_recv()
        twos_copy(t).wait_recv()

    for t in range(1, lines):
        place_scale[: send2_scale.shape[1], :] = recv2_scale[t - 1][...].astype(F32) * (1.0 / STEP)

        def gather(n, carry, t=t):
            own[n] = own[n] + decoded(recv2[t - 1][n]) * place_scale[pl.ds(n, 1), :]
            return carry

        lax.fori_loop(0, clusters, gather, 0, unroll=4)

    def descend(p, carry):
        top = own[leaves + p]
        extra = dot(lifts[p], right_of(spread(top, top))).reshape(2 * leaf_x, half, lanes)
        for i in range(leaf_x):
            for q in range(2):
                m = i * leaf_y + 2 * p + q
                own[m] = own[m] + extra[2 * i + q]
        return carry

    lax.fori_loop(0, uppers, descend, 0)

    def far(j, carry):
        high, rest = halves(spread(own[j], own[leaf_y + j]))
        near[j] = near[j] + dot(turned[j], jnp.concatenate([high, rest], axis=0))
        return carry

    lax.fori_loop(0, leaf_y, far, 0, unroll=2)

    def put_out(x, carry):
        line = near[:, pl.ds(pl.multiple_of(x * LS, LS), LS), :].reshape(rows_y, lanes).T
        out_ref[:, x, :] = line[:vecs]
        out_ref[:, LS + x, :] = line[vecs:]
        return carry

    lax.fori_loop(0, LS, put_out, 0, unroll=2)

    for n in range(8):

        @pl.when(present(*steps[n]))
        def _():
            near_copy(n).wait_send()

    for u in range(1, group):
        scale_copy(u).wait_send()
        for t in range(lines):
            one_copy(t, u).wait_send()
    for t in range(1, lines):
        two_copy(t).wait_send()
        twos_copy(t).wait_send()


def body(
    vectors,
    near_tiles,
    near_offset,
    col_basis,
    row_basis,
    up_transfer,
    down_transfer,
    coupling,
    couple_dest,
    couple_target,
):
    vecs, rows_x, rows_y = vectors.shape
    leaf_x, leaf_y = rows_x // LS, rows_y // LS
    leaves = leaf_x * leaf_y
    uppers = leaf_y // 2
    clusters = leaves + uppers
    rank = coupling.shape[2]
    half = rank // 2
    slots = coupling.shape[1]
    near_count = near_tiles.shape[2]
    points = LS * LS
    lanes = 2 * vecs
    plan = Plan(lax.axis_size("qx"), lax.axis_size("qy"), slots)
    lines, group, cap = plan.lines, plan.group, plan.cap
    scale2 = -(-clusters // 16) * 16
    devices = couple_dest.shape[0]
    width = max(plan.total, lines * KEYS)
    vmem, dma = pltpu.VMEM, pltpu.SemaphoreType.DMA
    int16 = jnp.int16
    scratch = [
        vmem((vecs, rows_x, rows_y), BF16),
        vmem((leaves, near_count, points, points), BF16),
        vmem((leaves, rank, points), BF16),
        vmem((leaves, rank, points), BF16),
        vmem((leaves, rank, rank), F32),
        vmem((leaves, rank, rank), F32),
        vmem((rank, rank, slots), F32),
        vmem((vecs, rows_x, rows_y), F32),
        vmem((2, vecs, LS, rows_y), BF16),
        vmem((leaf_x + 2, leaf_y + 2, points, lanes), BF16),
        vmem((2, leaf_x, LS // 2, LS, lanes), BF16),
        vmem((2, leaf_x + 2, LS // 2, LS, lanes), BF16),
        vmem((slots, half, lanes), F32),
        vmem((clusters, rank, lanes), F32),
        vmem((slots, half, lanes), int16),
        vmem((slots, 1, lanes), F32),
        vmem((group * plan.scale_rows, lanes), F32),
        vmem((group, plan.scale_rows, lanes), BF16),
        vmem((group, plan.scale_rows, lanes), BF16),
        vmem((group * plan.scale_rows, 1, lanes), F32),
        vmem((plan.total, half, lanes), int16),
        vmem((devices, slots), I32),
        vmem((devices, slots), I32),
        vmem((8, width), I32),
        pltpu.SMEM((8, width), I32),
        vmem((plan.each, half, lanes), F32),
        vmem((clusters, half, lanes), F32),
        vmem((max(lines - 1, 1), clusters, half, lanes), int16),
        vmem((max(lines - 1, 1), scale2, lanes), BF16),
        vmem((leaf_y, points, lanes), F32),
        vmem((leaf_y, points, 4 * rank), BF16),
        vmem((uppers, 2 * leaf_x * half, 6 * rank), BF16),
        dma((9,)),
        dma(()),
        dma((8,)),
        dma((8,)),
        dma((group,)),
        dma((group,)),
        dma((lines, group)),
        dma((lines, group)),
        dma((lines,)),
        dma((lines,)),
        dma((lines,)),
        dma((lines,)),
        dma((lines + 1,)),
    ]
    scratch += [vmem((plan.each, half, lanes), int16)] * lines
    scratch += [vmem((clusters, half, lanes), int16)] * (lines - 1)
    scratch += [vmem((scale2, lanes), BF16)] * (lines - 1)
    return pl.pallas_call(
        lambda *refs: kernel(plan, *refs),
        out_shape=jax.ShapeDtypeStruct((vecs, rows_x, rows_y), F32),
        in_specs=[ANY, ANY, SM, ANY, ANY, ANY, ANY, ANY, ANY, ANY],
        out_specs=VM,
        scratch_shapes=scratch,
        compiler_params=pltpu.CompilerParams(collective_id=0, has_side_effects=True, vmem_limit_bytes=60 << 20),
        name="product",
    )(
        vectors,
        near_tiles.reshape(leaves, near_count, points, points),
        near_offset.transpose(2, 0, 1),
        col_basis.reshape(leaves, rank, points),
        row_basis.reshape(leaves, rank, points),
        up_transfer.reshape(leaves, rank, rank),
        down_transfer.reshape(leaves, rank, rank),
        coupling[0].transpose(1, 2, 0),
        couple_dest,
        couple_target,
    )


def solution(mesh):
    return jax.shard_map(
        body,
        mesh=mesh,
        in_specs=(
            P(None, "qx", "qy"),
            P("qx", "qy", None, None, None),
            P("qx", "qy", None),
            P("qx", "qy", None, None),
            P("qx", "qy", None, None),
            P("qx", "qy", None, None),
            P("qx", "qy", None, None),
            P(("qx", "qy"), None, None, None),
            P(),
            P(),
        ),
        out_specs=P(None, "qx", "qy"),
        check_vma=False,
    )
```

```python
import jax
import jax.numpy as jnp
from jax import lax
from jax.experimental import pallas as pl
from jax.experimental.pallas import tpu as pltpu
from jax.sharding import PartitionSpec as P

LS = 16
K0 = 6
K1 = 8
KEYS = 32
STEP = 32767.0

ANY = pl.BlockSpec(memory_space=pl.ANY)
VM = pl.BlockSpec(memory_space=pltpu.VMEM)
SM = pl.BlockSpec(memory_space=pltpu.SMEM)
F32 = jnp.float32
BF16 = jnp.bfloat16
I32 = jnp.int32


def halves(value):
    high = value.astype(BF16)
    return high, (value - high.astype(F32)).astype(BF16)


def left_of(value):
    high, low = halves(value)
    return jnp.concatenate([high, low, high], axis=1)


def right_of(value):
    high, low = halves(value)
    return jnp.concatenate([high, high, low], axis=0)


def dot(left, right):
    return jnp.dot(left, right, preferred_element_type=F32)


def swapped(value):
    half = value.shape[-1] // 2
    return jnp.concatenate([value[..., half:], value[..., :half]], axis=-1)


def spread(first, second):
    low = lax.broadcasted_iota(I32, first.shape, 1) < first.shape[1] // 2
    return jnp.concatenate(
        [
            jnp.where(low, first, 0.0),
            jnp.where(low, swapped(first), 0.0),
            jnp.where(low, 0.0, swapped(second)),
            jnp.where(low, 0.0, second),
        ],
        axis=0,
    )


def twice(value):
    low = lax.broadcasted_iota(I32, value.shape, 1) < value.shape[1] // 2
    return jnp.concatenate([jnp.where(low, value, 0.0), jnp.where(low, 0.0, value)], axis=0)


def coded(blocks):
    peak = jnp.max(jnp.abs(blocks), axis=1)
    scale = (jnp.maximum(peak, 1e-30) * 1.004).astype(BF16).astype(F32)
    inverse = STEP / scale
    whole = jnp.round(blocks * inverse[:, None, :]).astype(I32).astype(jnp.int16)
    return whole, scale


def decoded(value):
    return value.astype(I32).astype(F32)


class Plan:
    def __init__(self, width_x, width_y, slots):
        part = max(1, width_y // 2)
        if width_x % part:
            part = 1
        stride = part if width_x % (part * part) == 0 else 1
        self.width_x, self.width_y = width_x, width_y
        self.part, self.stride = part, stride
        self.group = part * width_y
        self.lines = width_x // part
        devices = width_x * width_y
        self.cap = (slots + devices - 1) // devices
        self.total = devices * self.cap
        self.each = self.group * self.cap
        self.scale_rows = -(-(self.lines * self.cap) // 16) * 16
        self.xor_line = self.lines & (self.lines - 1) == 0
        self.xor_group = self.group & (self.group - 1) == 0
        self.order = list(range(self.lines - 1, -1, -1))
        self.hops = sorted({self.hop(t) for t in range(1, self.lines)})

    def hop(self, t):
        return t & -t if self.xor_line else t

    def into(self, t):
        return t - self.hop(t)

    def line(self, z, t):
        return z ^ t if self.xor_line else lax.rem(z + t, self.lines)

    def line_step(self, z, other):
        return other ^ z if self.xor_line else lax.rem(other - z + self.lines, self.lines)

    def peer(self, j, u):
        return j ^ u if self.xor_group else lax.rem(j + u, self.group)

    def place(self, x, y):
        low = lax.rem(x, self.stride)
        rest = lax.div(x, self.stride)
        return lax.div(rest, self.part) * self.stride + low, lax.rem(rest, self.part) * self.width_y + y

    def where(self, z, j):
        high, low = lax.div(z, self.stride), lax.rem(z, self.stride)
        return (high * self.part + lax.div(j, self.width_y)) * self.stride + low, lax.rem(j, self.width_y)

    def index(self, z, j):
        x, y = self.where(z, j)
        return x * self.width_y + y


def tables(plan, clusters, me_z, me_j, dest_ref, target_ref, dests_ref, targets_ref, tab_ref):
    slots = dest_ref.shape[1]
    cap, group, lines = plan.cap, plan.group, plan.lines
    own = dest_ref[pl.ds(plan.index(me_z, me_j), 1), :]
    across = jnp.broadcast_to(own.astype(F32), (slots, slots))
    down = across.T
    row = lax.broadcasted_iota(I32, (slots, slots), 0)
    col = lax.broadcasted_iota(I32, (slots, slots), 1)
    order = jnp.sum(jnp.where((across == down) & (col < row), 1.0, 0.0), axis=1, keepdims=True)
    dest = down[:, :1].astype(I32)
    whole = jnp.maximum(dest, 0)
    line, peer = plan.place(lax.div(whole, plan.width_y), lax.rem(whole, plan.width_y))
    place = (plan.line_step(me_z, line) * group + peer) * cap + order.astype(I32)
    place = jnp.where(dest >= 0, place, -1)
    lane = lax.broadcasted_iota(I32, (slots, plan.total), 1)
    slot = lax.broadcasted_iota(I32, (slots, plan.total), 0).astype(F32)
    slot_of = jnp.sum(jnp.where(place == lane, slot, 0.0), axis=0, keepdims=True)

    for j in range(group):
        at = plan.index(me_z, j)
        dests_ref[j : j + 1, :] = dest_ref[pl.ds(at, 1), :]
        targets_ref[j : j + 1, :] = target_ref[pl.ds(at, 1), :].astype(F32)
    dests, targets = dests_ref[...], targets_ref[...]
    match = jnp.concatenate([dests == plan.index(plan.line(me_z, t), me_j) for t in range(lines)], axis=0)
    target = jnp.concatenate([targets] * lines, axis=0)
    before = jnp.where(row < col, 1.0, 0.0).astype(BF16)
    rank_in = dot(jnp.where(match, 1.0, 0.0).astype(BF16), before)
    rows = lines * group
    step_row = lax.div(lax.broadcasted_iota(I32, (rows, 1), 0), group)
    from_row = lax.rem(lax.broadcasted_iota(I32, (rows, 1), 0), group)
    keys, blocks, scales = [], [], []
    for k in range(cap):
        landing = match & (rank_in == float(k))
        mine = clusters + jnp.sum(jnp.where(landing, target - clusters, 0.0), axis=1, keepdims=True)
        keys.append(mine + (step_row * KEYS).astype(F32))
        blocks.append((from_row * cap + k).astype(F32))
        scales.append((from_row * plan.scale_rows + step_row * cap + k).astype(F32))
    total = plan.total
    key_row = jnp.broadcast_to(jnp.concatenate(keys, axis=0), (total, total))
    key_col = key_row.T
    row = lax.broadcasted_iota(I32, (total, total), 0)
    col = lax.broadcasted_iota(I32, (total, total), 1)
    earlier = (key_row == key_col) & (col < row)
    rank = jnp.sum(jnp.where((key_col < key_row) | earlier, 1.0, 0.0), axis=1, keepdims=True)
    follows = jnp.max(jnp.where(earlier, 1.0, 0.0), axis=1, keepdims=True)
    hit = rank == col.astype(F32)

    def sorted_row(values):
        return jnp.sum(jnp.where(hit, values, 0.0), axis=0, keepdims=True)

    wide = lines * KEYS
    key = jnp.concatenate(keys, axis=0)
    place = lax.broadcasted_iota(I32, (total, wide), 1)
    code = place.astype(F32)
    last = jnp.sum(jnp.where(key <= code, 1.0, 0.0), axis=0, keepdims=True) - 1.0
    last = last - (lax.div(place[:1], KEYS) * plan.each).astype(F32)
    there = jnp.max(jnp.where(key == code, 1.0, 0.0), axis=0, keepdims=True)

    def put(at, values, size):
        tab_ref[at : at + 1, : values.shape[1]] = jnp.clip(values.astype(I32), 0, size - 1)

    put(0, slot_of, slots)
    put(1, sorted_row(jnp.concatenate(blocks, axis=0)), plan.each)
    put(2, sorted_row(jnp.concatenate(scales, axis=0)), group * plan.scale_rows)
    put(3, sorted_row(follows), 2)
    put(4, last, plan.each)
    put(5, there, 2)


def kernel(plan, *refs):
    lines, group, cap = plan.lines, plan.group, plan.cap
    (
        vec_hbm, tiles_hbm, off_ref, col_hbm, row_hbm, up_hbm, down_hbm, coup_hbm, dest_hbm, target_hbm,
        out_ref,
        vec, tiles, col, row, up, down, coup,
        wide, halo, grid, strips, rim, mats, coef, held, held_scale,
        place_scale, send_scale, got_scale, scale_of, send1,
        dest, target, dests, targets, tab_v, tab, run, own, send2, send2_scale, near, turned, lifts,
        load_sem, tab_sem, near_send, near_recv, scale_send, scale_recv,
        one_send, one_recv, two_send, two_recv, twos_send, twos_recv, local_sem,
        *landing,
    ) = refs
    recv1 = landing[:lines]
    recv2 = landing[lines : 2 * lines - 1]
    recv2_scale = landing[2 * lines - 1 :]

    here_x = lax.axis_index("qx")
    here_y = lax.axis_index("qy")
    me_z, me_j = plan.place(here_x, here_y)
    vecs, rows_x, rows_y = vec.shape
    leaf_x, leaf_y = rows_x // LS, rows_y // LS
    leaves = leaf_x * leaf_y
    uppers = leaf_y // 2
    clusters = leaves + uppers
    rank = coup.shape[0]
    half = rank // 2
    lanes = 2 * vecs
    points = LS * LS
    low = lax.broadcasted_iota(I32, (1, lanes), 1) < vecs

    pairs = [
        (vec_hbm, vec),
        (col_hbm, col),
        (up_hbm, up),
        (coup_hbm, coup),
        (row_hbm, row),
        (down_hbm, down),
        (tiles_hbm, tiles),
        (dest_hbm, dest),
        (target_hbm, target),
    ]
    loads = [pltpu.make_async_copy(src, dst, load_sem.at[n]) for n, (src, dst) in enumerate(pairs)]
    for n in (7, 8, 0, 1, 2, 3, 4, 5, 6):
        loads[n].start()

    def at_line(t):
        return plan.where(plan.line(me_z, t), me_j)

    def at_peer(u):
        return plan.where(me_z, plan.peer(me_j, u))

    steps = [(1, 0), (-1, 0), (0, 1), (0, -1), (1, 1), (1, -1), (-1, 1), (-1, -1)]

    def present(dx, dy):
        x = here_x + dx
        y = here_y + dy
        return (x >= 0) & (x < plan.width_x) & (y >= 0) & (y < plan.width_y)

    barrier = pltpu.get_barrier_semaphore()

    def greet(device):
        pl.semaphore_signal(barrier, inc=1, device_id=device, device_id_type=pl.DeviceIdType.MESH)

    for dx, dy in steps:

        @pl.when(present(dx, dy))
        def _():
            greet((here_x + dx, here_y + dy))

    for u in range(1, group):
        greet(at_peer(u))
    for t in plan.hops:
        greet(at_line(t))

    spans = []
    for here, width in ((here_x, plan.width_x), (here_y, plan.width_y)):
        spans.append(1 + (here > 0).astype(I32) + (here < width - 1).astype(I32))
    pl.semaphore_wait(barrier, spans[0] * spans[1] - 1 + group - 1 + len(plan.hops))

    def remote(src, dst, send, recv, device):
        return pltpu.make_async_remote_copy(
            src_ref=src,
            dst_ref=dst,
            send_sem=send,
            recv_sem=recv,
            device_id=device,
            device_id_type=pl.DeviceIdType.MESH,
        )

    def near_copy(n):
        dx, dy = steps[n]
        if dy == 0:
            src = vec.at[:, pl.ds(rows_x - LS if dx > 0 else 0, LS), :]
            dst = halo.at[0 if dx > 0 else 1]
        else:
            side = 1 if dy > 0 else 0
            if dx == 0:
                src = strips.at[side]
                dst = rim.at[1 - side, pl.ds(1, leaf_x)]
            else:
                src = strips.at[side, leaf_x - 1 if dx > 0 else 0]
                dst = rim.at[1 - side, 0 if dx > 0 else leaf_x + 1]
        return remote(src, dst, near_send.at[n], near_recv.at[n], (here_x + dx, here_y + dy))

    def near_start(first, end):
        for n in range(first, end):

            @pl.when(present(*steps[n]))
            def _():
                near_copy(n).start()

    loads[0].wait()
    near_start(0, 2)

    wide[...] = vec[...].astype(F32)

    def to_grid(x, carry):
        plane = wide[:, x, :]
        lines_of = jnp.concatenate([plane, plane], axis=0).T.astype(BF16).reshape(leaf_y, LS, lanes)
        at = pl.multiple_of(lax.rem(x, LS) * LS, LS)
        grid[1 + lax.div(x, LS), 1 : 1 + leaf_y, pl.ds(at, LS), :] = lines_of
        return carry

    lax.fori_loop(0, rows_x, to_grid, 0, unroll=4)
    for side in range(2):
        for i in range(leaf_x):
            block = grid[1 + i, leaf_y if side else 1].reshape(2, LS // 2, LS, lanes)
            strips[side, i] = jnp.where(low, block[0], block[1])
    near_start(2, 8)

    loads[7].wait()
    loads[8].wait()
    tables(plan, clusters, me_z, me_j, dest, target, dests, targets, tab_v)
    tab_copy = pltpu.make_async_copy(tab_v, tab, tab_sem)
    tab_copy.start()

    loads[1].wait()

    def leaf_coef(m, carry):
        i = lax.div(m, leaf_y)
        j = lax.rem(m, leaf_y)
        coef[m] = dot(col[m], grid[1 + i, 1 + j])
        return carry

    lax.fori_loop(0, leaves, leaf_coef, 0, unroll=4)
    loads[2].wait()

    def upper_coef(p, carry):
        children = [i * leaf_y + 2 * p + q for i in range(leaf_x) for q in range(2)]
        left = jnp.concatenate([up[m] for m in children], axis=1)
        right = jnp.concatenate([coef[m] for m in children], axis=0)
        coef[leaves + p] = dot(left_of(left), right_of(right))
        return carry

    lax.fori_loop(0, uppers, upper_coef, 0)

    loads[3].wait()

    def turn(r, carry):
        mats[:, r, :] = jnp.concatenate([coup[r], coup[r + half]], axis=0).T
        return carry

    lax.fori_loop(0, half, turn, 0, unroll=4)

    def contribute(first, count, m):
        left = left_of(mats[pl.ds(first, count)].reshape(count * half, lanes))
        blocks = dot(left, right_of(twice(coef[m]))).reshape(count, half, lanes)
        whole, scale = coded(blocks)
        held[pl.ds(first, count)] = whole
        for q in range(count):
            held_scale[first + q] = scale[q : q + 1]

    def leaf_slots(m, carry):
        contribute(m * K0, K0, m)
        return carry

    def upper_slots(p, carry):
        contribute(leaves * K0 + p * K1, K1, leaves + p)
        return carry

    lax.fori_loop(0, leaves, leaf_slots, 0, unroll=2)
    lax.fori_loop(0, uppers, upper_slots, 0, unroll=2)

    tab_copy.wait()
    place_scale[...] = jnp.zeros_like(place_scale)

    def put_scale(p, carry):
        t = lax.div(p, plan.each)
        q = lax.rem(p, plan.each)
        at = lax.div(q, cap) * plan.scale_rows + t * cap + lax.rem(q, cap)
        place_scale[pl.ds(at, 1), :] = held_scale[tab[0, p]]
        return carry

    lax.fori_loop(0, plan.total, put_scale, 0, unroll=8)
    send_scale[...] = place_scale[...].astype(BF16).reshape(send_scale.shape)

    def scale_copy(u):
        return remote(
            send_scale.at[plan.peer(me_j, u)], got_scale.at[me_j], scale_send.at[u], scale_recv.at[u], at_peer(u)
        )

    def one_copy(t, u):
        return remote(
            send1.at[pl.ds((t * group + plan.peer(me_j, u)) * cap, cap)],
            recv1[t].at[pl.ds(me_j * cap, cap)],
            one_send.at[t, u],
            one_recv.at[t, u],
            at_peer(u),
        )

    def one_local(t):
        return pltpu.make_async_copy(
            send1.at[pl.ds((t * group + me_j) * cap, cap)], recv1[t].at[pl.ds(me_j * cap, cap)], local_sem.at[t]
        )

    scale_local = pltpu.make_async_copy(send_scale.at[me_j], got_scale.at[me_j], local_sem.at[lines])
    scale_local.start()
    for u in range(1, group):
        scale_copy(u).start()

    for t in plan.order:

        def put(p, carry, t=t):
            send1[t * plan.each + p] = held[tab[0, t * plan.each + p]]
            return carry

        lax.fori_loop(0, plan.each, put, 0, unroll=8)
        for u in range(1, group):
            one_copy(t, u).start()
        one_local(t).start()

    loads[4].wait()
    loads[5].wait()

    def turn_row(j, carry):
        pair = jnp.concatenate([row[j], row[leaf_y + j]], axis=0)
        basis = pair.astype(F32).T.astype(BF16)
        turned[j] = jnp.concatenate([basis, basis], axis=1)
        return carry

    lax.fori_loop(0, leaf_y, turn_row, 0)

    def lift(p, carry):
        parts = []
        for i in range(leaf_x):
            for q in range(2):
                mat = down[i * leaf_y + 2 * p + q]
                parts.append(jnp.concatenate([mat[:half], mat[half:]], axis=1))
        lifts[p] = left_of(jnp.concatenate(parts, axis=0))
        return carry

    lax.fori_loop(0, uppers, lift, 0)

    def near_field(first, count):
        def pair(j, carry):
            sums = []
            for i in range(leaf_x):
                m = i * leaf_y + j
                total = None
                for k in range(tiles.shape[1]):
                    o = off_ref[k, i, j]
                    term = dot(tiles[m, k], grid[i + lax.div(o, 3), j + lax.rem(o, 3)])
                    total = term if total is None else total + term
                sums.append(total)
            near[j] = jnp.where(low, sums[0], sums[1])
            return carry

        lax.fori_loop(first, first + count, pair, 0)

    def near_rows():
        for side in range(2):
            keep = present(2 * side - 1, 0)
            wide[:, side * LS : (side + 1) * LS, :] = jnp.where(keep, halo[side].astype(F32), 0.0)

        def to_rows(x, carry):
            plane = wide[:, x, :]
            lines_of = jnp.concatenate([plane, plane], axis=0).T.astype(BF16).reshape(leaf_y, LS, lanes)
            at = pl.multiple_of(lax.rem(x, LS) * LS, LS)
            grid[lax.div(x, LS) * (leaf_x + 1), 1 : 1 + leaf_y, pl.ds(at, LS), :] = lines_of
            return carry

        lax.fori_loop(0, 2 * LS, to_rows, 0, unroll=4)

    def near_edges():
        for n, (dx, dy) in enumerate(steps):

            @pl.when(present(-dx, -dy))
            def _():
                near_copy(n).wait_recv()

        for side in range(2):
            dy = 1 if side else -1
            for i in range(leaf_x + 2):
                dx = -1 if i == 0 else (1 if i == leaf_x + 1 else 0)
                keep = present(dx, dy)
                value = jnp.where(keep, rim[side, i].astype(F32), 0.0).reshape(points // 2, lanes)
                other = swapped(value)
                y = leaf_y + 1 if side else 0
                grid[i, y, : points // 2, :] = jnp.where(low, value, other).astype(BF16)
                grid[i, y, points // 2 :, :] = jnp.where(low, other, value).astype(BF16)

    scale_local.wait()
    for u in range(1, group):
        scale_copy(u).wait_recv()
    scale_of[...] = got_scale[...].astype(F32).reshape(scale_of.shape) * (1.0 / STEP)

    def two_copy(t):
        return remote(send2.at[t - 1], recv2[t - 1], two_send.at[t], two_recv.at[t], at_line(plan.hop(t)))

    def twos_copy(t):
        return remote(send2_scale.at[t - 1], recv2_scale[t - 1], twos_send.at[t], twos_recv.at[t], at_line(plan.hop(t)))

    def merge(t):
        two_copy(t).wait_recv()
        twos_copy(t).wait_recv()
        place_scale[: send2_scale.shape[1], :] = recv2_scale[t - 1][...].astype(F32) * (1.0 / STEP)

        def gather(n, carry):
            own[n] = own[n] + decoded(recv2[t - 1][n]) * place_scale[pl.ds(n, 1), :]
            return carry

        lax.fori_loop(0, clusters, gather, 0, unroll=4)

    done = 0
    for step, t in enumerate(plan.order):
        one_local(t).wait()
        for u in range(1, group):
            one_copy(t, u).wait_recv()

        def collect(i, total, t=t):
            at = t * plan.each + i
            block = decoded(recv1[t][tab[1, at]]) * scale_of[tab[2, at]]
            total = total * tab[3, at].astype(F32) + block
            run[i] = total
            return total

        lax.fori_loop(0, plan.each, collect, jnp.zeros((half, lanes), F32), unroll=4)

        def pick(n, carry, t=t):
            own[n] = run[tab[4, t * KEYS + n]] * tab[5, t * KEYS + n].astype(F32)
            return carry

        lax.fori_loop(0, clusters, pick, 0, unroll=4)
        if step:
            count = leaf_y - done if step == lines - 1 else min(-(-leaf_y // max(lines - 1, 1)), leaf_y - done)
            near_field(done, count)
            done += count
        for other in plan.order:
            if other and plan.into(other) == t:
                merge(other)
        if t:
            send2_scale[t - 1] = jnp.zeros(send2_scale.shape[1:], BF16)
            group_of = 4

            def pack(g, carry, t=t):
                whole, scale = coded(own[pl.ds(g * group_of, group_of)])
                send2[t - 1, pl.ds(g * group_of, group_of)] = whole
                for q in range(group_of):
                    place_scale[pl.ds(g * group_of + q, 1), :] = scale[q : q + 1]
                return carry

            lax.fori_loop(0, clusters // group_of, pack, 0)
            send2_scale[t - 1] = place_scale[: send2_scale.shape[1], :].astype(BF16)
            two_copy(t).start()
            twos_copy(t).start()
        if step == 0:
            near_edges()
            near_rows()
            loads[6].wait()
            if lines == 1:
                near_field(0, leaf_y)

    def descend(p, carry):
        top = own[leaves + p]
        extra = dot(lifts[p], right_of(spread(top, top))).reshape(2 * leaf_x, half, lanes)
        for i in range(leaf_x):
            for q in range(2):
                m = i * leaf_y + 2 * p + q
                own[m] = own[m] + extra[2 * i + q]
        return carry

    lax.fori_loop(0, uppers, descend, 0)

    def far(j, carry):
        high, rest = halves(spread(own[j], own[leaf_y + j]))
        near[j] = near[j] + dot(turned[j], jnp.concatenate([high, rest], axis=0))
        return carry

    lax.fori_loop(0, leaf_y, far, 0, unroll=2)

    def put_out(x, carry):
        line = near[:, pl.ds(pl.multiple_of(x * LS, LS), LS), :].reshape(rows_y, lanes).T
        out_ref[:, x, :] = line[:vecs]
        out_ref[:, LS + x, :] = line[vecs:]
        return carry

    lax.fori_loop(0, LS, put_out, 0, unroll=2)

    for n in range(8):

        @pl.when(present(*steps[n]))
        def _():
            near_copy(n).wait_send()

    for u in range(1, group):
        scale_copy(u).wait_send()
        for t in range(lines):
            one_copy(t, u).wait_send()
    for t in range(1, lines):
        two_copy(t).wait_send()
        twos_copy(t).wait_send()


def body(
    vectors,
    near_tiles,
    near_offset,
    col_basis,
    row_basis,
    up_transfer,
    down_transfer,
    coupling,
    couple_dest,
    couple_target,
):
    vecs, rows_x, rows_y = vectors.shape
    leaf_x, leaf_y = rows_x // LS, rows_y // LS
    leaves = leaf_x * leaf_y
    uppers = leaf_y // 2
    clusters = leaves + uppers
    rank = coupling.shape[2]
    half = rank // 2
    slots = coupling.shape[1]
    near_count = near_tiles.shape[2]
    points = LS * LS
    lanes = 2 * vecs
    plan = Plan(lax.axis_size("qx"), lax.axis_size("qy"), slots)
    lines, group, cap = plan.lines, plan.group, plan.cap
    scale2 = -(-clusters // 16) * 16
    devices = couple_dest.shape[0]
    width = max(plan.total, lines * KEYS)
    vmem, dma = pltpu.VMEM, pltpu.SemaphoreType.DMA
    int16 = jnp.int16
    scratch = [
        vmem((vecs, rows_x, rows_y), BF16),
        vmem((leaves, near_count, points, points), BF16),
        vmem((leaves, rank, points), BF16),
        vmem((leaves, rank, points), BF16),
        vmem((leaves, rank, rank), F32),
        vmem((leaves, rank, rank), F32),
        vmem((rank, rank, slots), F32),
        vmem((vecs, rows_x, rows_y), F32),
        vmem((2, vecs, LS, rows_y), BF16),
        vmem((leaf_x + 2, leaf_y + 2, points, lanes), BF16),
        vmem((2, leaf_x, LS // 2, LS, lanes), BF16),
        vmem((2, leaf_x + 2, LS // 2, LS, lanes), BF16),
        vmem((slots, half, lanes), F32),
        vmem((clusters, rank, lanes), F32),
        vmem((slots, half, lanes), int16),
        vmem((slots, 1, lanes), F32),
        vmem((group * plan.scale_rows, lanes), F32),
        vmem((group, plan.scale_rows, lanes), BF16),
        vmem((group, plan.scale_rows, lanes), BF16),
        vmem((group * plan.scale_rows, 1, lanes), F32),
        vmem((plan.total, half, lanes), int16),
        vmem((devices, slots), I32),
        vmem((devices, slots), I32),
        vmem((group, slots), I32),
        vmem((group, slots), F32),
        vmem((8, width), I32),
        pltpu.SMEM((8, width), I32),
        vmem((plan.each, half, lanes), F32),
        vmem((clusters, half, lanes), F32),
        vmem((max(lines - 1, 1), clusters, half, lanes), int16),
        vmem((max(lines - 1, 1), scale2, lanes), BF16),
        vmem((leaf_y, points, lanes), F32),
        vmem((leaf_y, points, 4 * rank), BF16),
        vmem((uppers, 2 * leaf_x * half, 6 * rank), BF16),
        dma((9,)),
        dma(()),
        dma((8,)),
        dma((8,)),
        dma((group,)),
        dma((group,)),
        dma((lines, group)),
        dma((lines, group)),
        dma((lines,)),
        dma((lines,)),
        dma((lines,)),
        dma((lines,)),
        dma((lines + 1,)),
    ]
    scratch += [vmem((plan.each, half, lanes), int16)] * lines
    scratch += [vmem((clusters, half, lanes), int16)] * (lines - 1)
    scratch += [vmem((scale2, lanes), BF16)] * (lines - 1)
    return pl.pallas_call(
        lambda *refs: kernel(plan, *refs),
        out_shape=jax.ShapeDtypeStruct((vecs, rows_x, rows_y), F32),
        in_specs=[ANY, ANY, SM, ANY, ANY, ANY, ANY, ANY, ANY, ANY],
        out_specs=VM,
        scratch_shapes=scratch,
        compiler_params=pltpu.CompilerParams(collective_id=0, has_side_effects=True, vmem_limit_bytes=60 << 20),
        name="product",
    )(
        vectors,
        near_tiles.reshape(leaves, near_count, points, points),
        near_offset.transpose(2, 0, 1),
        col_basis.reshape(leaves, rank, points),
        row_basis.reshape(leaves, rank, points),
        up_transfer.reshape(leaves, rank, rank),
        down_transfer.reshape(leaves, rank, rank),
        coupling[0].transpose(1, 2, 0),
        couple_dest,
        couple_target,
    )


def solution(mesh):
    return jax.shard_map(
        body,
        mesh=mesh,
        in_specs=(
            P(None, "qx", "qy"),
            P("qx", "qy", None, None, None),
            P("qx", "qy", None),
            P("qx", "qy", None, None),
            P("qx", "qy", None, None),
            P("qx", "qy", None, None),
            P("qx", "qy", None, None),
            P(("qx", "qy"), None, None, None),
            P(),
            P(),
        ),
        out_specs=P(None, "qx", "qy"),
        check_vma=False,
    )
```

```python
import jax
import jax.numpy as jnp
from jax import lax
from jax.experimental import pallas as pl
from jax.experimental.pallas import tpu as pltpu
from jax.sharding import PartitionSpec as P

LS = 16
K0 = 6
K1 = 8
KEYS = 32
STEP = 32767.0

ANY = pl.BlockSpec(memory_space=pl.ANY)
VM = pl.BlockSpec(memory_space=pltpu.VMEM)
SM = pl.BlockSpec(memory_space=pltpu.SMEM)
F32 = jnp.float32
BF16 = jnp.bfloat16
I32 = jnp.int32


def halves(value):
    high = value.astype(BF16)
    return high, (value - high.astype(F32)).astype(BF16)


def left_of(value):
    high, low = halves(value)
    return jnp.concatenate([high, low, high], axis=1)


def right_of(value):
    high, low = halves(value)
    return jnp.concatenate([high, high, low], axis=0)


def dot(left, right):
    return jnp.dot(left, right, preferred_element_type=F32)


def swapped(value):
    half = value.shape[-1] // 2
    return jnp.concatenate([value[..., half:], value[..., :half]], axis=-1)


def spread(first, second):
    low = lax.broadcasted_iota(I32, first.shape, 1) < first.shape[1] // 2
    return jnp.concatenate(
        [
            jnp.where(low, first, 0.0),
            jnp.where(low, swapped(first), 0.0),
            jnp.where(low, 0.0, swapped(second)),
            jnp.where(low, 0.0, second),
        ],
        axis=0,
    )


def twice(value):
    low = lax.broadcasted_iota(I32, value.shape, 1) < value.shape[1] // 2
    return jnp.concatenate([jnp.where(low, value, 0.0), jnp.where(low, 0.0, value)], axis=0)


def coded(blocks):
    peak = jnp.max(jnp.abs(blocks), axis=1)
    scale = (jnp.maximum(peak, 1e-30) * 1.004).astype(BF16).astype(F32)
    inverse = STEP / scale
    whole = jnp.round(blocks * inverse[:, None, :]).astype(I32).astype(jnp.int16)
    return whole, scale


def decoded(value):
    return value.astype(I32).astype(F32)


class Plan:
    def __init__(self, width_x, width_y, slots):
        part = max(1, width_y // 2)
        if width_x % part:
            part = 1
        stride = part if width_x % (part * part) == 0 else 1
        self.width_x, self.width_y = width_x, width_y
        self.part, self.stride = part, stride
        self.group = part * width_y
        self.lines = width_x // part
        devices = width_x * width_y
        self.cap = (slots + devices - 1) // devices
        self.total = devices * self.cap
        self.each = self.group * self.cap
        self.scale_rows = -(-(self.lines * self.cap) // 16) * 16
        self.xor_line = self.lines & (self.lines - 1) == 0
        self.xor_group = self.group & (self.group - 1) == 0
        self.order = list(range(self.lines - 1, -1, -1))
        self.hops = sorted({self.hop(t) for t in range(1, self.lines)})

    def hop(self, t):
        return t & -t if self.xor_line else t

    def into(self, t):
        return t - self.hop(t)

    def line(self, z, t):
        return z ^ t if self.xor_line else lax.rem(z + t, self.lines)

    def line_step(self, z, other):
        return other ^ z if self.xor_line else lax.rem(other - z + self.lines, self.lines)

    def peer(self, j, u):
        return j ^ u if self.xor_group else lax.rem(j + u, self.group)

    def place(self, x, y):
        low = lax.rem(x, self.stride)
        rest = lax.div(x, self.stride)
        return lax.div(rest, self.part) * self.stride + low, lax.rem(rest, self.part) * self.width_y + y

    def where(self, z, j):
        high, low = lax.div(z, self.stride), lax.rem(z, self.stride)
        return (high * self.part + lax.div(j, self.width_y)) * self.stride + low, lax.rem(j, self.width_y)

    def index(self, z, j):
        x, y = self.where(z, j)
        return x * self.width_y + y


def tables(plan, clusters, me_z, me_j, dest_ref, target_ref, dests_ref, targets_ref, tab_ref, order_ref):
    slots = dest_ref.shape[1]
    cap, group, lines = plan.cap, plan.group, plan.lines
    own = dest_ref[pl.ds(plan.index(me_z, me_j), 1), :]
    across = jnp.broadcast_to(own.astype(F32), (slots, slots))
    down = across.T
    row = lax.broadcasted_iota(I32, (slots, slots), 0)
    col = lax.broadcasted_iota(I32, (slots, slots), 1)
    order = jnp.sum(jnp.where((across == down) & (col < row), 1.0, 0.0), axis=1, keepdims=True)
    dest = down[:, :1].astype(I32)
    whole = jnp.maximum(dest, 0)
    line, peer = plan.place(lax.div(whole, plan.width_y), lax.rem(whole, plan.width_y))
    step = plan.line_step(me_z, line)
    scale_place = jnp.where(dest >= 0, peer * plan.scale_rows + step * cap + order.astype(I32), -1)
    rows = order_ref.shape[1]
    order_ref[...] = jnp.where(
        scale_place == lax.broadcasted_iota(I32, (slots, rows), 1), 1.0, 0.0
    ).astype(BF16)
    place = (step * group + peer) * cap + order.astype(I32)
    place = jnp.where(dest >= 0, place, -1)
    lane = lax.broadcasted_iota(I32, (slots, plan.total), 1)
    slot = lax.broadcasted_iota(I32, (slots, plan.total), 0).astype(F32)
    slot_of = jnp.sum(jnp.where(place == lane, slot, 0.0), axis=0, keepdims=True)

    for j in range(group):
        at = plan.index(me_z, j)
        dests_ref[j : j + 1, :] = dest_ref[pl.ds(at, 1), :]
        targets_ref[j : j + 1, :] = target_ref[pl.ds(at, 1), :].astype(F32)
    dests, targets = dests_ref[...], targets_ref[...]
    match = jnp.concatenate([dests == plan.index(plan.line(me_z, t), me_j) for t in range(lines)], axis=0)
    target = jnp.concatenate([targets] * lines, axis=0)
    before = jnp.where(row < col, 1.0, 0.0).astype(BF16)
    rank_in = dot(jnp.where(match, 1.0, 0.0).astype(BF16), before)
    rows = lines * group
    step_row = lax.div(lax.broadcasted_iota(I32, (rows, 1), 0), group)
    from_row = lax.rem(lax.broadcasted_iota(I32, (rows, 1), 0), group)
    keys, blocks, scales = [], [], []
    for k in range(cap):
        landing = match & (rank_in == float(k))
        mine = clusters + jnp.sum(jnp.where(landing, target - clusters, 0.0), axis=1, keepdims=True)
        keys.append(mine + (step_row * KEYS).astype(F32))
        blocks.append((from_row * cap + k).astype(F32))
        scales.append((from_row * plan.scale_rows + step_row * cap + k).astype(F32))
    total = plan.total
    key_row = jnp.broadcast_to(jnp.concatenate(keys, axis=0), (total, total))
    key_col = key_row.T
    row = lax.broadcasted_iota(I32, (total, total), 0)
    col = lax.broadcasted_iota(I32, (total, total), 1)
    earlier = (key_row == key_col) & (col < row)
    rank = jnp.sum(jnp.where((key_col < key_row) | earlier, 1.0, 0.0), axis=1, keepdims=True)
    follows = jnp.max(jnp.where(earlier, 1.0, 0.0), axis=1, keepdims=True)
    hit = rank == col.astype(F32)

    def sorted_row(values):
        return jnp.sum(jnp.where(hit, values, 0.0), axis=0, keepdims=True)

    wide = lines * KEYS
    key = jnp.concatenate(keys, axis=0)
    place = lax.broadcasted_iota(I32, (total, wide), 1)
    code = place.astype(F32)
    last = jnp.sum(jnp.where(key <= code, 1.0, 0.0), axis=0, keepdims=True) - 1.0
    last = last - (lax.div(place[:1], KEYS) * plan.each).astype(F32)
    there = jnp.max(jnp.where(key == code, 1.0, 0.0), axis=0, keepdims=True)

    def put(at, values, size):
        tab_ref[at : at + 1, : values.shape[1]] = jnp.clip(values.astype(I32), 0, size - 1)

    put(0, slot_of, slots)
    put(1, sorted_row(jnp.concatenate(blocks, axis=0)), plan.each)
    put(2, sorted_row(jnp.concatenate(scales, axis=0)), group * plan.scale_rows)
    put(3, sorted_row(follows), 2)
    put(4, last, plan.each)
    put(5, there, 2)


def kernel(plan, *refs):
    lines, group, cap = plan.lines, plan.group, plan.cap
    (
        vec_hbm, tiles_hbm, off_ref, col_hbm, row_hbm, up_hbm, down_hbm, coup_hbm, dest_hbm, target_hbm,
        out_hbm,
        vec, tiles, col, row, up, down, coup,
        wide, halo, grid, strips, rim, mats, coef, held, held_scale,
        place_scale, send_scale, got_scale, scale_of, send1,
        dest, target, dests, targets, tab_v, order_of, tab, run, own, send2, send2_scale, near, turned, lifts,
        load_sem, tab_sem, near_send, near_recv, scale_send, scale_recv,
        one_send, one_recv, two_send, two_recv, twos_send, twos_recv, local_sem, out_sem,
        *landing,
    ) = refs
    recv1 = landing[:lines]
    recv2 = landing[lines : 2 * lines - 1]
    recv2_scale = landing[2 * lines - 1 :]

    here_x = lax.axis_index("qx")
    here_y = lax.axis_index("qy")
    me_z, me_j = plan.place(here_x, here_y)
    vecs, rows_x, rows_y = vec.shape
    leaf_x, leaf_y = rows_x // LS, rows_y // LS
    leaves = leaf_x * leaf_y
    uppers = leaf_y // 2
    clusters = leaves + uppers
    rank = coup.shape[0]
    half = rank // 2
    lanes = 2 * vecs
    points = LS * LS
    low = lax.broadcasted_iota(I32, (1, lanes), 1) < vecs

    pairs = [
        (vec_hbm, vec),
        (col_hbm, col),
        (up_hbm, up),
        (coup_hbm, coup),
        (row_hbm, row),
        (down_hbm, down),
        (tiles_hbm, tiles),
        (dest_hbm, dest),
        (target_hbm, target),
    ]
    loads = [pltpu.make_async_copy(src, dst, load_sem.at[n]) for n, (src, dst) in enumerate(pairs)]
    for n in (7, 8, 0):
        loads[n].start()

    def at_line(t):
        return plan.where(plan.line(me_z, t), me_j)

    def at_peer(u):
        return plan.where(me_z, plan.peer(me_j, u))

    steps = [(1, 0), (-1, 0), (0, 1), (0, -1), (1, 1), (1, -1), (-1, 1), (-1, -1)]

    def present(dx, dy):
        x = here_x + dx
        y = here_y + dy
        return (x >= 0) & (x < plan.width_x) & (y >= 0) & (y < plan.width_y)

    barrier = pltpu.get_barrier_semaphore()

    def greet(device):
        pl.semaphore_signal(barrier, inc=1, device_id=device, device_id_type=pl.DeviceIdType.MESH)

    for dx, dy in steps:

        @pl.when(present(dx, dy))
        def _():
            greet((here_x + dx, here_y + dy))

    for u in range(1, group):
        greet(at_peer(u))
    for t in plan.hops:
        greet(at_line(t))

    loads[7].wait()
    loads[8].wait()
    tables(plan, clusters, me_z, me_j, dest, target, dests, targets, tab_v, order_of)
    tab_copy = pltpu.make_async_copy(tab_v, tab, tab_sem)
    tab_copy.start()
    loads[0].wait()
    for n in (1, 2, 3, 4, 5, 6):
        loads[n].start()

    spans = []
    for here, width in ((here_x, plan.width_x), (here_y, plan.width_y)):
        spans.append(1 + (here > 0).astype(I32) + (here < width - 1).astype(I32))
    pl.semaphore_wait(barrier, spans[0] * spans[1] - 1 + group - 1 + len(plan.hops))

    def remote(src, dst, send, recv, device):
        return pltpu.make_async_remote_copy(
            src_ref=src,
            dst_ref=dst,
            send_sem=send,
            recv_sem=recv,
            device_id=device,
            device_id_type=pl.DeviceIdType.MESH,
        )

    def near_copy(n):
        dx, dy = steps[n]
        if dy == 0:
            src = vec.at[:, pl.ds(rows_x - LS if dx > 0 else 0, LS), :]
            dst = halo.at[0 if dx > 0 else 1]
        else:
            side = 1 if dy > 0 else 0
            if dx == 0:
                src = strips.at[side]
                dst = rim.at[1 - side, pl.ds(1, leaf_x)]
            else:
                src = strips.at[side, leaf_x - 1 if dx > 0 else 0]
                dst = rim.at[1 - side, 0 if dx > 0 else leaf_x + 1]
        return remote(src, dst, near_send.at[n], near_recv.at[n], (here_x + dx, here_y + dy))

    def near_start(first, end):
        for n in range(first, end):

            @pl.when(present(*steps[n]))
            def _():
                near_copy(n).start()

    near_start(0, 2)

    wide[...] = vec[...].astype(F32)

    def to_grid(x, carry):
        plane = wide[:, x, :]
        lines_of = jnp.concatenate([plane, plane], axis=0).T.astype(BF16).reshape(leaf_y, LS, lanes)
        at = pl.multiple_of(lax.rem(x, LS) * LS, LS)
        grid[1 + lax.div(x, LS), 1 : 1 + leaf_y, pl.ds(at, LS), :] = lines_of
        return carry

    lax.fori_loop(0, rows_x, to_grid, 0, unroll=4)
    for side in range(2):
        for i in range(leaf_x):
            block = grid[1 + i, leaf_y if side else 1].reshape(2, LS // 2, LS, lanes)
            strips[side, i] = jnp.where(low, block[0], block[1])
    near_start(2, 8)

    loads[1].wait()

    def leaf_coef(m, carry):
        i = lax.div(m, leaf_y)
        j = lax.rem(m, leaf_y)
        coef[m] = dot(col[m], grid[1 + i, 1 + j])
        return carry

    lax.fori_loop(0, leaves, leaf_coef, 0, unroll=4)
    loads[2].wait()

    def upper_coef(p, carry):
        children = [i * leaf_y + 2 * p + q for i in range(leaf_x) for q in range(2)]
        left = jnp.concatenate([up[m] for m in children], axis=1)
        right = jnp.concatenate([coef[m] for m in children], axis=0)
        coef[leaves + p] = dot(left_of(left), right_of(right))
        return carry

    lax.fori_loop(0, uppers, upper_coef, 0, unroll=4)

    loads[3].wait()

    def turn(r, carry):
        mats[:, r, :] = jnp.concatenate([coup[r], coup[r + half]], axis=0).T
        return carry

    lax.fori_loop(0, half, turn, 0, unroll=8)

    def contribute(first, count, m):
        left = left_of(mats[pl.ds(first, count)].reshape(count * half, lanes))
        blocks = dot(left, right_of(twice(coef[m]))).reshape(count, half, lanes)
        whole, scale = coded(blocks)
        held[pl.ds(first, count)] = whole
        for q in range(count):
            held_scale[pl.ds(first + q, 1), :] = scale[q : q + 1]

    def leaf_slots(m, carry):
        contribute(m * K0, K0, m)
        return carry

    def upper_slots(p, carry):
        contribute(leaves * K0 + p * K1, K1, leaves + p)
        return carry

    lax.fori_loop(0, leaves, leaf_slots, 0, unroll=4)
    lax.fori_loop(0, uppers, upper_slots, 0, unroll=4)

    tab_copy.wait()
    ordered = lax.dot_general(
        order_of[...], held_scale[...].astype(BF16), (((0,), (0,)), ((), ())), preferred_element_type=F32
    )
    send_scale[...] = ordered.astype(BF16).reshape(send_scale.shape)

    def scale_copy(u):
        return remote(
            send_scale.at[plan.peer(me_j, u)], got_scale.at[me_j], scale_send.at[u], scale_recv.at[u], at_peer(u)
        )

    def one_copy(t, u):
        return remote(
            send1.at[pl.ds((t * group + plan.peer(me_j, u)) * cap, cap)],
            recv1[t].at[pl.ds(me_j * cap, cap)],
            one_send.at[t, u],
            one_recv.at[t, u],
            at_peer(u),
        )

    def one_local(t):
        return pltpu.make_async_copy(
            send1.at[pl.ds((t * group + me_j) * cap, cap)], recv1[t].at[pl.ds(me_j * cap, cap)], local_sem.at[t]
        )

    scale_local = pltpu.make_async_copy(send_scale.at[me_j], got_scale.at[me_j], local_sem.at[lines])
    scale_local.start()
    for u in range(1, group):
        scale_copy(u).start()

    for t in plan.order:

        def put(p, carry, t=t):
            send1[t * plan.each + p] = held[tab[0, t * plan.each + p]]
            return carry

        lax.fori_loop(0, plan.each, put, 0, unroll=16)
        for u in range(1, group):
            one_copy(t, u).start()
        one_local(t).start()

    loads[4].wait()
    loads[5].wait()

    def turn_row(j, carry):
        pair = jnp.concatenate([row[j], row[leaf_y + j]], axis=0)
        basis = pair.astype(F32).T.astype(BF16)
        turned[j] = jnp.concatenate([basis, basis], axis=1)
        return carry

    lax.fori_loop(0, leaf_y, turn_row, 0, unroll=2)

    def lift(p, carry):
        parts = []
        for i in range(leaf_x):
            for q in range(2):
                mat = down[i * leaf_y + 2 * p + q]
                parts.append(jnp.concatenate([mat[:half], mat[half:]], axis=1))
        lifts[p] = left_of(jnp.concatenate(parts, axis=0))
        return carry

    lax.fori_loop(0, uppers, lift, 0, unroll=2)

    def near_field(first, count):
        def pair(j, carry):
            sums = []
            for i in range(leaf_x):
                m = i * leaf_y + j
                total = None
                for k in range(tiles.shape[1]):
                    o = off_ref[k, i, j]
                    term = dot(tiles[m, k], grid[i + lax.div(o, 3), j + lax.rem(o, 3)])
                    total = term if total is None else total + term
                sums.append(total)
            near[j] = jnp.where(low, sums[0], sums[1])
            return carry

        lax.fori_loop(first, first + count, pair, 0)

    def near_rows():
        for side in range(2):
            keep = present(2 * side - 1, 0)
            wide[:, side * LS : (side + 1) * LS, :] = jnp.where(keep, halo[side].astype(F32), 0.0)

        def to_rows(x, carry):
            plane = wide[:, x, :]
            lines_of = jnp.concatenate([plane, plane], axis=0).T.astype(BF16).reshape(leaf_y, LS, lanes)
            at = pl.multiple_of(lax.rem(x, LS) * LS, LS)
            grid[lax.div(x, LS) * (leaf_x + 1), 1 : 1 + leaf_y, pl.ds(at, LS), :] = lines_of
            return carry

        lax.fori_loop(0, 2 * LS, to_rows, 0, unroll=4)

    def near_edges():
        for n, (dx, dy) in enumerate(steps):

            @pl.when(present(-dx, -dy))
            def _():
                near_copy(n).wait_recv()

        for side in range(2):
            dy = 1 if side else -1
            for i in range(leaf_x + 2):
                dx = -1 if i == 0 else (1 if i == leaf_x + 1 else 0)
                keep = present(dx, dy)
                value = jnp.where(keep, rim[side, i].astype(F32), 0.0).reshape(points // 2, lanes)
                other = swapped(value)
                y = leaf_y + 1 if side else 0
                grid[i, y, : points // 2, :] = jnp.where(low, value, other).astype(BF16)
                grid[i, y, points // 2 :, :] = jnp.where(low, other, value).astype(BF16)

    scale_local.wait()
    for u in range(1, group):
        scale_copy(u).wait_recv()
    scale_of[...] = got_scale[...].astype(F32).reshape(scale_of.shape) * (1.0 / STEP)

    def two_copy(t):
        return remote(send2.at[t - 1], recv2[t - 1], two_send.at[t], two_recv.at[t], at_line(plan.hop(t)))

    def twos_copy(t):
        return remote(send2_scale.at[t - 1], recv2_scale[t - 1], twos_send.at[t], twos_recv.at[t], at_line(plan.hop(t)))

    def merge(t):
        two_copy(t).wait_recv()
        twos_copy(t).wait_recv()
        place_scale[...] = recv2_scale[t - 1][...].astype(F32) * (1.0 / STEP)

        def gather(n, carry):
            own[n] = own[n] + decoded(recv2[t - 1][n]) * place_scale[pl.ds(n, 1), :]
            return carry

        lax.fori_loop(0, clusters, gather, 0, unroll=10)

    place_scale[...] = jnp.zeros_like(place_scale)
    done = 0
    for step, t in enumerate(plan.order):
        one_local(t).wait()
        for u in range(1, group):
            one_copy(t, u).wait_recv()

        def collect(i, total, t=t):
            at = t * plan.each + i
            block = decoded(recv1[t][tab[1, at]]) * scale_of[tab[2, at]]
            total = total * tab[3, at].astype(F32) + block
            run[i] = total
            return total

        lax.fori_loop(0, plan.each, collect, jnp.zeros((half, lanes), F32), unroll=8)

        def pick(n, carry, t=t):
            own[n] = run[tab[4, t * KEYS + n]] * tab[5, t * KEYS + n].astype(F32)
            return carry

        lax.fori_loop(0, clusters, pick, 0, unroll=10)
        if step:
            count = leaf_y - done if step == lines - 1 else min(-(-leaf_y // max(lines - 1, 1)), leaf_y - done)
            near_field(done, count)
            done += count
        for other in plan.order:
            if other and plan.into(other) == t:
                merge(other)
        if t:
            group_of = 4

            def pack(g, carry, t=t):
                whole, scale = coded(own[pl.ds(g * group_of, group_of)])
                send2[t - 1, pl.ds(g * group_of, group_of)] = whole
                for q in range(group_of):
                    place_scale[pl.ds(g * group_of + q, 1), :] = scale[q : q + 1]
                return carry

            lax.fori_loop(0, clusters // group_of, pack, 0, unroll=5)
            send2_scale[t - 1] = place_scale[...].astype(BF16)
            two_copy(t).start()
            twos_copy(t).start()
        if step == 0:
            near_edges()
            near_rows()
            loads[6].wait()
            if lines == 1:
                near_field(0, leaf_y)

    def descend(p, carry):
        top = own[leaves + p]
        extra = dot(lifts[p], right_of(spread(top, top))).reshape(2 * leaf_x, half, lanes)
        for i in range(leaf_x):
            for q in range(2):
                m = i * leaf_y + 2 * p + q
                own[m] = own[m] + extra[2 * i + q]
        return carry

    lax.fori_loop(0, uppers, descend, 0, unroll=4)

    def out_copy(j):
        return pltpu.make_async_copy(near.at[j], out_hbm.at[j], out_sem.at[j])

    for j in range(leaf_y):
        high, rest = halves(spread(own[j], own[leaf_y + j]))
        near[j] = near[j] + dot(turned[j], jnp.concatenate([high, rest], axis=0))
        out_copy(j).start()

    for j in range(leaf_y):
        out_copy(j).wait()

    for n in range(8):

        @pl.when(present(*steps[n]))
        def _():
            near_copy(n).wait_send()

    for u in range(1, group):
        scale_copy(u).wait_send()
        for t in range(lines):
            one_copy(t, u).wait_send()
    for t in range(1, lines):
        two_copy(t).wait_send()
        twos_copy(t).wait_send()


def turn_out(sum_ref, out_ref):
    vecs = out_ref.shape[0]
    for x in range(out_ref.shape[2]):
        line = sum_ref[:, x * LS : (x + 1) * LS, :].reshape(out_ref.shape[3], 2 * vecs).T
        out_ref[:, 0, x, :] = line[:vecs]
        out_ref[:, 1, x, :] = line[vecs:]


def body(
    vectors,
    near_tiles,
    near_offset,
    col_basis,
    row_basis,
    up_transfer,
    down_transfer,
    coupling,
    couple_dest,
    couple_target,
):
    vecs, rows_x, rows_y = vectors.shape
    leaf_x, leaf_y = rows_x // LS, rows_y // LS
    leaves = leaf_x * leaf_y
    uppers = leaf_y // 2
    clusters = leaves + uppers
    rank = coupling.shape[2]
    half = rank // 2
    slots = coupling.shape[1]
    near_count = near_tiles.shape[2]
    points = LS * LS
    lanes = 2 * vecs
    plan = Plan(lax.axis_size("qx"), lax.axis_size("qy"), slots)
    lines, group, cap = plan.lines, plan.group, plan.cap
    scale2 = -(-clusters // 16) * 16
    devices = couple_dest.shape[0]
    width = max(plan.total, lines * KEYS)
    vmem, dma = pltpu.VMEM, pltpu.SemaphoreType.DMA
    int16 = jnp.int16
    scratch = [
        vmem((vecs, rows_x, rows_y), BF16),
        vmem((leaves, near_count, points, points), BF16),
        vmem((leaves, rank, points), BF16),
        vmem((leaves, rank, points), BF16),
        vmem((leaves, rank, rank), F32),
        vmem((leaves, rank, rank), F32),
        vmem((rank, rank, slots), F32),
        vmem((vecs, rows_x, rows_y), F32),
        vmem((2, vecs, LS, rows_y), BF16),
        vmem((leaf_x + 2, leaf_y + 2, points, lanes), BF16),
        vmem((2, leaf_x, LS // 2, LS, lanes), BF16),
        vmem((2, leaf_x + 2, LS // 2, LS, lanes), BF16),
        vmem((slots, half, lanes), F32),
        vmem((clusters, rank, lanes), F32),
        vmem((slots, half, lanes), int16),
        vmem((slots, lanes), F32),
        vmem((scale2, lanes), F32),
        vmem((group, plan.scale_rows, lanes), BF16),
        vmem((group, plan.scale_rows, lanes), BF16),
        vmem((group * plan.scale_rows, 1, lanes), F32),
        vmem((plan.total, half, lanes), int16),
        vmem((devices, slots), I32),
        vmem((devices, slots), I32),
        vmem((group, slots), I32),
        vmem((group, slots), F32),
        vmem((8, width), I32),
        vmem((slots, group * plan.scale_rows), BF16),
        pltpu.SMEM((8, width), I32),
        vmem((plan.each, half, lanes), F32),
        vmem((clusters, half, lanes), F32),
        vmem((max(lines - 1, 1), clusters, half, lanes), int16),
        vmem((max(lines - 1, 1), scale2, lanes), BF16),
        vmem((leaf_y, points, lanes), F32),
        vmem((leaf_y, points, 4 * rank), BF16),
        vmem((uppers, 2 * leaf_x * half, 6 * rank), BF16),
        dma((9,)),
        dma(()),
        dma((8,)),
        dma((8,)),
        dma((group,)),
        dma((group,)),
        dma((lines, group)),
        dma((lines, group)),
        dma((lines,)),
        dma((lines,)),
        dma((lines,)),
        dma((lines,)),
        dma((lines + 1,)),
        dma((leaf_y,)),
    ]
    scratch += [vmem((plan.each, half, lanes), int16)] * lines
    scratch += [vmem((clusters, half, lanes), int16)] * (lines - 1)
    scratch += [vmem((scale2, lanes), BF16)] * (lines - 1)
    summed = pl.pallas_call(
        lambda *refs: kernel(plan, *refs),
        out_shape=jax.ShapeDtypeStruct((leaf_y, points, lanes), F32),
        in_specs=[ANY, ANY, SM, ANY, ANY, ANY, ANY, ANY, ANY, ANY],
        out_specs=ANY,
        scratch_shapes=scratch,
        compiler_params=pltpu.CompilerParams(collective_id=0, has_side_effects=True, vmem_limit_bytes=60 << 20),
        name="product",
    )(
        vectors,
        near_tiles.reshape(leaves, near_count, points, points),
        near_offset.transpose(2, 0, 1),
        col_basis.reshape(leaves, rank, points),
        row_basis.reshape(leaves, rank, points),
        up_transfer.reshape(leaves, rank, rank),
        down_transfer.reshape(leaves, rank, rank),
        coupling[0].transpose(1, 2, 0),
        couple_dest,
        couple_target,
    )
    cuts = 2
    part = LS // cuts
    turned = pl.pallas_call(
        turn_out,
        grid=(cuts,),
        out_shape=jax.ShapeDtypeStruct((vecs, leaf_x, LS, rows_y), F32),
        in_specs=[pl.BlockSpec((leaf_y, part * LS, lanes), lambda n: (0, n, 0))],
        out_specs=pl.BlockSpec((vecs, leaf_x, part, rows_y), lambda n: (0, 0, n, 0)),
        name="turn",
    )(summed)
    return turned.reshape(vecs, rows_x, rows_y)


def solution(mesh):
    return jax.shard_map(
        body,
        mesh=mesh,
        in_specs=(
            P(None, "qx", "qy"),
            P("qx", "qy", None, None, None),
            P("qx", "qy", None),
            P("qx", "qy", None, None),
            P("qx", "qy", None, None),
            P("qx", "qy", None, None),
            P("qx", "qy", None, None),
            P(("qx", "qy"), None, None, None),
            P(),
            P(),
        ),
        out_specs=P(None, "qx", "qy"),
        check_vma=False,
    )
```

```python
import jax
import jax.numpy as jnp
from jax import lax
from jax.experimental import pallas as pl
from jax.experimental.pallas import tpu as pltpu
from jax.sharding import PartitionSpec as P

LS = 16
K0 = 6
K1 = 8
KEYS = 32
STEP = 32767.0

ANY = pl.BlockSpec(memory_space=pl.ANY)
VM = pl.BlockSpec(memory_space=pltpu.VMEM)
SM = pl.BlockSpec(memory_space=pltpu.SMEM)
F32 = jnp.float32
BF16 = jnp.bfloat16
I32 = jnp.int32


def halves(value):
    high = value.astype(BF16)
    return high, (value - high.astype(F32)).astype(BF16)


def left_of(value):
    high, low = halves(value)
    return jnp.concatenate([high, low, high], axis=1)


def right_of(value):
    high, low = halves(value)
    return jnp.concatenate([high, high, low], axis=0)


def dot(left, right):
    return jnp.dot(left, right, preferred_element_type=F32)


def swapped(value):
    half = value.shape[-1] // 2
    return jnp.concatenate([value[..., half:], value[..., :half]], axis=-1)


def spread(first, second):
    low = lax.broadcasted_iota(I32, first.shape, 1) < first.shape[1] // 2
    return jnp.concatenate(
        [
            jnp.where(low, first, 0.0),
            jnp.where(low, swapped(first), 0.0),
            jnp.where(low, 0.0, swapped(second)),
            jnp.where(low, 0.0, second),
        ],
        axis=0,
    )


def twice(value):
    low = lax.broadcasted_iota(I32, value.shape, 1) < value.shape[1] // 2
    return jnp.concatenate([jnp.where(low, value, 0.0), jnp.where(low, 0.0, value)], axis=0)


def coded(blocks):
    peak = jnp.max(jnp.abs(blocks), axis=1)
    scale = (jnp.maximum(peak, 1e-30) * 1.004).astype(BF16).astype(F32)
    inverse = STEP / scale
    whole = jnp.round(blocks * inverse[:, None, :]).astype(I32).astype(jnp.int16)
    return whole, scale


def decoded(value):
    return value.astype(I32).astype(F32)


class Plan:
    def __init__(self, width_x, width_y, slots):
        part = max(1, width_y // 2)
        if width_x % part:
            part = 1
        stride = part if width_x % (part * part) == 0 else 1
        self.width_x, self.width_y = width_x, width_y
        self.part, self.stride = part, stride
        self.group = part * width_y
        self.lines = width_x // part
        devices = width_x * width_y
        self.cap = (slots + devices - 1) // devices
        self.total = devices * self.cap
        self.each = self.group * self.cap
        self.scale_rows = -(-(self.lines * self.cap) // 16) * 16
        self.xor_line = self.lines & (self.lines - 1) == 0
        self.xor_group = self.group & (self.group - 1) == 0
        self.order = list(range(self.lines - 1, -1, -1))
        self.hops = sorted({self.hop(t) for t in range(1, self.lines)})

    def hop(self, t):
        return t & -t if self.xor_line else t

    def into(self, t):
        return t - self.hop(t)

    def line(self, z, t):
        return z ^ t if self.xor_line else lax.rem(z + t, self.lines)

    def line_step(self, z, other):
        return other ^ z if self.xor_line else lax.rem(other - z + self.lines, self.lines)

    def peer(self, j, u):
        return j ^ u if self.xor_group else lax.rem(j + u, self.group)

    def place(self, x, y):
        low = lax.rem(x, self.stride)
        rest = lax.div(x, self.stride)
        return lax.div(rest, self.part) * self.stride + low, lax.rem(rest, self.part) * self.width_y + y

    def where(self, z, j):
        high, low = lax.div(z, self.stride), lax.rem(z, self.stride)
        return (high * self.part + lax.div(j, self.width_y)) * self.stride + low, lax.rem(j, self.width_y)

    def index(self, z, j):
        x, y = self.where(z, j)
        return x * self.width_y + y


def tables(plan, clusters, me_z, me_j, dest_ref, target_ref, dests_ref, targets_ref, tab_ref, order_ref):
    slots = dest_ref.shape[1]
    cap, group, lines = plan.cap, plan.group, plan.lines
    own = dest_ref[pl.ds(plan.index(me_z, me_j), 1), :]
    across = jnp.broadcast_to(own.astype(F32), (slots, slots))
    down = across.T
    row = lax.broadcasted_iota(I32, (slots, slots), 0)
    col = lax.broadcasted_iota(I32, (slots, slots), 1)
    order = jnp.sum(jnp.where((across == down) & (col < row), 1.0, 0.0), axis=1, keepdims=True)
    dest = down[:, :1].astype(I32)
    whole = jnp.maximum(dest, 0)
    line, peer = plan.place(lax.div(whole, plan.width_y), lax.rem(whole, plan.width_y))
    step = plan.line_step(me_z, line)
    scale_place = jnp.where(dest >= 0, peer * plan.scale_rows + step * cap + order.astype(I32), -1)
    rows = order_ref.shape[1]
    order_ref[...] = jnp.where(
        scale_place == lax.broadcasted_iota(I32, (slots, rows), 1), 1.0, 0.0
    ).astype(BF16)
    place = (step * group + peer) * cap + order.astype(I32)
    place = jnp.where(dest >= 0, place, -1)
    lane = lax.broadcasted_iota(I32, (slots, plan.total), 1)
    slot = lax.broadcasted_iota(I32, (slots, plan.total), 0).astype(F32)
    slot_of = jnp.sum(jnp.where(place == lane, slot, 0.0), axis=0, keepdims=True)

    for j in range(group):
        at = plan.index(me_z, j)
        dests_ref[j : j + 1, :] = dest_ref[pl.ds(at, 1), :]
        targets_ref[j : j + 1, :] = target_ref[pl.ds(at, 1), :].astype(F32)
    dests, targets = dests_ref[...], targets_ref[...]
    match = jnp.concatenate([dests == plan.index(plan.line(me_z, t), me_j) for t in range(lines)], axis=0)
    target = jnp.concatenate([targets] * lines, axis=0)
    before = jnp.where(row < col, 1.0, 0.0).astype(BF16)
    rank_in = dot(jnp.where(match, 1.0, 0.0).astype(BF16), before)
    rows = lines * group
    step_row = lax.div(lax.broadcasted_iota(I32, (rows, 1), 0), group)
    from_row = lax.rem(lax.broadcasted_iota(I32, (rows, 1), 0), group)
    keys, blocks, scales = [], [], []
    for k in range(cap):
        landing = match & (rank_in == float(k))
        mine = clusters + jnp.sum(jnp.where(landing, target - clusters, 0.0), axis=1, keepdims=True)
        keys.append(mine + (step_row * KEYS).astype(F32))
        blocks.append((from_row * cap + k).astype(F32))
        scales.append((from_row * plan.scale_rows + step_row * cap + k).astype(F32))
    total = plan.total
    key_row = jnp.broadcast_to(jnp.concatenate(keys, axis=0), (total, total))
    key_col = key_row.T
    row = lax.broadcasted_iota(I32, (total, total), 0)
    col = lax.broadcasted_iota(I32, (total, total), 1)
    earlier = (key_row == key_col) & (col < row)
    rank = jnp.sum(jnp.where((key_col < key_row) | earlier, 1.0, 0.0), axis=1, keepdims=True)
    follows = jnp.max(jnp.where(earlier, 1.0, 0.0), axis=1, keepdims=True)
    hit = rank == col.astype(F32)

    def sorted_row(values):
        return jnp.sum(jnp.where(hit, values, 0.0), axis=0, keepdims=True)

    wide = lines * KEYS
    key = jnp.concatenate(keys, axis=0)
    place = lax.broadcasted_iota(I32, (total, wide), 1)
    code = place.astype(F32)
    last = jnp.sum(jnp.where(key <= code, 1.0, 0.0), axis=0, keepdims=True) - 1.0
    last = last - (lax.div(place[:1], KEYS) * plan.each).astype(F32)
    there = jnp.max(jnp.where(key == code, 1.0, 0.0), axis=0, keepdims=True)

    def put(at, values, size):
        tab_ref[at : at + 1, : values.shape[1]] = jnp.clip(values.astype(I32), 0, size - 1)

    put(0, slot_of, slots)
    put(1, sorted_row(jnp.concatenate(blocks, axis=0)), plan.each)
    put(2, sorted_row(jnp.concatenate(scales, axis=0)), group * plan.scale_rows)
    put(3, sorted_row(follows), 2)
    put(4, last, plan.each)
    put(5, there, 2)


def kernel(plan, *refs):
    lines, group, cap = plan.lines, plan.group, plan.cap
    (
        vec_hbm, tiles_hbm, off_ref, col_hbm, row_hbm, up_hbm, down_hbm, coup_hbm, dest_hbm, target_hbm,
        out_hbm,
        vec, tiles, col, row, up, down, coup,
        wide, halo, grid, strips, rim, mats, coef, held, held_scale,
        place_scale, send_scale, got_scale, scale_of, send1,
        dest, target, dests, targets, tab_v, order_of, tab, run, own, send2, send2_scale, near, turned, lifts,
        load_sem, tab_sem, near_send, near_recv, scale_send, scale_recv,
        one_send, one_recv, two_send, two_recv, twos_send, twos_recv, local_sem, out_sem,
        *landing,
    ) = refs
    recv1 = landing[:lines]
    recv2 = landing[lines : 2 * lines - 1]
    recv2_scale = landing[2 * lines - 1 :]

    here_x = lax.axis_index("qx")
    here_y = lax.axis_index("qy")
    me_z, me_j = plan.place(here_x, here_y)
    vecs, rows_x, rows_y = vec.shape
    leaf_x, leaf_y = rows_x // LS, rows_y // LS
    leaves = leaf_x * leaf_y
    uppers = leaf_y // 2
    clusters = leaves + uppers
    rank = coup.shape[0]
    half = rank // 2
    lanes = 2 * vecs
    points = LS * LS
    low = lax.broadcasted_iota(I32, (1, lanes), 1) < vecs
    pieces = send2_scale.shape[1]

    pairs = [
        (vec_hbm, vec),
        (col_hbm, col),
        (up_hbm, up),
        (coup_hbm, coup),
        (row_hbm, row),
        (down_hbm, down),
        (tiles_hbm, tiles),
        (dest_hbm, dest),
        (target_hbm, target),
    ]
    loads = [pltpu.make_async_copy(src, dst, load_sem.at[n]) for n, (src, dst) in enumerate(pairs)]
    for n in (7, 8, 0, 1, 3, 2):
        loads[n].start()

    def at_line(t):
        return plan.where(plan.line(me_z, t), me_j)

    def at_peer(u):
        return plan.where(me_z, plan.peer(me_j, u))

    steps = [(1, 0), (-1, 0), (0, 1), (0, -1), (1, 1), (1, -1), (-1, 1), (-1, -1)]

    def present(dx, dy):
        x = here_x + dx
        y = here_y + dy
        return (x >= 0) & (x < plan.width_x) & (y >= 0) & (y < plan.width_y)

    barrier = pltpu.get_barrier_semaphore()

    def greet(device):
        pl.semaphore_signal(barrier, inc=1, device_id=device, device_id_type=pl.DeviceIdType.MESH)

    for dx, dy in steps:

        @pl.when(present(dx, dy))
        def _():
            greet((here_x + dx, here_y + dy))

    for u in range(1, group):
        greet(at_peer(u))
    for t in plan.hops:
        greet(at_line(t))

    loads[7].wait()
    loads[8].wait()
    tables(plan, clusters, me_z, me_j, dest, target, dests, targets, tab_v, order_of)
    tab_copy = pltpu.make_async_copy(tab_v, tab, tab_sem)
    tab_copy.start()
    loads[0].wait()

    spans = []
    for here, width in ((here_x, plan.width_x), (here_y, plan.width_y)):
        spans.append(1 + (here > 0).astype(I32) + (here < width - 1).astype(I32))
    pl.semaphore_wait(barrier, spans[0] * spans[1] - 1 + group - 1 + len(plan.hops))

    def remote(src, dst, send, recv, device):
        return pltpu.make_async_remote_copy(
            src_ref=src,
            dst_ref=dst,
            send_sem=send,
            recv_sem=recv,
            device_id=device,
            device_id_type=pl.DeviceIdType.MESH,
        )

    def near_copy(n):
        dx, dy = steps[n]
        if dy == 0:
            src = vec.at[:, pl.ds(rows_x - LS if dx > 0 else 0, LS), :]
            dst = halo.at[0 if dx > 0 else 1]
        else:
            side = 1 if dy > 0 else 0
            if dx == 0:
                src = strips.at[side]
                dst = rim.at[1 - side, pl.ds(1, leaf_x)]
            else:
                src = strips.at[side, leaf_x - 1 if dx > 0 else 0]
                dst = rim.at[1 - side, 0 if dx > 0 else leaf_x + 1]
        return remote(src, dst, near_send.at[n], near_recv.at[n], (here_x + dx, here_y + dy))

    def near_start(first, end):
        for n in range(first, end):

            @pl.when(present(*steps[n]))
            def _():
                near_copy(n).start()

    near_start(0, 2)

    wide[...] = vec[...].astype(F32)

    def to_grid(x, carry):
        plane = wide[:, x, :]
        lines_of = jnp.concatenate([plane, plane], axis=0).T.astype(BF16).reshape(leaf_y, LS, lanes)
        at = pl.multiple_of(lax.rem(x, LS) * LS, LS)
        grid[1 + lax.div(x, LS), 1 : 1 + leaf_y, pl.ds(at, LS), :] = lines_of
        return carry

    lax.fori_loop(0, rows_x, to_grid, 0, unroll=4)
    for side in range(2):
        for i in range(leaf_x):
            block = grid[1 + i, leaf_y if side else 1].reshape(2, LS // 2, LS, lanes)
            strips[side, i] = jnp.where(low, block[0], block[1])
    near_start(2, 8)

    loads[1].wait()

    def leaf_coef(m, carry):
        i = lax.div(m, leaf_y)
        j = lax.rem(m, leaf_y)
        coef[m] = dot(col[m], grid[1 + i, 1 + j])
        return carry

    lax.fori_loop(0, leaves, leaf_coef, 0, unroll=4)
    loads[2].wait()

    def upper_coef(p, carry):
        children = [i * leaf_y + 2 * p + q for i in range(leaf_x) for q in range(2)]
        left = jnp.concatenate([up[m] for m in children], axis=1)
        right = jnp.concatenate([coef[m] for m in children], axis=0)
        coef[leaves + p] = dot(left_of(left), right_of(right))
        return carry

    lax.fori_loop(0, uppers, upper_coef, 0, unroll=4)

    loads[3].wait()
    for n in (4, 5, 6):
        loads[n].start()

    def turn(r, carry):
        mats[:, r, :] = jnp.concatenate([coup[r], coup[r + half]], axis=0).T
        return carry

    lax.fori_loop(0, half, turn, 0, unroll=8)

    def contribute(first, count, m):
        left = left_of(mats[pl.ds(first, count)].reshape(count * half, lanes))
        blocks = dot(left, right_of(twice(coef[m]))).reshape(count, half, lanes)
        whole, scale = coded(blocks)
        held[pl.ds(first, count)] = whole
        for q in range(count):
            held_scale[pl.ds(first + q, 1), :] = scale[q : q + 1]

    def leaf_slots(m, carry):
        contribute(m * K0, K0, m)
        return carry

    def upper_slots(p, carry):
        contribute(leaves * K0 + p * K1, K1, leaves + p)
        return carry

    lax.fori_loop(0, leaves, leaf_slots, 0, unroll=4)
    lax.fori_loop(0, uppers, upper_slots, 0, unroll=4)

    tab_copy.wait()
    ordered = lax.dot_general(
        order_of[...], held_scale[...].astype(BF16), (((0,), (0,)), ((), ())), preferred_element_type=F32
    )
    send_scale[...] = ordered.astype(BF16).reshape(send_scale.shape)

    def scale_copy(u):
        return remote(
            send_scale.at[plan.peer(me_j, u)], got_scale.at[me_j], scale_send.at[u], scale_recv.at[u], at_peer(u)
        )

    def one_copy(t, u):
        return remote(
            send1.at[pl.ds((t * group + plan.peer(me_j, u)) * cap, cap)],
            recv1[t].at[pl.ds(me_j * cap, cap)],
            one_send.at[t, u],
            one_recv.at[t, u],
            at_peer(u),
        )

    def one_local(t):
        return pltpu.make_async_copy(
            send1.at[pl.ds((t * group + me_j) * cap, cap)], recv1[t].at[pl.ds(me_j * cap, cap)], local_sem.at[t]
        )

    scale_local = pltpu.make_async_copy(send_scale.at[me_j], got_scale.at[me_j], local_sem.at[lines])
    scale_local.start()
    for u in range(1, group):
        scale_copy(u).start()

    for t in plan.order:

        def put(p, carry, t=t):
            send1[t * plan.each + p] = held[tab[0, t * plan.each + p]]
            return carry

        lax.fori_loop(0, plan.each, put, 0, unroll=16)
        for u in range(1, group):
            one_copy(t, u).start()
        one_local(t).start()

    loads[4].wait()
    loads[5].wait()

    def turn_row(j, carry):
        pair = jnp.concatenate([row[j], row[leaf_y + j]], axis=0)
        basis = pair.astype(F32).T.astype(BF16)
        turned[j] = jnp.concatenate([basis, basis], axis=1)
        return carry

    lax.fori_loop(0, leaf_y, turn_row, 0, unroll=2)

    def lift(p, carry):
        parts = []
        for i in range(leaf_x):
            for q in range(2):
                mat = down[i * leaf_y + 2 * p + q]
                parts.append(jnp.concatenate([mat[:half], mat[half:]], axis=1))
        lifts[p] = left_of(jnp.concatenate(parts, axis=0))
        return carry

    lax.fori_loop(0, uppers, lift, 0, unroll=2)

    def near_field(first, count):
        def pair(j, carry):
            sums = []
            for i in range(leaf_x):
                m = i * leaf_y + j
                total = None
                for k in range(tiles.shape[1]):
                    o = off_ref[k, i, j]
                    term = dot(tiles[m, k], grid[i + lax.div(o, 3), j + lax.rem(o, 3)])
                    total = term if total is None else total + term
                sums.append(total)
            near[j] = jnp.where(low, sums[0], sums[1])
            return carry

        lax.fori_loop(first, first + count, pair, 0)

    def near_rows():
        for side in range(2):
            keep = present(2 * side - 1, 0)
            wide[:, side * LS : (side + 1) * LS, :] = jnp.where(keep, halo[side].astype(F32), 0.0)

        def to_rows(x, carry):
            plane = wide[:, x, :]
            lines_of = jnp.concatenate([plane, plane], axis=0).T.astype(BF16).reshape(leaf_y, LS, lanes)
            at = pl.multiple_of(lax.rem(x, LS) * LS, LS)
            grid[lax.div(x, LS) * (leaf_x + 1), 1 : 1 + leaf_y, pl.ds(at, LS), :] = lines_of
            return carry

        lax.fori_loop(0, 2 * LS, to_rows, 0, unroll=4)

    def near_edges():
        loads[6].wait()
        near_edges_of()
        near_rows()

    def near_edges_of():
        for n, (dx, dy) in enumerate(steps):

            @pl.when(present(-dx, -dy))
            def _():
                near_copy(n).wait_recv()

        for side in range(2):
            dy = 1 if side else -1
            for i in range(leaf_x + 2):
                dx = -1 if i == 0 else (1 if i == leaf_x + 1 else 0)
                keep = present(dx, dy)
                value = jnp.where(keep, rim[side, i].astype(F32), 0.0).reshape(points // 2, lanes)
                other = swapped(value)
                y = leaf_y + 1 if side else 0
                grid[i, y, : points // 2, :] = jnp.where(low, value, other).astype(BF16)
                grid[i, y, points // 2 :, :] = jnp.where(low, other, value).astype(BF16)

    scale_local.wait()
    for u in range(1, group):
        scale_copy(u).wait_recv()
    scale_of[...] = got_scale[...].astype(F32).reshape(scale_of.shape) * (1.0 / STEP)

    some = clusters // pieces

    def two_copy(t, h):
        return remote(
            send2.at[t - 1, pl.ds(h * some, some)],
            recv2[t - 1].at[pl.ds(h * some, some)],
            two_send.at[t, h],
            two_recv.at[t, h],
            at_line(plan.hop(t)),
        )

    def twos_copy(t, h):
        return remote(
            send2_scale.at[t - 1, h], recv2_scale[t - 1].at[h], twos_send.at[t, h], twos_recv.at[t, h], at_line(plan.hop(t))
        )

    def collect_all(t):
        one_local(t).wait()
        for u in range(1, group):
            one_copy(t, u).wait_recv()

        def collect(i, total):
            at = t * plan.each + i
            block = decoded(recv1[t][tab[1, at]]) * scale_of[tab[2, at]]
            total = total * tab[3, at].astype(F32) + block
            run[i] = total
            return total

        lax.fori_loop(0, plan.each, collect, jnp.zeros((half, lanes), F32), unroll=8)

        def pick(n, carry):
            own[n] = run[tab[4, t * KEYS + n]] * tab[5, t * KEYS + n].astype(F32)
            return carry

        lax.fori_loop(0, clusters, pick, 0, unroll=10)

    def merge(t, h):
        two_copy(t, h).wait_recv()
        twos_copy(t, h).wait_recv()
        place_scale[...] = recv2_scale[t - 1][h].astype(F32) * (1.0 / STEP)

        def gather(n, carry):
            own[h * some + n] = own[h * some + n] + decoded(recv2[t - 1][h * some + n]) * place_scale[pl.ds(n, 1), :]
            return carry

        lax.fori_loop(0, some, gather, 0, unroll=5)

    def pass_on(t, h):
        group_of = 5 if some % 5 == 0 else 1

        def pack(g, carry):
            first = h * some + g * group_of
            whole, scale = coded(own[pl.ds(first, group_of)])
            send2[t - 1, pl.ds(first, group_of)] = whole
            for q in range(group_of):
                place_scale[pl.ds(g * group_of + q, 1), :] = scale[q : q + 1]
            return carry

        lax.fori_loop(0, some // group_of, pack, 0, unroll=2)
        send2_scale[t - 1, h] = place_scale[...].astype(BF16)
        twos_copy(t, h).start()
        two_copy(t, h).start()

    place_scale[...] = jnp.zeros_like(place_scale)
    edges_at = min(1, lines - 1)
    done = 0
    for step, t in enumerate(plan.order):
        collect_all(t)
        if step == edges_at and t == 0:
            near_edges()
        if t == 0:
            near_field(done, leaf_y - done)
        incoming = [other for other in plan.order if other and plan.into(other) == t]
        for h in range(pieces):
            for other in sorted(incoming):
                merge(other, h)
            if t:
                pass_on(t, h)
        if step == edges_at and t:
            near_edges()
        elif step > edges_at and t:
            count = min(-(-leaf_y // max(lines - 2, 1)), leaf_y - done)
            near_field(done, count)
            done += count

    def descend(p, carry):
        top = own[leaves + p]
        extra = dot(lifts[p], right_of(spread(top, top))).reshape(2 * leaf_x, half, lanes)
        for i in range(leaf_x):
            for q in range(2):
                m = i * leaf_y + 2 * p + q
                own[m] = own[m] + extra[2 * i + q]
        return carry

    lax.fori_loop(0, uppers, descend, 0, unroll=4)

    def out_copy(j):
        return pltpu.make_async_copy(near.at[j], out_hbm.at[j], out_sem.at[j])

    for j in range(leaf_y):
        high, rest = halves(spread(own[j], own[leaf_y + j]))
        near[j] = near[j] + dot(turned[j], jnp.concatenate([high, rest], axis=0))
        out_copy(j).start()

    for j in range(leaf_y):
        out_copy(j).wait()

    for n in range(8):

        @pl.when(present(*steps[n]))
        def _():
            near_copy(n).wait_send()

    for u in range(1, group):
        scale_copy(u).wait_send()
        for t in range(lines):
            one_copy(t, u).wait_send()
    for t in range(1, lines):
        for h in range(pieces):
            two_copy(t, h).wait_send()
            twos_copy(t, h).wait_send()


def turn_out(sum_ref, out_ref):
    vecs = out_ref.shape[0]
    for x in range(out_ref.shape[2]):
        line = sum_ref[:, x * LS : (x + 1) * LS, :].reshape(out_ref.shape[3], 2 * vecs).T
        out_ref[:, 0, x, :] = line[:vecs]
        out_ref[:, 1, x, :] = line[vecs:]


def body(
    vectors,
    near_tiles,
    near_offset,
    col_basis,
    row_basis,
    up_transfer,
    down_transfer,
    coupling,
    couple_dest,
    couple_target,
):
    vecs, rows_x, rows_y = vectors.shape
    leaf_x, leaf_y = rows_x // LS, rows_y // LS
    leaves = leaf_x * leaf_y
    uppers = leaf_y // 2
    clusters = leaves + uppers
    rank = coupling.shape[2]
    half = rank // 2
    slots = coupling.shape[1]
    near_count = near_tiles.shape[2]
    points = LS * LS
    lanes = 2 * vecs
    plan = Plan(lax.axis_size("qx"), lax.axis_size("qy"), slots)
    lines, group, cap = plan.lines, plan.group, plan.cap
    pieces = 2 if clusters % 2 == 0 else 1
    scale2 = -(-(clusters // pieces) // 16) * 16
    devices = couple_dest.shape[0]
    width = max(plan.total, lines * KEYS)
    vmem, dma = pltpu.VMEM, pltpu.SemaphoreType.DMA
    int16 = jnp.int16
    scratch = [
        vmem((vecs, rows_x, rows_y), BF16),
        vmem((leaves, near_count, points, points), BF16),
        vmem((leaves, rank, points), BF16),
        vmem((leaves, rank, points), BF16),
        vmem((leaves, rank, rank), F32),
        vmem((leaves, rank, rank), F32),
        vmem((rank, rank, slots), F32),
        vmem((vecs, rows_x, rows_y), F32),
        vmem((2, vecs, LS, rows_y), BF16),
        vmem((leaf_x + 2, leaf_y + 2, points, lanes), BF16),
        vmem((2, leaf_x, LS // 2, LS, lanes), BF16),
        vmem((2, leaf_x + 2, LS // 2, LS, lanes), BF16),
        vmem((slots, half, lanes), F32),
        vmem((clusters, rank, lanes), F32),
        vmem((slots, half, lanes), int16),
        vmem((slots, lanes), F32),
        vmem((scale2, lanes), F32),
        vmem((group, plan.scale_rows, lanes), BF16),
        vmem((group, plan.scale_rows, lanes), BF16),
        vmem((group * plan.scale_rows, 1, lanes), F32),
        vmem((plan.total, half, lanes), int16),
        vmem((devices, slots), I32),
        vmem((devices, slots), I32),
        vmem((group, slots), I32),
        vmem((group, slots), F32),
        vmem((8, width), I32),
        vmem((slots, group * plan.scale_rows), BF16),
        pltpu.SMEM((8, width), I32),
        vmem((plan.each, half, lanes), F32),
        vmem((clusters, half, lanes), F32),
        vmem((max(lines - 1, 1), clusters, half, lanes), int16),
        vmem((max(lines - 1, 1), pieces, scale2, lanes), BF16),
        vmem((leaf_y, points, lanes), F32),
        vmem((leaf_y, points, 4 * rank), BF16),
        vmem((uppers, 2 * leaf_x * half, 6 * rank), BF16),
        dma((9,)),
        dma(()),
        dma((8,)),
        dma((8,)),
        dma((group,)),
        dma((group,)),
        dma((lines, group)),
        dma((lines, group)),
        dma((lines, pieces)),
        dma((lines, pieces)),
        dma((lines, pieces)),
        dma((lines, pieces)),
        dma((lines + 1,)),
        dma((leaf_y,)),
    ]
    scratch += [vmem((plan.each, half, lanes), int16)] * lines
    scratch += [vmem((clusters, half, lanes), int16)] * (lines - 1)
    scratch += [vmem((pieces, scale2, lanes), BF16)] * (lines - 1)
    summed = pl.pallas_call(
        lambda *refs: kernel(plan, *refs),
        out_shape=jax.ShapeDtypeStruct((leaf_y, points, lanes), F32),
        in_specs=[ANY, ANY, SM, ANY, ANY, ANY, ANY, ANY, ANY, ANY],
        out_specs=ANY,
        scratch_shapes=scratch,
        compiler_params=pltpu.CompilerParams(collective_id=0, has_side_effects=True, vmem_limit_bytes=60 << 20),
        name="product",
    )(
        vectors,
        near_tiles.reshape(leaves, near_count, points, points),
        near_offset.transpose(2, 0, 1),
        col_basis.reshape(leaves, rank, points),
        row_basis.reshape(leaves, rank, points),
        up_transfer.reshape(leaves, rank, rank),
        down_transfer.reshape(leaves, rank, rank),
        coupling[0].transpose(1, 2, 0),
        couple_dest,
        couple_target,
    )
    cuts = 2
    part = LS // cuts
    turned = pl.pallas_call(
        turn_out,
        grid=(cuts,),
        out_shape=jax.ShapeDtypeStruct((vecs, leaf_x, LS, rows_y), F32),
        in_specs=[pl.BlockSpec((leaf_y, part * LS, lanes), lambda n: (0, n, 0))],
        out_specs=pl.BlockSpec((vecs, leaf_x, part, rows_y), lambda n: (0, 0, n, 0)),
        name="turn",
    )(summed)
    return turned.reshape(vecs, rows_x, rows_y)


def solution(mesh):
    return jax.shard_map(
        body,
        mesh=mesh,
        in_specs=(
            P(None, "qx", "qy"),
            P("qx", "qy", None, None, None),
            P("qx", "qy", None),
            P("qx", "qy", None, None),
            P("qx", "qy", None, None),
            P("qx", "qy", None, None),
            P("qx", "qy", None, None),
            P(("qx", "qy"), None, None, None),
            P(),
            P(),
        ),
        out_specs=P(None, "qx", "qy"),
        check_vma=False,
    )
```

```python
import jax
import jax.numpy as jnp
from jax import lax
from jax.experimental import pallas as pl
from jax.experimental.pallas import tpu as pltpu
from jax.sharding import PartitionSpec as P

LS = 16
K0 = 6
K1 = 8
KEYS = 32
STEP = 32767.0

ANY = pl.BlockSpec(memory_space=pl.ANY)
VM = pl.BlockSpec(memory_space=pltpu.VMEM)
SM = pl.BlockSpec(memory_space=pltpu.SMEM)
F32 = jnp.float32
BF16 = jnp.bfloat16
I32 = jnp.int32


def halves(value):
    high = value.astype(BF16)
    return high, (value - high.astype(F32)).astype(BF16)


def left_of(value):
    high, low = halves(value)
    return jnp.concatenate([high, low, high], axis=1)


def right_of(value):
    high, low = halves(value)
    return jnp.concatenate([high, high, low], axis=0)


def dot(left, right):
    return jnp.dot(left, right, preferred_element_type=F32)


def swapped(value):
    half = value.shape[-1] // 2
    return jnp.concatenate([value[..., half:], value[..., :half]], axis=-1)


def spread(first, second):
    low = lax.broadcasted_iota(I32, first.shape, 1) < first.shape[1] // 2
    return jnp.concatenate(
        [
            jnp.where(low, first, 0.0),
            jnp.where(low, swapped(first), 0.0),
            jnp.where(low, 0.0, swapped(second)),
            jnp.where(low, 0.0, second),
        ],
        axis=0,
    )


def twice(value):
    low = lax.broadcasted_iota(I32, value.shape, 1) < value.shape[1] // 2
    return jnp.concatenate([jnp.where(low, value, 0.0), jnp.where(low, 0.0, value)], axis=0)


def coded(blocks):
    peak = jnp.max(jnp.abs(blocks), axis=1)
    scale = (jnp.maximum(peak, 1e-30) * 1.004).astype(BF16).astype(F32)
    inverse = STEP / scale
    whole = jnp.round(blocks * inverse[:, None, :]).astype(I32).astype(jnp.int16)
    return whole, scale


def decoded(value):
    return value.astype(I32).astype(F32)


class Plan:
    def __init__(self, width_x, width_y, slots):
        part = max(1, width_y // 2)
        if width_x % part:
            part = 1
        stride = part if width_x % (part * part) == 0 else 1
        self.width_x, self.width_y = width_x, width_y
        self.part, self.stride = part, stride
        self.group = part * width_y
        self.lines = width_x // part
        devices = width_x * width_y
        self.cap = (slots + devices - 1) // devices
        self.total = devices * self.cap
        self.each = self.group * self.cap
        self.scale_rows = -(-(self.lines * self.cap) // 16) * 16
        self.xor_line = self.lines & (self.lines - 1) == 0
        self.xor_group = self.group & (self.group - 1) == 0
        self.order = list(range(self.lines - 1, -1, -1))
        self.hops = sorted({self.hop(t) for t in range(1, self.lines)})

    def hop(self, t):
        return t & -t if self.xor_line else t

    def into(self, t):
        return t - self.hop(t)

    def line(self, z, t):
        return z ^ t if self.xor_line else lax.rem(z + t, self.lines)

    def line_step(self, z, other):
        return other ^ z if self.xor_line else lax.rem(other - z + self.lines, self.lines)

    def peer(self, j, u):
        return j ^ u if self.xor_group else lax.rem(j + u, self.group)

    def place(self, x, y):
        low = lax.rem(x, self.stride)
        rest = lax.div(x, self.stride)
        return lax.div(rest, self.part) * self.stride + low, lax.rem(rest, self.part) * self.width_y + y

    def where(self, z, j):
        high, low = lax.div(z, self.stride), lax.rem(z, self.stride)
        return (high * self.part + lax.div(j, self.width_y)) * self.stride + low, lax.rem(j, self.width_y)

    def index(self, z, j):
        x, y = self.where(z, j)
        return x * self.width_y + y


def tables(plan, clusters, me_z, me_j, dest_ref, target_ref, dests_ref, targets_ref, tab_ref, order_ref):
    slots = dest_ref.shape[1]
    cap, group, lines = plan.cap, plan.group, plan.lines
    own = dest_ref[pl.ds(plan.index(me_z, me_j), 1), :]
    across = jnp.broadcast_to(own.astype(F32), (slots, slots))
    down = across.T
    row = lax.broadcasted_iota(I32, (slots, slots), 0)
    col = lax.broadcasted_iota(I32, (slots, slots), 1)
    order = jnp.sum(jnp.where((across == down) & (col < row), 1.0, 0.0), axis=1, keepdims=True)
    dest = down[:, :1].astype(I32)
    whole = jnp.maximum(dest, 0)
    line, peer = plan.place(lax.div(whole, plan.width_y), lax.rem(whole, plan.width_y))
    step = plan.line_step(me_z, line)
    scale_place = jnp.where(dest >= 0, peer * plan.scale_rows + step * cap + order.astype(I32), -1)
    rows = order_ref.shape[1]
    order_ref[...] = jnp.where(
        scale_place == lax.broadcasted_iota(I32, (slots, rows), 1), 1.0, 0.0
    ).astype(BF16)
    place = (step * group + peer) * cap + order.astype(I32)
    place = jnp.where(dest >= 0, place, -1)
    lane = lax.broadcasted_iota(I32, (slots, plan.total), 1)
    slot = lax.broadcasted_iota(I32, (slots, plan.total), 0).astype(F32)
    slot_of = jnp.sum(jnp.where(place == lane, slot, 0.0), axis=0, keepdims=True)

    for j in range(group):
        at = plan.index(me_z, j)
        dests_ref[j : j + 1, :] = dest_ref[pl.ds(at, 1), :]
        targets_ref[j : j + 1, :] = target_ref[pl.ds(at, 1), :].astype(F32)
    dests, targets = dests_ref[...], targets_ref[...]
    match = jnp.concatenate([dests == plan.index(plan.line(me_z, t), me_j) for t in range(lines)], axis=0)
    target = jnp.concatenate([targets] * lines, axis=0)
    before = jnp.where(row < col, 1.0, 0.0).astype(BF16)
    rank_in = dot(jnp.where(match, 1.0, 0.0).astype(BF16), before)
    rows = lines * group
    step_row = lax.div(lax.broadcasted_iota(I32, (rows, 1), 0), group)
    from_row = lax.rem(lax.broadcasted_iota(I32, (rows, 1), 0), group)
    keys, blocks, scales = [], [], []
    for k in range(cap):
        landing = match & (rank_in == float(k))
        mine = clusters + jnp.sum(jnp.where(landing, target - clusters, 0.0), axis=1, keepdims=True)
        keys.append(mine + (step_row * KEYS).astype(F32))
        blocks.append((from_row * cap + k).astype(F32))
        scales.append((from_row * plan.scale_rows + step_row * cap + k).astype(F32))
    total = plan.total
    key_row = jnp.broadcast_to(jnp.concatenate(keys, axis=0), (total, total))
    key_col = key_row.T
    row = lax.broadcasted_iota(I32, (total, total), 0)
    col = lax.broadcasted_iota(I32, (total, total), 1)
    earlier = (key_row == key_col) & (col < row)
    rank = jnp.sum(jnp.where((key_col < key_row) | earlier, 1.0, 0.0), axis=1, keepdims=True)
    follows = jnp.max(jnp.where(earlier, 1.0, 0.0), axis=1, keepdims=True)
    hit = rank == col.astype(F32)

    def sorted_row(values):
        return jnp.sum(jnp.where(hit, values, 0.0), axis=0, keepdims=True)

    wide = lines * KEYS
    key = jnp.concatenate(keys, axis=0)
    place = lax.broadcasted_iota(I32, (total, wide), 1)
    code = place.astype(F32)
    last = jnp.sum(jnp.where(key <= code, 1.0, 0.0), axis=0, keepdims=True) - 1.0
    last = last - (lax.div(place[:1], KEYS) * plan.each).astype(F32)
    there = jnp.max(jnp.where(key == code, 1.0, 0.0), axis=0, keepdims=True)

    def put(at, values, size):
        tab_ref[at : at + 1, : values.shape[1]] = jnp.clip(values.astype(I32), 0, size - 1)

    put(0, slot_of, slots)
    put(1, sorted_row(jnp.concatenate(blocks, axis=0)), plan.each)
    put(2, sorted_row(jnp.concatenate(scales, axis=0)), group * plan.scale_rows)
    put(3, sorted_row(follows), 2)
    put(4, last, plan.each)
    put(5, there, 2)


def kernel(plan, *refs):
    lines, group, cap = plan.lines, plan.group, plan.cap
    (
        vec_hbm, tiles_hbm, off_ref, col_hbm, row_hbm, up_hbm, down_hbm, coup_hbm, dest_hbm, target_hbm,
        out_hbm,
        vec, tiles, col, row, up, down, coup,
        wide, halo, grid, strips, corners, rim, mats, coef, held, held_scale,
        place_scale, send_scale, got_scale, scale_of, send1,
        dest, target, dests, targets, tab_v, order_of, tab, run, own, send2, send2_scale, near, turned, lifts,
        load_sem, tab_sem, near_send, near_recv, scale_send, scale_recv,
        one_send, one_recv, two_send, two_recv, twos_send, twos_recv, local_sem, out_sem,
        *landing,
    ) = refs
    recv1 = landing[:lines]
    recv2 = landing[lines : 2 * lines - 1]
    recv2_scale = landing[2 * lines - 1 :]

    here_x = lax.axis_index("qx")
    here_y = lax.axis_index("qy")
    me_z, me_j = plan.place(here_x, here_y)
    vecs, rows_x, rows_y = vec.shape
    leaf_x, leaf_y = rows_x // LS, rows_y // LS
    leaves = leaf_x * leaf_y
    uppers = leaf_y // 2
    clusters = leaves + uppers
    rank = coup.shape[0]
    half = rank // 2
    lanes = 2 * vecs
    points = LS * LS
    low = lax.broadcasted_iota(I32, (1, lanes), 1) < vecs
    pieces = send2_scale.shape[1]

    pairs = [
        (vec_hbm, vec),
        (col_hbm, col),
        (up_hbm, up),
        (coup_hbm, coup),
        (row_hbm, row),
        (down_hbm, down),
        (tiles_hbm, tiles),
        (dest_hbm, dest),
        (target_hbm, target),
    ]
    loads = [pltpu.make_async_copy(src, dst, load_sem.at[n]) for n, (src, dst) in enumerate(pairs)]
    for n in (7, 8, 0, 1, 3, 2):
        loads[n].start()

    def at_line(t):
        return plan.where(plan.line(me_z, t), me_j)

    def at_peer(u):
        return plan.where(me_z, plan.peer(me_j, u))

    steps = [(1, 0), (-1, 0), (0, 1), (0, -1), (0, 1), (0, -1), (0, 1), (0, -1)]

    def present(dx, dy):
        x = here_x + dx
        y = here_y + dy
        return (x >= 0) & (x < plan.width_x) & (y >= 0) & (y < plan.width_y)

    barrier = pltpu.get_barrier_semaphore()

    def greet(device):
        pl.semaphore_signal(barrier, inc=1, device_id=device, device_id_type=pl.DeviceIdType.MESH)

    for dx, dy in steps[:4]:

        @pl.when(present(dx, dy))
        def _():
            greet((here_x + dx, here_y + dy))

    for u in range(1, group):
        greet(at_peer(u))
    for t in plan.hops:
        greet(at_line(t))

    loads[7].wait()
    loads[8].wait()
    tables(plan, clusters, me_z, me_j, dest, target, dests, targets, tab_v, order_of)
    tab_copy = pltpu.make_async_copy(tab_v, tab, tab_sem)
    tab_copy.start()
    loads[0].wait()

    spans = []
    for here, width in ((here_x, plan.width_x), (here_y, plan.width_y)):
        spans.append((here > 0).astype(I32) + (here < width - 1).astype(I32))
    pl.semaphore_wait(barrier, spans[0] + spans[1] + group - 1 + len(plan.hops))

    def remote(src, dst, send, recv, device):
        return pltpu.make_async_remote_copy(
            src_ref=src,
            dst_ref=dst,
            send_sem=send,
            recv_sem=recv,
            device_id=device,
            device_id_type=pl.DeviceIdType.MESH,
        )

    def near_copy(n):
        dx, dy = steps[n]
        if dy == 0:
            src = vec.at[:, pl.ds(rows_x - LS if dx > 0 else 0, LS), :]
            dst = halo.at[0 if dx > 0 else 1]
        else:
            side = 1 if dy > 0 else 0
            if n < 4:
                src = strips.at[side]
                dst = rim.at[1 - side, pl.ds(1, leaf_x)]
            else:
                end = (n - 4) // 2
                src = corners.at[end, side]
                dst = rim.at[1 - side, end * (leaf_x + 1)]
        return remote(src, dst, near_send.at[n], near_recv.at[n], (here_x + dx, here_y + dy))

    def near_start(first, end):
        for n in range(first, end):

            @pl.when(present(*steps[n]))
            def _():
                near_copy(n).start()

    near_start(0, 2)

    wide[...] = vec[...].astype(F32)

    def to_grid(x, carry):
        plane = wide[:, x, :]
        lines_of = jnp.concatenate([plane, plane], axis=0).T.astype(BF16).reshape(leaf_y, LS, lanes)
        at = pl.multiple_of(lax.rem(x, LS) * LS, LS)
        grid[1 + lax.div(x, LS), 1 : 1 + leaf_y, pl.ds(at, LS), :] = lines_of
        return carry

    lax.fori_loop(0, rows_x, to_grid, 0, unroll=8)
    for side in range(2):
        for i in range(leaf_x):
            block = grid[1 + i, leaf_y if side else 1].reshape(2, LS // 2, LS, lanes)
            strips[side, i] = jnp.where(low, block[0], block[1])
    near_start(2, 4)

    loads[1].wait()

    def leaf_coef(m, carry):
        i = lax.div(m, leaf_y)
        j = lax.rem(m, leaf_y)
        coef[m] = dot(col[m], grid[1 + i, 1 + j])
        return carry

    lax.fori_loop(0, leaves, leaf_coef, 0, unroll=8)
    loads[2].wait()

    def upper_coef(p, carry):
        children = [i * leaf_y + 2 * p + q for i in range(leaf_x) for q in range(2)]
        left = jnp.concatenate([up[m] for m in children], axis=1)
        right = jnp.concatenate([coef[m] for m in children], axis=0)
        coef[leaves + p] = dot(left_of(left), right_of(right))
        return carry

    lax.fori_loop(0, uppers, upper_coef, 0, unroll=4)

    loads[3].wait()
    for n in (4, 5, 6):
        loads[n].start()

    def turn(r, carry):
        mats[:, r, :] = jnp.concatenate([coup[r], coup[r + half]], axis=0).T
        return carry

    lax.fori_loop(0, half, turn, 0, unroll=8)

    def contribute(first, count, m):
        left = left_of(mats[pl.ds(first, count)].reshape(count * half, lanes))
        blocks = dot(left, right_of(twice(coef[m]))).reshape(count, half, lanes)
        whole, scale = coded(blocks)
        held[pl.ds(first, count)] = whole
        for q in range(count):
            held_scale[pl.ds(first + q, 1), :] = scale[q : q + 1]

    def leaf_slots(m, carry):
        contribute(m * K0, K0, m)
        return carry

    def upper_slots(p, carry):
        contribute(leaves * K0 + p * K1, K1, leaves + p)
        return carry

    lax.fori_loop(0, leaves, leaf_slots, 0, unroll=8)
    lax.fori_loop(0, uppers, upper_slots, 0, unroll=4)

    tab_copy.wait()
    ordered = lax.dot_general(
        order_of[...], held_scale[...].astype(BF16), (((0,), (0,)), ((), ())), preferred_element_type=F32
    )
    send_scale[...] = ordered.astype(BF16).reshape(send_scale.shape)

    def scale_copy(u):
        return remote(
            send_scale.at[plan.peer(me_j, u)], got_scale.at[me_j], scale_send.at[u], scale_recv.at[u], at_peer(u)
        )

    def one_copy(t, u):
        return remote(
            send1.at[pl.ds((t * group + plan.peer(me_j, u)) * cap, cap)],
            recv1[t].at[pl.ds(me_j * cap, cap)],
            one_send.at[t, u],
            one_recv.at[t, u],
            at_peer(u),
        )

    def one_local(t):
        return pltpu.make_async_copy(
            send1.at[pl.ds((t * group + me_j) * cap, cap)], recv1[t].at[pl.ds(me_j * cap, cap)], local_sem.at[t]
        )

    scale_local = pltpu.make_async_copy(send_scale.at[me_j], got_scale.at[me_j], local_sem.at[lines])
    scale_local.start()
    for u in range(1, group):
        scale_copy(u).start()

    for t in plan.order:

        def put(p, carry, t=t):
            send1[t * plan.each + p] = held[tab[0, t * plan.each + p]]
            return carry

        lax.fori_loop(0, plan.each, put, 0, unroll=16)
        for u in range(1, group):
            one_copy(t, u).start()
        one_local(t).start()

    loads[4].wait()
    loads[5].wait()

    def turn_row(j, carry):
        pair = jnp.concatenate([row[j], row[leaf_y + j]], axis=0)
        basis = pair.astype(F32).T.astype(BF16)
        turned[j] = jnp.concatenate([basis, basis], axis=1)
        return carry

    lax.fori_loop(0, leaf_y, turn_row, 0, unroll=2)

    def lift(p, carry):
        parts = []
        for i in range(leaf_x):
            for q in range(2):
                mat = down[i * leaf_y + 2 * p + q]
                parts.append(jnp.concatenate([mat[:half], mat[half:]], axis=1))
        lifts[p] = left_of(jnp.concatenate(parts, axis=0))
        return carry

    lax.fori_loop(0, uppers, lift, 0, unroll=2)

    def near_field(first, count):
        def pair(j, carry):
            sums = []
            for i in range(leaf_x):
                m = i * leaf_y + j
                total = None
                for k in range(tiles.shape[1]):
                    o = off_ref[k, i, j]
                    term = dot(tiles[m, k], grid[i + lax.div(o, 3), j + lax.rem(o, 3)])
                    total = term if total is None else total + term
                sums.append(total)
            near[j] = jnp.where(low, sums[0], sums[1])
            return carry

        lax.fori_loop(first, first + count, pair, 0)

    def near_rows():
        for side in range(2):
            keep = present(2 * side - 1, 0)
            wide[:, side * LS : (side + 1) * LS, :] = jnp.where(keep, halo[side].astype(F32), 0.0)

        def to_rows(x, carry):
            plane = wide[:, x, :]
            lines_of = jnp.concatenate([plane, plane], axis=0).T.astype(BF16).reshape(leaf_y, LS, lanes)
            at = pl.multiple_of(lax.rem(x, LS) * LS, LS)
            grid[lax.div(x, LS) * (leaf_x + 1), 1 : 1 + leaf_y, pl.ds(at, LS), :] = lines_of
            return carry

        lax.fori_loop(0, 2 * LS, to_rows, 0, unroll=4)

    def near_wait(first, end):
        for n in range(first, end):

            @pl.when(present(-steps[n][0], -steps[n][1]))
            def _():
                near_copy(n).wait_recv()

    def near_corners():
        near_wait(0, 2)
        near_rows()
        for end in range(2):
            for side in range(2):
                block = grid[end * (leaf_x + 1), leaf_y if side else 1].reshape(2, LS // 2, LS, lanes)
                corners[end, side] = jnp.where(low, block[0], block[1])
        near_start(4, 8)

    def near_edges():
        near_wait(2, 8)
        loads[6].wait()
        for side in range(2):
            dy = 1 if side else -1
            for i in range(leaf_x + 2):
                dx = -1 if i == 0 else (1 if i == leaf_x + 1 else 0)
                keep = present(dx, dy)
                value = jnp.where(keep, rim[side, i].astype(F32), 0.0).reshape(points // 2, lanes)
                other = swapped(value)
                y = leaf_y + 1 if side else 0
                grid[i, y, : points // 2, :] = jnp.where(low, value, other).astype(BF16)
                grid[i, y, points // 2 :, :] = jnp.where(low, other, value).astype(BF16)

    scale_local.wait()
    for u in range(1, group):
        scale_copy(u).wait_recv()
    scale_of[...] = got_scale[...].astype(F32).reshape(scale_of.shape) * (1.0 / STEP)

    some = clusters // pieces

    def two_copy(t, h):
        return remote(
            send2.at[t - 1, pl.ds(h * some, some)],
            recv2[t - 1].at[pl.ds(h * some, some)],
            two_send.at[t, h],
            two_recv.at[t, h],
            at_line(plan.hop(t)),
        )

    def twos_copy(t, h):
        return remote(
            send2_scale.at[t - 1, h], recv2_scale[t - 1].at[h], twos_send.at[t, h], twos_recv.at[t, h], at_line(plan.hop(t))
        )

    def collect_all(t):
        one_local(t).wait()
        for u in range(1, group):
            one_copy(t, u).wait_recv()

        def collect(i, total):
            at = t * plan.each + i
            block = decoded(recv1[t][tab[1, at]]) * scale_of[tab[2, at]]
            total = total * tab[3, at].astype(F32) + block
            run[i] = total
            return total

        lax.fori_loop(0, plan.each, collect, jnp.zeros((half, lanes), F32), unroll=8)

        def pick(n, carry):
            own[n] = run[tab[4, t * KEYS + n]] * tab[5, t * KEYS + n].astype(F32)
            return carry

        lax.fori_loop(0, clusters, pick, 0, unroll=10)

    def merge(t, h):
        two_copy(t, h).wait_recv()
        twos_copy(t, h).wait_recv()
        place_scale[...] = recv2_scale[t - 1][h].astype(F32) * (1.0 / STEP)

        def gather(n, carry):
            own[h * some + n] = own[h * some + n] + decoded(recv2[t - 1][h * some + n]) * place_scale[pl.ds(n, 1), :]
            return carry

        lax.fori_loop(0, some, gather, 0, unroll=5)

    def pass_on(t, h):
        group_of = 5 if some % 5 == 0 else 1

        def pack(g, carry):
            first = h * some + g * group_of
            whole, scale = coded(own[pl.ds(first, group_of)])
            send2[t - 1, pl.ds(first, group_of)] = whole
            for q in range(group_of):
                place_scale[pl.ds(g * group_of + q, 1), :] = scale[q : q + 1]
            return carry

        lax.fori_loop(0, some // group_of, pack, 0, unroll=2)
        send2_scale[t - 1, h] = place_scale[...].astype(BF16)
        twos_copy(t, h).start()
        two_copy(t, h).start()

    def descend(p, carry):
        top = own[leaves + p]
        extra = dot(lifts[p], right_of(spread(top, top))).reshape(2 * leaf_x, half, lanes)
        for i in range(leaf_x):
            for q in range(2):
                m = i * leaf_y + 2 * p + q
                own[m] = own[m] + extra[2 * i + q]
        return carry

    place_scale[...] = jnp.zeros_like(place_scale)
    done = 0
    for step, t in enumerate(plan.order):
        collect_all(t)
        if t == 0:
            if step <= 1:
                near_corners()
            if step <= 2:
                near_edges()
            near_field(done, leaf_y - done)
        incoming = [other for other in plan.order if other and plan.into(other) == t]
        for h in range(pieces - 1, -1, -1):
            for other in sorted(incoming):
                merge(other, h)
            if t:
                pass_on(t, h)
            elif h == pieces - 1:
                lax.fori_loop(0, uppers, descend, 0, unroll=4)
        if step == 1 and t:
            near_corners()
        if step == 2 and t:
            near_edges()
        if step >= 2 and t:
            count = min(-(-leaf_y // max(lines - 2, 1)), leaf_y - done)
            near_field(done, count)
            done += count

    def out_copy(j):
        return pltpu.make_async_copy(near.at[j], out_hbm.at[j], out_sem.at[j])

    for j in range(leaf_y):
        high, rest = halves(spread(own[j], own[leaf_y + j]))
        near[j] = near[j] + dot(turned[j], jnp.concatenate([high, rest], axis=0))
        out_copy(j).start()

    for j in range(leaf_y):
        out_copy(j).wait()

    for n in range(8):

        @pl.when(present(*steps[n]))
        def _():
            near_copy(n).wait_send()

    for u in range(1, group):
        scale_copy(u).wait_send()
        for t in range(lines):
            one_copy(t, u).wait_send()
    for t in range(1, lines):
        for h in range(pieces):
            two_copy(t, h).wait_send()
            twos_copy(t, h).wait_send()


def turn_out(sum_ref, out_ref):
    vecs = out_ref.shape[0]
    for x in range(out_ref.shape[2]):
        line = sum_ref[:, x * LS : (x + 1) * LS, :].reshape(out_ref.shape[3], 2 * vecs).T
        out_ref[:, 0, x, :] = line[:vecs]
        out_ref[:, 1, x, :] = line[vecs:]


def body(
    vectors,
    near_tiles,
    near_offset,
    col_basis,
    row_basis,
    up_transfer,
    down_transfer,
    coupling,
    couple_dest,
    couple_target,
):
    vecs, rows_x, rows_y = vectors.shape
    leaf_x, leaf_y = rows_x // LS, rows_y // LS
    leaves = leaf_x * leaf_y
    uppers = leaf_y // 2
    clusters = leaves + uppers
    rank = coupling.shape[2]
    half = rank // 2
    slots = coupling.shape[1]
    near_count = near_tiles.shape[2]
    points = LS * LS
    lanes = 2 * vecs
    plan = Plan(lax.axis_size("qx"), lax.axis_size("qy"), slots)
    lines, group, cap = plan.lines, plan.group, plan.cap
    pieces = 2 if clusters % 2 == 0 else 1
    scale2 = -(-(clusters // pieces) // 16) * 16
    devices = couple_dest.shape[0]
    width = max(plan.total, lines * KEYS)
    vmem, dma = pltpu.VMEM, pltpu.SemaphoreType.DMA
    int16 = jnp.int16
    scratch = [
        vmem((vecs, rows_x, rows_y), BF16),
        vmem((leaves, near_count, points, points), BF16),
        vmem((leaves, rank, points), BF16),
        vmem((leaves, rank, points), BF16),
        vmem((leaves, rank, rank), F32),
        vmem((leaves, rank, rank), F32),
        vmem((rank, rank, slots), F32),
        vmem((vecs, rows_x, rows_y), F32),
        vmem((2, vecs, LS, rows_y), BF16),
        vmem((leaf_x + 2, leaf_y + 2, points, lanes), BF16),
        vmem((2, leaf_x, LS // 2, LS, lanes), BF16),
        vmem((2, 2, LS // 2, LS, lanes), BF16),
        vmem((2, leaf_x + 2, LS // 2, LS, lanes), BF16),
        vmem((slots, half, lanes), F32),
        vmem((clusters, rank, lanes), F32),
        vmem((slots, half, lanes), int16),
        vmem((slots, lanes), F32),
        vmem((scale2, lanes), F32),
        vmem((group, plan.scale_rows, lanes), BF16),
        vmem((group, plan.scale_rows, lanes), BF16),
        vmem((group * plan.scale_rows, 1, lanes), F32),
        vmem((plan.total, half, lanes), int16),
        vmem((devices, slots), I32),
        vmem((devices, slots), I32),
        vmem((group, slots), I32),
        vmem((group, slots), F32),
        vmem((8, width), I32),
        vmem((slots, group * plan.scale_rows), BF16),
        pltpu.SMEM((8, width), I32),
        vmem((plan.each, half, lanes), F32),
        vmem((clusters, half, lanes), F32),
        vmem((max(lines - 1, 1), clusters, half, lanes), int16),
        vmem((max(lines - 1, 1), pieces, scale2, lanes), BF16),
        vmem((leaf_y, points, lanes), F32),
        vmem((leaf_y, points, 4 * rank), BF16),
        vmem((uppers, 2 * leaf_x * half, 6 * rank), BF16),
        dma((9,)),
        dma(()),
        dma((8,)),
        dma((8,)),
        dma((group,)),
        dma((group,)),
        dma((lines, group)),
        dma((lines, group)),
        dma((lines, pieces)),
        dma((lines, pieces)),
        dma((lines, pieces)),
        dma((lines, pieces)),
        dma((lines + 1,)),
        dma((leaf_y,)),
    ]
    scratch += [vmem((plan.each, half, lanes), int16)] * lines
    scratch += [vmem((clusters, half, lanes), int16)] * (lines - 1)
    scratch += [vmem((pieces, scale2, lanes), BF16)] * (lines - 1)
    summed = pl.pallas_call(
        lambda *refs: kernel(plan, *refs),
        out_shape=jax.ShapeDtypeStruct((leaf_y, points, lanes), F32),
        in_specs=[ANY, ANY, SM, ANY, ANY, ANY, ANY, ANY, ANY, ANY],
        out_specs=ANY,
        scratch_shapes=scratch,
        compiler_params=pltpu.CompilerParams(collective_id=0, has_side_effects=True, vmem_limit_bytes=60 << 20),
        name="product",
    )(
        vectors,
        near_tiles.reshape(leaves, near_count, points, points),
        near_offset.transpose(2, 0, 1),
        col_basis.reshape(leaves, rank, points),
        row_basis.reshape(leaves, rank, points),
        up_transfer.reshape(leaves, rank, rank),
        down_transfer.reshape(leaves, rank, rank),
        coupling[0].transpose(1, 2, 0),
        couple_dest,
        couple_target,
    )
    cuts = 2
    part = LS // cuts
    turned = pl.pallas_call(
        turn_out,
        grid=(cuts,),
        out_shape=jax.ShapeDtypeStruct((vecs, leaf_x, LS, rows_y), F32),
        in_specs=[pl.BlockSpec((leaf_y, part * LS, lanes), lambda n: (0, n, 0))],
        out_specs=pl.BlockSpec((vecs, leaf_x, part, rows_y), lambda n: (0, 0, n, 0)),
        name="turn",
    )(summed)
    return turned.reshape(vecs, rows_x, rows_y)


def solution(mesh):
    return jax.shard_map(
        body,
        mesh=mesh,
        in_specs=(
            P(None, "qx", "qy"),
            P("qx", "qy", None, None, None),
            P("qx", "qy", None),
            P("qx", "qy", None, None),
            P("qx", "qy", None, None),
            P("qx", "qy", None, None),
            P("qx", "qy", None, None),
            P(("qx", "qy"), None, None, None),
            P(),
            P(),
        ),
        out_specs=P(None, "qx", "qy"),
        check_vma=False,
    )
```

```python
import jax
import jax.numpy as jnp
from jax import lax
from jax.experimental import pallas as pl
from jax.experimental.pallas import tpu as pltpu
from jax.sharding import PartitionSpec as P

LS = 16
K0 = 6
K1 = 8
KEYS = 32
STEP = 32767.0

ANY = pl.BlockSpec(memory_space=pl.ANY)
VM = pl.BlockSpec(memory_space=pltpu.VMEM)
SM = pl.BlockSpec(memory_space=pltpu.SMEM)
F32 = jnp.float32
BF16 = jnp.bfloat16
I32 = jnp.int32


def halves(value):
    high = value.astype(BF16)
    return high, (value - high.astype(F32)).astype(BF16)


def left_of(value):
    high, low = halves(value)
    return jnp.concatenate([high, low, high], axis=1)


def right_of(value):
    high, low = halves(value)
    return jnp.concatenate([high, high, low], axis=0)


def dot(left, right):
    return jnp.dot(left, right, preferred_element_type=F32)


def swapped(value):
    half = value.shape[-1] // 2
    return jnp.concatenate([value[..., half:], value[..., :half]], axis=-1)


def spread(first, second):
    low = lax.broadcasted_iota(I32, first.shape, 1) < first.shape[1] // 2
    return jnp.concatenate(
        [
            jnp.where(low, first, 0.0),
            jnp.where(low, swapped(first), 0.0),
            jnp.where(low, 0.0, swapped(second)),
            jnp.where(low, 0.0, second),
        ],
        axis=0,
    )


def twice(value):
    low = lax.broadcasted_iota(I32, value.shape, 1) < value.shape[1] // 2
    return jnp.concatenate([jnp.where(low, value, 0.0), jnp.where(low, 0.0, value)], axis=0)


def coded(blocks):
    peak = jnp.max(jnp.abs(blocks), axis=1)
    scale = (jnp.maximum(peak, 1e-30) * 1.004).astype(BF16).astype(F32)
    inverse = STEP / scale
    whole = jnp.round(blocks * inverse[:, None, :]).astype(I32).astype(jnp.int16)
    return whole, scale


def decoded(value):
    return value.astype(I32).astype(F32)


class Plan:
    def __init__(self, width_x, width_y, slots):
        part = max(1, width_y // 2)
        if width_x % part:
            part = 1
        stride = part if width_x % (part * part) == 0 else 1
        self.width_x, self.width_y = width_x, width_y
        self.part, self.stride = part, stride
        self.group = part * width_y
        self.lines = width_x // part
        devices = width_x * width_y
        self.cap = (slots + devices - 1) // devices
        self.total = devices * self.cap
        self.each = self.group * self.cap
        self.scale_rows = -(-(self.lines * self.cap) // 16) * 16
        self.xor_line = self.lines & (self.lines - 1) == 0
        self.xor_group = self.group & (self.group - 1) == 0
        self.order = list(range(self.lines - 1, -1, -1))
        self.hops = sorted({self.hop(t) for t in range(1, self.lines)})

    def hop(self, t):
        return t & -t if self.xor_line else t

    def into(self, t):
        return t - self.hop(t)

    def line(self, z, t):
        return z ^ t if self.xor_line else lax.rem(z + t, self.lines)

    def line_step(self, z, other):
        return other ^ z if self.xor_line else lax.rem(other - z + self.lines, self.lines)

    def peer(self, j, u):
        return j ^ u if self.xor_group else lax.rem(j + u, self.group)

    def place(self, x, y):
        low = lax.rem(x, self.stride)
        rest = lax.div(x, self.stride)
        return lax.div(rest, self.part) * self.stride + low, lax.rem(rest, self.part) * self.width_y + y

    def where(self, z, j):
        high, low = lax.div(z, self.stride), lax.rem(z, self.stride)
        return (high * self.part + lax.div(j, self.width_y)) * self.stride + low, lax.rem(j, self.width_y)

    def index(self, z, j):
        x, y = self.where(z, j)
        return x * self.width_y + y


def tables(plan, clusters, leaves, leaf_y, me_z, me_j, dest_ref, target_ref, dests_ref, targets_ref, tab_ref, order_ref):
    slots = dest_ref.shape[1]
    cap, group, lines = plan.cap, plan.group, plan.lines
    own = dest_ref[pl.ds(plan.index(me_z, me_j), 1), :]
    across = jnp.broadcast_to(own.astype(F32), (slots, slots))
    down = across.T
    row = lax.broadcasted_iota(I32, (slots, slots), 0)
    col = lax.broadcasted_iota(I32, (slots, slots), 1)
    order = jnp.sum(jnp.where((across == down) & (col < row), 1.0, 0.0), axis=1, keepdims=True)
    dest = down[:, :1].astype(I32)
    whole = jnp.maximum(dest, 0)
    line, peer = plan.place(lax.div(whole, plan.width_y), lax.rem(whole, plan.width_y))
    step = plan.line_step(me_z, line)
    scale_place = jnp.where(dest >= 0, peer * plan.scale_rows + step * cap + order.astype(I32), -1)
    rows = order_ref.shape[1]
    order_ref[...] = jnp.where(
        scale_place == lax.broadcasted_iota(I32, (slots, rows), 1), 1.0, 0.0
    ).astype(BF16)
    place = (step * group + peer) * cap + order.astype(I32)
    place = jnp.where(dest >= 0, place, -1)
    lane = lax.broadcasted_iota(I32, (slots, plan.total), 1)
    slot = lax.broadcasted_iota(I32, (slots, plan.total), 0).astype(F32)
    slot_of = jnp.sum(jnp.where(place == lane, slot, 0.0), axis=0, keepdims=True)

    for j in range(group):
        at = plan.index(me_z, j)
        dests_ref[j : j + 1, :] = dest_ref[pl.ds(at, 1), :]
        target = target_ref[pl.ds(at, 1), :]
        paired = lax.rem(target, leaf_y) * (leaves // leaf_y) + lax.div(target, leaf_y)
        targets_ref[j : j + 1, :] = jnp.where(target < leaves, paired, target).astype(F32)
    dests, targets = dests_ref[...], targets_ref[...]
    match = jnp.concatenate([dests == plan.index(plan.line(me_z, t), me_j) for t in range(lines)], axis=0)
    target = jnp.concatenate([targets] * lines, axis=0)
    before = jnp.where(row < col, 1.0, 0.0).astype(BF16)
    rank_in = dot(jnp.where(match, 1.0, 0.0).astype(BF16), before)
    rows = lines * group
    step_row = lax.div(lax.broadcasted_iota(I32, (rows, 1), 0), group)
    from_row = lax.rem(lax.broadcasted_iota(I32, (rows, 1), 0), group)
    keys, blocks, scales = [], [], []
    for k in range(cap):
        landing = match & (rank_in == float(k))
        mine = clusters + jnp.sum(jnp.where(landing, target - clusters, 0.0), axis=1, keepdims=True)
        keys.append(mine + (step_row * KEYS).astype(F32))
        blocks.append((from_row * cap + k).astype(F32))
        scales.append((from_row * plan.scale_rows + step_row * cap + k).astype(F32))
    total = plan.total
    key_row = jnp.broadcast_to(jnp.concatenate(keys, axis=0), (total, total))
    key_col = key_row.T
    row = lax.broadcasted_iota(I32, (total, total), 0)
    col = lax.broadcasted_iota(I32, (total, total), 1)
    earlier = (key_row == key_col) & (col < row)
    rank = jnp.sum(jnp.where((key_col < key_row) | earlier, 1.0, 0.0), axis=1, keepdims=True)
    follows = jnp.max(jnp.where(earlier, 1.0, 0.0), axis=1, keepdims=True)
    hit = rank == col.astype(F32)

    def sorted_row(values):
        return jnp.sum(jnp.where(hit, values, 0.0), axis=0, keepdims=True)

    wide = lines * KEYS
    key = jnp.concatenate(keys, axis=0)
    place = lax.broadcasted_iota(I32, (total, wide), 1)
    code = place.astype(F32)
    last = jnp.sum(jnp.where(key <= code, 1.0, 0.0), axis=0, keepdims=True) - 1.0
    last = last - (lax.div(place[:1], KEYS) * plan.each).astype(F32)
    there = jnp.max(jnp.where(key == code, 1.0, 0.0), axis=0, keepdims=True)

    def put(at, values, size):
        tab_ref[at : at + 1, : values.shape[1]] = jnp.clip(values.astype(I32), 0, size - 1)

    put(0, slot_of, slots)
    put(1, sorted_row(jnp.concatenate(blocks, axis=0)), plan.each)
    put(2, sorted_row(jnp.concatenate(scales, axis=0)), group * plan.scale_rows)
    put(3, sorted_row(follows), 2)
    put(4, last, plan.each)
    put(5, there, 2)


def kernel(plan, *refs):
    lines, group, cap = plan.lines, plan.group, plan.cap
    (
        vec_hbm, tiles_hbm, off_ref, col_hbm, row_hbm, up_hbm, down_hbm, coup_hbm, dest_hbm, target_hbm,
        out_hbm,
        vec, tiles, col, row, up, down, coup,
        wide, halo, grid, strips, corners, rim, mats, coef, held, held_scale,
        place_scale, send_scale, got_scale, scale_of, send1,
        dest, target, dests, targets, tab_v, order_of, tab, run, own, send2, send2_scale, near, turned, lifts,
        load_sem, tab_sem, near_send, near_recv, scale_send, scale_recv,
        one_send, one_recv, two_send, two_recv, twos_send, twos_recv, local_sem, out_sem,
        *landing,
    ) = refs
    recv1 = landing[:lines]
    recv2 = landing[lines : 2 * lines - 1]
    recv2_scale = landing[2 * lines - 1 :]

    here_x = lax.axis_index("qx")
    here_y = lax.axis_index("qy")
    me_z, me_j = plan.place(here_x, here_y)
    vecs, rows_x, rows_y = vec.shape
    leaf_x, leaf_y = rows_x // LS, rows_y // LS
    leaves = leaf_x * leaf_y
    uppers = leaf_y // 2
    clusters = leaves + uppers
    rank = coup.shape[0]
    half = rank // 2
    lanes = 2 * vecs
    points = LS * LS
    low = lax.broadcasted_iota(I32, (1, lanes), 1) < vecs
    pieces = send2_scale.shape[1]

    pairs = [
        (vec_hbm, vec),
        (col_hbm, col),
        (up_hbm, up),
        (coup_hbm, coup),
        (row_hbm, row),
        (down_hbm, down),
        (tiles_hbm, tiles),
        (dest_hbm, dest),
        (target_hbm, target),
    ]
    loads = [pltpu.make_async_copy(src, dst, load_sem.at[n]) for n, (src, dst) in enumerate(pairs)]
    for n in (7, 8, 0, 1, 3, 2):
        loads[n].start()

    def at_line(t):
        return plan.where(plan.line(me_z, t), me_j)

    def at_peer(u):
        return plan.where(me_z, plan.peer(me_j, u))

    steps = [(1, 0), (-1, 0), (0, 1), (0, -1), (0, 1), (0, -1), (0, 1), (0, -1)]

    def present(dx, dy):
        x = here_x + dx
        y = here_y + dy
        return (x >= 0) & (x < plan.width_x) & (y >= 0) & (y < plan.width_y)

    barrier = pltpu.get_barrier_semaphore()

    def greet(device):
        pl.semaphore_signal(barrier, inc=1, device_id=device, device_id_type=pl.DeviceIdType.MESH)

    for dx, dy in steps[:4]:

        @pl.when(present(dx, dy))
        def _():
            greet((here_x + dx, here_y + dy))

    for u in range(1, group):
        greet(at_peer(u))
    for t in plan.hops:
        greet(at_line(t))

    loads[7].wait()
    loads[8].wait()
    tables(plan, clusters, leaves, leaf_y, me_z, me_j, dest, target, dests, targets, tab_v, order_of)
    tab_copy = pltpu.make_async_copy(tab_v, tab, tab_sem)
    tab_copy.start()
    loads[0].wait()

    spans = []
    for here, width in ((here_x, plan.width_x), (here_y, plan.width_y)):
        spans.append((here > 0).astype(I32) + (here < width - 1).astype(I32))
    pl.semaphore_wait(barrier, spans[0] + spans[1] + group - 1 + len(plan.hops))

    def remote(src, dst, send, recv, device):
        return pltpu.make_async_remote_copy(
            src_ref=src,
            dst_ref=dst,
            send_sem=send,
            recv_sem=recv,
            device_id=device,
            device_id_type=pl.DeviceIdType.MESH,
        )

    def near_copy(n):
        dx, dy = steps[n]
        if dy == 0:
            src = vec.at[:, pl.ds(rows_x - LS if dx > 0 else 0, LS), :]
            dst = halo.at[0 if dx > 0 else 1]
        else:
            side = 1 if dy > 0 else 0
            if n < 4:
                src = strips.at[side]
                dst = rim.at[1 - side, pl.ds(1, leaf_x)]
            else:
                end = (n - 4) // 2
                src = corners.at[end, side]
                dst = rim.at[1 - side, end * (leaf_x + 1)]
        return remote(src, dst, near_send.at[n], near_recv.at[n], (here_x + dx, here_y + dy))

    def near_start(first, end):
        for n in range(first, end):

            @pl.when(present(*steps[n]))
            def _():
                near_copy(n).start()

    near_start(0, 2)

    wide[...] = vec[...].astype(F32)

    def to_grid(x, carry):
        plane = wide[:, x, :]
        lines_of = jnp.concatenate([plane, plane], axis=0).T.astype(BF16).reshape(leaf_y, LS, lanes)
        at = pl.multiple_of(lax.rem(x, LS) * LS, LS)
        grid[1 + lax.div(x, LS), 1 : 1 + leaf_y, pl.ds(at, LS), :] = lines_of
        return carry

    lax.fori_loop(0, rows_x, to_grid, 0, unroll=16)
    for side in range(2):
        for i in range(leaf_x):
            block = grid[1 + i, leaf_y if side else 1].reshape(2, LS // 2, LS, lanes)
            strips[side, i] = jnp.where(low, block[0], block[1])
    near_start(2, 4)

    loads[1].wait()

    def leaf_coef(m, carry):
        i = lax.div(m, leaf_y)
        j = lax.rem(m, leaf_y)
        coef[m] = dot(col[m], grid[1 + i, 1 + j])
        return carry

    lax.fori_loop(0, leaves, leaf_coef, 0, unroll=16)
    loads[2].wait()

    def upper_coef(p, carry):
        children = [i * leaf_y + 2 * p + q for i in range(leaf_x) for q in range(2)]
        left = jnp.concatenate([up[m] for m in children], axis=1)
        right = jnp.concatenate([coef[m] for m in children], axis=0)
        coef[leaves + p] = dot(left_of(left), right_of(right))
        return carry

    lax.fori_loop(0, uppers, upper_coef, 0, unroll=4)

    loads[3].wait()
    for n in (4, 5, 6):
        loads[n].start()

    def turn(r, carry):
        mats[:, r, :] = jnp.concatenate([coup[r], coup[r + half]], axis=0).T
        return carry

    lax.fori_loop(0, half, turn, 0, unroll=16)

    def contribute(first, count, m):
        left = jnp.concatenate(halves(mats[pl.ds(first, count)].reshape(count * half, lanes)), axis=1)
        high, rest = halves(twice(coef[m]))
        right = jnp.concatenate([jnp.concatenate([high, high], axis=0), jnp.concatenate([rest, jnp.zeros_like(rest)], axis=0)], axis=1)
        both = dot(left, right)
        blocks = (both[:, :lanes] + both[:, lanes:]).reshape(count, half, lanes)
        whole, scale = coded(blocks)
        held[pl.ds(first, count)] = whole
        for q in range(count):
            held_scale[pl.ds(first + q, 1), :] = scale[q : q + 1]

    def leaf_slots(m, carry):
        contribute(m * K0, K0, m)
        return carry

    def upper_slots(p, carry):
        contribute(leaves * K0 + p * K1, K1, leaves + p)
        return carry

    lax.fori_loop(0, leaves, leaf_slots, 0, unroll=16)
    lax.fori_loop(0, uppers, upper_slots, 0, unroll=4)

    tab_copy.wait()
    ordered = lax.dot_general(
        order_of[...], held_scale[...].astype(BF16), (((0,), (0,)), ((), ())), preferred_element_type=F32
    )
    send_scale[...] = ordered.astype(BF16).reshape(send_scale.shape)

    def scale_copy(u):
        return remote(
            send_scale.at[plan.peer(me_j, u)], got_scale.at[me_j], scale_send.at[u], scale_recv.at[u], at_peer(u)
        )

    def one_copy(t, u):
        return remote(
            send1.at[pl.ds((t * group + plan.peer(me_j, u)) * cap, cap)],
            recv1[t].at[pl.ds(me_j * cap, cap)],
            one_send.at[t, u],
            one_recv.at[t, u],
            at_peer(u),
        )

    def one_local(t):
        return pltpu.make_async_copy(
            send1.at[pl.ds((t * group + me_j) * cap, cap)], recv1[t].at[pl.ds(me_j * cap, cap)], local_sem.at[t]
        )

    scale_local = pltpu.make_async_copy(send_scale.at[me_j], got_scale.at[me_j], local_sem.at[lines])
    scale_local.start()
    for u in range(1, group):
        scale_copy(u).start()

    for t in plan.order:

        def put(p, carry, t=t):
            send1[t * plan.each + p] = held[tab[0, t * plan.each + p]]
            return carry

        lax.fori_loop(0, plan.each, put, 0, unroll=32)
        for u in range(1, group):
            one_copy(t, u).start()
        one_local(t).start()

    loads[4].wait()
    loads[5].wait()

    def turn_row(j, carry):
        pair = jnp.concatenate([row[j], row[leaf_y + j]], axis=0)
        basis = pair.astype(F32).T.astype(BF16)
        turned[j] = jnp.concatenate([basis, basis], axis=1)
        return carry

    lax.fori_loop(0, leaf_y, turn_row, 0, unroll=2)

    def lift(p, carry):
        parts = []
        for i in range(leaf_x):
            for q in range(2):
                mat = down[i * leaf_y + 2 * p + q]
                parts.append(jnp.concatenate([mat[:half], mat[half:]], axis=1))
        lifts[p] = left_of(jnp.concatenate(parts, axis=0))
        return carry

    lax.fori_loop(0, uppers, lift, 0, unroll=2)

    def near_field(first, count):
        def pair(j, carry):
            sums = []
            for i in range(leaf_x):
                m = i * leaf_y + j
                total = None
                for k in range(tiles.shape[1]):
                    o = off_ref[k, i, j]
                    term = dot(tiles[m, k], grid[i + lax.div(o, 3), j + lax.rem(o, 3)])
                    total = term if total is None else total + term
                sums.append(total)
            near[j] = jnp.where(low, sums[0], sums[1])
            return carry

        lax.fori_loop(first, first + count, pair, 0)

    def near_rows():
        for side in range(2):
            keep = present(2 * side - 1, 0)
            wide[:, side * LS : (side + 1) * LS, :] = jnp.where(keep, halo[side].astype(F32), 0.0)

        def to_rows(x, carry):
            plane = wide[:, x, :]
            lines_of = jnp.concatenate([plane, plane], axis=0).T.astype(BF16).reshape(leaf_y, LS, lanes)
            at = pl.multiple_of(lax.rem(x, LS) * LS, LS)
            grid[lax.div(x, LS) * (leaf_x + 1), 1 : 1 + leaf_y, pl.ds(at, LS), :] = lines_of
            return carry

        lax.fori_loop(0, 2 * LS, to_rows, 0, unroll=4)

    def near_wait(first, end):
        for n in range(first, end):

            @pl.when(present(-steps[n][0], -steps[n][1]))
            def _():
                near_copy(n).wait_recv()

    def near_corners():
        near_wait(0, 2)
        near_rows()
        for end in range(2):
            for side in range(2):
                block = grid[end * (leaf_x + 1), leaf_y if side else 1].reshape(2, LS // 2, LS, lanes)
                corners[end, side] = jnp.where(low, block[0], block[1])
        near_start(4, 8)

    def near_edges():
        near_wait(2, 8)
        loads[6].wait()
        for side in range(2):
            dy = 1 if side else -1
            for i in range(leaf_x + 2):
                dx = -1 if i == 0 else (1 if i == leaf_x + 1 else 0)
                keep = present(dx, dy)
                value = jnp.where(keep, rim[side, i].astype(F32), 0.0).reshape(points // 2, lanes)
                other = swapped(value)
                y = leaf_y + 1 if side else 0
                grid[i, y, : points // 2, :] = jnp.where(low, value, other).astype(BF16)
                grid[i, y, points // 2 :, :] = jnp.where(low, other, value).astype(BF16)

    scale_local.wait()
    for u in range(1, group):
        scale_copy(u).wait_recv()
    scale_of[...] = got_scale[...].astype(F32).reshape(scale_of.shape) * (1.0 / STEP)

    some = clusters // pieces

    def two_copy(t, h):
        return remote(
            send2.at[t - 1, pl.ds(h * some, some)],
            recv2[t - 1].at[pl.ds(h * some, some)],
            two_send.at[t, h],
            two_recv.at[t, h],
            at_line(plan.hop(t)),
        )

    def twos_copy(t, h):
        return remote(
            send2_scale.at[t - 1, h], recv2_scale[t - 1].at[h], twos_send.at[t, h], twos_recv.at[t, h], at_line(plan.hop(t))
        )

    def collect_all(t):
        one_local(t).wait()
        for u in range(1, group):
            one_copy(t, u).wait_recv()

        def collect(i, total):
            at = t * plan.each + i
            block = decoded(recv1[t][tab[1, at]]) * scale_of[tab[2, at]]
            total = total * tab[3, at].astype(F32) + block
            run[i] = total
            return total

        lax.fori_loop(0, plan.each, collect, jnp.zeros((half, lanes), F32), unroll=8)

        def pick(n, carry):
            own[n] = run[tab[4, t * KEYS + n]] * tab[5, t * KEYS + n].astype(F32)
            return carry

        lax.fori_loop(0, clusters, pick, 0, unroll=10)

    def merge(t, h):
        two_copy(t, h).wait_recv()
        twos_copy(t, h).wait_recv()
        place_scale[...] = recv2_scale[t - 1][h].astype(F32) * (1.0 / STEP)

        def gather(n, carry):
            own[h * some + n] = own[h * some + n] + decoded(recv2[t - 1][h * some + n]) * place_scale[pl.ds(n, 1), :]
            return carry

        lax.fori_loop(0, some, gather, 0, unroll=5)

    def pass_on(t, h):
        group_of = 5 if some % 5 == 0 else 1

        def pack(g, carry):
            first = h * some + g * group_of
            whole, scale = coded(own[pl.ds(first, group_of)])
            send2[t - 1, pl.ds(first, group_of)] = whole
            for q in range(group_of):
                place_scale[pl.ds(g * group_of + q, 1), :] = scale[q : q + 1]
            return carry

        lax.fori_loop(0, some // group_of, pack, 0, unroll=2)
        send2_scale[t - 1, h] = place_scale[...].astype(BF16)
        twos_copy(t, h).start()
        two_copy(t, h).start()

    def descend(p, carry):
        top = own[leaves + p]
        extra = dot(lifts[p], right_of(spread(top, top))).reshape(2 * leaf_x, half, lanes)
        for i in range(leaf_x):
            for q in range(2):
                m = leaf_x * (2 * p + q) + i
                own[m] = own[m] + extra[2 * i + q]
        return carry

    def out_copy(j):
        return pltpu.make_async_copy(near.at[j], out_hbm.at[j], out_sem.at[j])

    def far_field(first, end):
        for j in range(first, end):
            high, rest = halves(spread(own[leaf_x * j], own[leaf_x * j + 1]))
            near[j] = near[j] + dot(turned[j], jnp.concatenate([high, rest], axis=0))
            out_copy(j).start()

    place_scale[...] = jnp.zeros_like(place_scale)
    done = 0
    for step, t in enumerate(plan.order):
        collect_all(t)
        if t == 0:
            if step <= 1:
                near_corners()
            if step <= 2:
                near_edges()
            near_field(done, leaf_y - done)
        incoming = [other for other in plan.order if other and plan.into(other) == t]
        for h in range(pieces - 1, -1, -1):
            for other in sorted(incoming):
                merge(other, h)
            if t:
                pass_on(t, h)
            else:
                if h == pieces - 1:
                    lax.fori_loop(0, uppers, descend, 0, unroll=4)
                    left = leaf_y
                whole = -(-h * some // leaf_x)
                far_field(whole, left)
                left = min(whole, left)
        if step == 1 and t:
            near_corners()
        if step == 2 and t:
            near_edges()
        if step >= 2 and t:
            count = min(-(-leaf_y // max(lines - 2, 1)), leaf_y - done)
            near_field(done, count)
            done += count

    for j in range(leaf_y):
        out_copy(j).wait()

    for n in range(8):

        @pl.when(present(*steps[n]))
        def _():
            near_copy(n).wait_send()

    for u in range(1, group):
        scale_copy(u).wait_send()
        for t in range(lines):
            one_copy(t, u).wait_send()
    for t in range(1, lines):
        for h in range(pieces):
            two_copy(t, h).wait_send()
            twos_copy(t, h).wait_send()


def turn_out(sum_ref, out_ref):
    vecs = out_ref.shape[0]
    for x in range(out_ref.shape[2]):
        line = sum_ref[:, x * LS : (x + 1) * LS, :].reshape(out_ref.shape[3], 2 * vecs).T
        out_ref[:, 0, x, :] = line[:vecs]
        out_ref[:, 1, x, :] = line[vecs:]


def body(
    vectors,
    near_tiles,
    near_offset,
    col_basis,
    row_basis,
    up_transfer,
    down_transfer,
    coupling,
    couple_dest,
    couple_target,
):
    vecs, rows_x, rows_y = vectors.shape
    leaf_x, leaf_y = rows_x // LS, rows_y // LS
    leaves = leaf_x * leaf_y
    uppers = leaf_y // 2
    clusters = leaves + uppers
    rank = coupling.shape[2]
    half = rank // 2
    slots = coupling.shape[1]
    near_count = near_tiles.shape[2]
    points = LS * LS
    lanes = 2 * vecs
    plan = Plan(lax.axis_size("qx"), lax.axis_size("qy"), slots)
    lines, group, cap = plan.lines, plan.group, plan.cap
    pieces = 2 if clusters % 2 == 0 else 1
    scale2 = -(-(clusters // pieces) // 16) * 16
    devices = couple_dest.shape[0]
    width = max(plan.total, lines * KEYS)
    vmem, dma = pltpu.VMEM, pltpu.SemaphoreType.DMA
    int16 = jnp.int16
    scratch = [
        vmem((vecs, rows_x, rows_y), BF16),
        vmem((leaves, near_count, points, points), BF16),
        vmem((leaves, rank, points), BF16),
        vmem((leaves, rank, points), BF16),
        vmem((leaves, rank, rank), F32),
        vmem((leaves, rank, rank), F32),
        vmem((rank, rank, slots), F32),
        vmem((vecs, rows_x, rows_y), F32),
        vmem((2, vecs, LS, rows_y), BF16),
        vmem((leaf_x + 2, leaf_y + 2, points, lanes), BF16),
        vmem((2, leaf_x, LS // 2, LS, lanes), BF16),
        vmem((2, 2, LS // 2, LS, lanes), BF16),
        vmem((2, leaf_x + 2, LS // 2, LS, lanes), BF16),
        vmem((slots, half, lanes), F32),
        vmem((clusters, rank, lanes), F32),
        vmem((slots, half, lanes), int16),
        vmem((slots, lanes), F32),
        vmem((scale2, lanes), F32),
        vmem((group, plan.scale_rows, lanes), BF16),
        vmem((group, plan.scale_rows, lanes), BF16),
        vmem((group * plan.scale_rows, 1, lanes), F32),
        vmem((plan.total, half, lanes), int16),
        vmem((devices, slots), I32),
        vmem((devices, slots), I32),
        vmem((group, slots), I32),
        vmem((group, slots), F32),
        vmem((8, width), I32),
        vmem((slots, group * plan.scale_rows), BF16),
        pltpu.SMEM((8, width), I32),
        vmem((plan.each, half, lanes), F32),
        vmem((clusters, half, lanes), F32),
        vmem((max(lines - 1, 1), clusters, half, lanes), int16),
        vmem((max(lines - 1, 1), pieces, scale2, lanes), BF16),
        vmem((leaf_y, points, lanes), F32),
        vmem((leaf_y, points, 4 * rank), BF16),
        vmem((uppers, 2 * leaf_x * half, 6 * rank), BF16),
        dma((9,)),
        dma(()),
        dma((8,)),
        dma((8,)),
        dma((group,)),
        dma((group,)),
        dma((lines, group)),
        dma((lines, group)),
        dma((lines, pieces)),
        dma((lines, pieces)),
        dma((lines, pieces)),
        dma((lines, pieces)),
        dma((lines + 1,)),
        dma((leaf_y,)),
    ]
    scratch += [vmem((plan.each, half, lanes), int16)] * lines
    scratch += [vmem((clusters, half, lanes), int16)] * (lines - 1)
    scratch += [vmem((pieces, scale2, lanes), BF16)] * (lines - 1)
    summed = pl.pallas_call(
        lambda *refs: kernel(plan, *refs),
        out_shape=jax.ShapeDtypeStruct((leaf_y, points, lanes), F32),
        in_specs=[ANY, ANY, SM, ANY, ANY, ANY, ANY, ANY, ANY, ANY],
        out_specs=ANY,
        scratch_shapes=scratch,
        compiler_params=pltpu.CompilerParams(collective_id=0, has_side_effects=True, vmem_limit_bytes=60 << 20),
        name="product",
    )(
        vectors,
        near_tiles.reshape(leaves, near_count, points, points),
        near_offset.transpose(2, 0, 1),
        col_basis.reshape(leaves, rank, points),
        row_basis.reshape(leaves, rank, points),
        up_transfer.reshape(leaves, rank, rank),
        down_transfer.reshape(leaves, rank, rank),
        coupling[0].transpose(1, 2, 0),
        couple_dest,
        couple_target,
    )
    cuts = 2
    part = LS // cuts
    turned = pl.pallas_call(
        turn_out,
        grid=(cuts,),
        out_shape=jax.ShapeDtypeStruct((vecs, leaf_x, LS, rows_y), F32),
        in_specs=[pl.BlockSpec((leaf_y, part * LS, lanes), lambda n: (0, n, 0))],
        out_specs=pl.BlockSpec((vecs, leaf_x, part, rows_y), lambda n: (0, 0, n, 0)),
        name="turn",
    )(summed)
    return turned.reshape(vecs, rows_x, rows_y)


def solution(mesh):
    return jax.shard_map(
        body,
        mesh=mesh,
        in_specs=(
            P(None, "qx", "qy"),
            P("qx", "qy", None, None, None),
            P("qx", "qy", None),
            P("qx", "qy", None, None),
            P("qx", "qy", None, None),
            P("qx", "qy", None, None),
            P("qx", "qy", None, None),
            P(("qx", "qy"), None, None, None),
            P(),
            P(),
        ),
        out_specs=P(None, "qx", "qy"),
        check_vma=False,
    )
```

```python
import jax
import jax.numpy as jnp
from jax import lax
from jax.experimental import pallas as pl
from jax.experimental.pallas import tpu as pltpu
from jax.sharding import PartitionSpec as P

LS = 16
K0 = 6
K1 = 8
KEYS = 32
STEP = 32767.0

ANY = pl.BlockSpec(memory_space=pl.ANY)
VM = pl.BlockSpec(memory_space=pltpu.VMEM)
SM = pl.BlockSpec(memory_space=pltpu.SMEM)
F32 = jnp.float32
BF16 = jnp.bfloat16
I32 = jnp.int32


def halves(value):
    high = value.astype(BF16)
    return high, (value - high.astype(F32)).astype(BF16)


def left_of(value):
    high, low = halves(value)
    return jnp.concatenate([high, low, high], axis=1)


def right_of(value):
    high, low = halves(value)
    return jnp.concatenate([high, high, low], axis=0)


def dot(left, right):
    return jnp.dot(left, right, preferred_element_type=F32)


def swapped(value):
    half = value.shape[-1] // 2
    return jnp.concatenate([value[..., half:], value[..., :half]], axis=-1)


def spread(first, second):
    low = lax.broadcasted_iota(I32, first.shape, 1) < first.shape[1] // 2
    return jnp.concatenate(
        [
            jnp.where(low, first, 0.0),
            jnp.where(low, swapped(first), 0.0),
            jnp.where(low, 0.0, swapped(second)),
            jnp.where(low, 0.0, second),
        ],
        axis=0,
    )


def twice(value):
    low = lax.broadcasted_iota(I32, value.shape, 1) < value.shape[1] // 2
    return jnp.concatenate([jnp.where(low, value, 0.0), jnp.where(low, 0.0, value)], axis=0)


def coded(blocks):
    peak = jnp.max(jnp.abs(blocks), axis=1)
    scale = (jnp.maximum(peak, 1e-30) * 1.004).astype(BF16).astype(F32)
    inverse = STEP / scale
    whole = jnp.round(blocks * inverse[:, None, :]).astype(I32).astype(jnp.int16)
    return whole, scale


def decoded(value):
    return value.astype(I32).astype(F32)


class Plan:
    def __init__(self, width_x, width_y, slots):
        part = max(1, width_y // 2)
        if width_x % part:
            part = 1
        stride = part if width_x % (part * part) == 0 else 1
        self.width_x, self.width_y = width_x, width_y
        self.part, self.stride = part, stride
        self.group = part * width_y
        self.lines = width_x // part
        devices = width_x * width_y
        self.cap = (slots + devices - 1) // devices
        self.total = devices * self.cap
        self.each = self.group * self.cap
        self.scale_rows = -(-(self.lines * self.cap) // 16) * 16
        self.xor_line = self.lines & (self.lines - 1) == 0
        self.xor_group = self.group & (self.group - 1) == 0
        self.order = list(range(self.lines - 1, -1, -1))
        self.hops = sorted({self.hop(t) for t in range(1, self.lines)})

    def hop(self, t):
        return t & -t if self.xor_line else t

    def into(self, t):
        return t - self.hop(t)

    def line(self, z, t):
        return z ^ t if self.xor_line else lax.rem(z + t, self.lines)

    def line_step(self, z, other):
        return other ^ z if self.xor_line else lax.rem(other - z + self.lines, self.lines)

    def peer(self, j, u):
        return j ^ u if self.xor_group else lax.rem(j + u, self.group)

    def place(self, x, y):
        low = lax.rem(x, self.stride)
        rest = lax.div(x, self.stride)
        return lax.div(rest, self.part) * self.stride + low, lax.rem(rest, self.part) * self.width_y + y

    def where(self, z, j):
        high, low = lax.div(z, self.stride), lax.rem(z, self.stride)
        return (high * self.part + lax.div(j, self.width_y)) * self.stride + low, lax.rem(j, self.width_y)

    def index(self, z, j):
        x, y = self.where(z, j)
        return x * self.width_y + y


def tables(plan, clusters, leaves, leaf_y, me_z, me_j, dest_ref, target_ref, dests_ref, targets_ref, tab_ref, order_ref):
    slots = dest_ref.shape[1]
    cap, group, lines = plan.cap, plan.group, plan.lines
    own = dest_ref[pl.ds(plan.index(me_z, me_j), 1), :]
    across = jnp.broadcast_to(own.astype(F32), (slots, slots))
    down = across.T
    row = lax.broadcasted_iota(I32, (slots, slots), 0)
    col = lax.broadcasted_iota(I32, (slots, slots), 1)
    order = jnp.sum(jnp.where((across == down) & (col < row), 1.0, 0.0), axis=1, keepdims=True)
    dest = down[:, :1].astype(I32)
    whole = jnp.maximum(dest, 0)
    line, peer = plan.place(lax.div(whole, plan.width_y), lax.rem(whole, plan.width_y))
    step = plan.line_step(me_z, line)
    scale_place = jnp.where(dest >= 0, peer * plan.scale_rows + step * cap + order.astype(I32), -1)
    rows = order_ref.shape[1]
    order_ref[...] = jnp.where(
        scale_place == lax.broadcasted_iota(I32, (slots, rows), 1), 1.0, 0.0
    ).astype(BF16)
    place = (step * group + peer) * cap + order.astype(I32)
    place = jnp.where(dest >= 0, place, -1)
    lane = lax.broadcasted_iota(I32, (slots, plan.total), 1)
    slot = lax.broadcasted_iota(I32, (slots, plan.total), 0).astype(F32)
    slot_of = jnp.sum(jnp.where(place == lane, slot, 0.0), axis=0, keepdims=True)

    for j in range(group):
        at = plan.index(me_z, j)
        dests_ref[j : j + 1, :] = dest_ref[pl.ds(at, 1), :]
        target = target_ref[pl.ds(at, 1), :]
        paired = lax.rem(target, leaf_y) * (leaves // leaf_y) + lax.div(target, leaf_y)
        targets_ref[j : j + 1, :] = jnp.where(target < leaves, paired, target).astype(F32)
    dests, targets = dests_ref[...], targets_ref[...]
    match = jnp.concatenate([dests == plan.index(plan.line(me_z, t), me_j) for t in range(lines)], axis=0)
    target = jnp.concatenate([targets] * lines, axis=0)
    before = jnp.where(row < col, 1.0, 0.0).astype(BF16)
    rank_in = dot(jnp.where(match, 1.0, 0.0).astype(BF16), before)
    rows = lines * group
    step_row = lax.div(lax.broadcasted_iota(I32, (rows, 1), 0), group)
    from_row = lax.rem(lax.broadcasted_iota(I32, (rows, 1), 0), group)
    keys, blocks, scales = [], [], []
    for k in range(cap):
        landing = match & (rank_in == float(k))
        mine = clusters + jnp.sum(jnp.where(landing, target - clusters, 0.0), axis=1, keepdims=True)
        keys.append(mine + (step_row * KEYS).astype(F32))
        blocks.append((from_row * cap + k).astype(F32))
        scales.append((from_row * plan.scale_rows + step_row * cap + k).astype(F32))
    total = plan.total
    key_row = jnp.broadcast_to(jnp.concatenate(keys, axis=0), (total, total))
    key_col = key_row.T
    row = lax.broadcasted_iota(I32, (total, total), 0)
    col = lax.broadcasted_iota(I32, (total, total), 1)
    earlier = (key_row == key_col) & (col < row)
    rank = jnp.sum(jnp.where((key_col < key_row) | earlier, 1.0, 0.0), axis=1, keepdims=True)
    follows = jnp.max(jnp.where(earlier, 1.0, 0.0), axis=1, keepdims=True)
    hit = rank == col.astype(F32)

    def sorted_row(values):
        return jnp.sum(jnp.where(hit, values, 0.0), axis=0, keepdims=True)

    wide = lines * KEYS
    key = jnp.concatenate(keys, axis=0)
    place = lax.broadcasted_iota(I32, (total, wide), 1)
    code = place.astype(F32)
    last = jnp.sum(jnp.where(key <= code, 1.0, 0.0), axis=0, keepdims=True) - 1.0
    last = last - (lax.div(place[:1], KEYS) * plan.each).astype(F32)
    there = jnp.max(jnp.where(key == code, 1.0, 0.0), axis=0, keepdims=True)

    def put(at, values, size):
        tab_ref[at : at + 1, : values.shape[1]] = jnp.clip(values.astype(I32), 0, size - 1)

    put(0, slot_of, slots)
    put(1, sorted_row(jnp.concatenate(blocks, axis=0)), plan.each)
    put(2, sorted_row(jnp.concatenate(scales, axis=0)), group * plan.scale_rows)
    put(3, sorted_row(follows), 2)
    put(4, last, plan.each)
    put(5, there, 2)


def kernel(plan, *refs):
    lines, group, cap = plan.lines, plan.group, plan.cap
    (
        vec_hbm, tiles_hbm, off_ref, col_hbm, row_hbm, up_hbm, down_hbm, coup_hbm, dest_hbm, target_hbm,
        out_hbm,
        vec, tiles, col, row, up, down, coup,
        wide, halo, grid, strips, corners, rim, mats, coef, held, held_scale,
        place_scale, send_scale, got_scale, scale_of, send1,
        dest, target, dests, targets, tab_v, order_of, tab, run, own, send2, send2_scale, near, turned, lifts,
        load_sem, tab_sem, near_send, near_recv, scale_send, scale_recv,
        one_send, one_recv, two_send, two_recv, twos_send, twos_recv, local_sem, out_sem,
        *landing,
    ) = refs
    recv1 = landing[:lines]
    recv2 = landing[lines : 2 * lines - 1]
    recv2_scale = landing[2 * lines - 1 :]

    here_x = lax.axis_index("qx")
    here_y = lax.axis_index("qy")
    me_z, me_j = plan.place(here_x, here_y)
    vecs, rows_x, rows_y = vec.shape
    leaf_x, leaf_y = rows_x // LS, rows_y // LS
    leaves = leaf_x * leaf_y
    uppers = leaf_y // 2
    clusters = leaves + uppers
    rank = coup.shape[0]
    half = rank // 2
    lanes = 2 * vecs
    points = LS * LS
    low = lax.broadcasted_iota(I32, (1, lanes), 1) < vecs
    pieces = send2_scale.shape[1]

    pairs = [
        (vec_hbm, vec),
        (col_hbm, col),
        (up_hbm, up),
        (coup_hbm, coup),
        (row_hbm, row),
        (down_hbm, down),
        (tiles_hbm, tiles),
        (dest_hbm, dest),
        (target_hbm, target),
    ]
    loads = [pltpu.make_async_copy(src, dst, load_sem.at[n]) for n, (src, dst) in enumerate(pairs)]
    for n in (7, 8, 0, 1, 3, 2):
        loads[n].start()

    def at_line(t):
        return plan.where(plan.line(me_z, t), me_j)

    def at_peer(u):
        return plan.where(me_z, plan.peer(me_j, u))

    steps = [(1, 0), (-1, 0), (0, 1), (0, -1), (0, 1), (0, -1), (0, 1), (0, -1)]

    def present(dx, dy):
        x = here_x + dx
        y = here_y + dy
        return (x >= 0) & (x < plan.width_x) & (y >= 0) & (y < plan.width_y)

    barrier = pltpu.get_barrier_semaphore()

    def greet(device):
        pl.semaphore_signal(barrier, inc=1, device_id=device, device_id_type=pl.DeviceIdType.MESH)

    for dx, dy in steps[:4]:

        @pl.when(present(dx, dy))
        def _():
            greet((here_x + dx, here_y + dy))

    for u in range(1, group):
        greet(at_peer(u))
    for t in plan.hops:
        greet(at_line(t))

    loads[7].wait()
    loads[8].wait()
    tables(plan, clusters, leaves, leaf_y, me_z, me_j, dest, target, dests, targets, tab_v, order_of)
    tab_copy = pltpu.make_async_copy(tab_v, tab, tab_sem)
    tab_copy.start()
    loads[0].wait()

    spans = []
    for here, width in ((here_x, plan.width_x), (here_y, plan.width_y)):
        spans.append((here > 0).astype(I32) + (here < width - 1).astype(I32))
    pl.semaphore_wait(barrier, spans[0] + spans[1] + group - 1 + len(plan.hops))

    def remote(src, dst, send, recv, device):
        return pltpu.make_async_remote_copy(
            src_ref=src,
            dst_ref=dst,
            send_sem=send,
            recv_sem=recv,
            device_id=device,
            device_id_type=pl.DeviceIdType.MESH,
        )

    def near_copy(n):
        dx, dy = steps[n]
        if dy == 0:
            src = vec.at[:, pl.ds(rows_x - LS if dx > 0 else 0, LS), :]
            dst = halo.at[0 if dx > 0 else 1]
        else:
            side = 1 if dy > 0 else 0
            if n < 4:
                src = strips.at[side]
                dst = rim.at[1 - side, pl.ds(1, leaf_x)]
            else:
                end = (n - 4) // 2
                src = corners.at[end, side]
                dst = rim.at[1 - side, end * (leaf_x + 1)]
        return remote(src, dst, near_send.at[n], near_recv.at[n], (here_x + dx, here_y + dy))

    def near_start(first, end):
        for n in range(first, end):

            @pl.when(present(*steps[n]))
            def _():
                near_copy(n).start()

    near_start(0, 2)

    wide[...] = vec[...].astype(F32)

    def to_grid(x, carry):
        plane = wide[:, x, :]
        lines_of = jnp.concatenate([plane, plane], axis=0).T.astype(BF16).reshape(leaf_y, LS, lanes)
        at = pl.multiple_of(lax.rem(x, LS) * LS, LS)
        grid[1 + lax.div(x, LS), 1 : 1 + leaf_y, pl.ds(at, LS), :] = lines_of
        return carry

    lax.fori_loop(0, rows_x, to_grid, 0, unroll=16)
    for side in range(2):
        for i in range(leaf_x):
            block = grid[1 + i, leaf_y if side else 1].reshape(2, LS // 2, LS, lanes)
            strips[side, i] = jnp.where(low, block[0], block[1])
    near_start(2, 4)

    loads[1].wait()

    def leaf_coef(m, carry):
        i = lax.div(m, leaf_y)
        j = lax.rem(m, leaf_y)
        coef[m] = dot(col[m], grid[1 + i, 1 + j])
        return carry

    lax.fori_loop(0, leaves, leaf_coef, 0, unroll=16)
    loads[2].wait()

    def upper_coef(p, carry):
        children = [i * leaf_y + 2 * p + q for i in range(leaf_x) for q in range(2)]
        left = jnp.concatenate([up[m] for m in children], axis=1)
        right = jnp.concatenate([coef[m] for m in children], axis=0)
        coef[leaves + p] = dot(left_of(left), right_of(right))
        return carry

    lax.fori_loop(0, uppers, upper_coef, 0, unroll=4)

    loads[3].wait()
    for n in (4, 5, 6):
        loads[n].start()

    def turn(r, carry):
        mats[:, r, :] = jnp.concatenate([coup[r], coup[r + half]], axis=0).T
        return carry

    lax.fori_loop(0, half, turn, 0, unroll=16)

    def contribute(first, count, m):
        left = jnp.concatenate(halves(mats[pl.ds(first, count)].reshape(count * half, lanes)), axis=1)
        high, rest = halves(twice(coef[m]))
        right = jnp.concatenate([jnp.concatenate([high, high], axis=0), jnp.concatenate([rest, jnp.zeros_like(rest)], axis=0)], axis=1)
        both = dot(left, right)
        blocks = (both[:, :lanes] + both[:, lanes:]).reshape(count, half, lanes)
        whole, scale = coded(blocks)
        held[pl.ds(first, count)] = whole
        for q in range(count):
            held_scale[pl.ds(first + q, 1), :] = scale[q : q + 1]

    def leaf_slots(m, carry):
        contribute(m * K0, K0, m)
        return carry

    def upper_slots(p, carry):
        contribute(leaves * K0 + p * K1, K1, leaves + p)
        return carry

    lax.fori_loop(0, leaves, leaf_slots, 0, unroll=16)
    lax.fori_loop(0, uppers, upper_slots, 0, unroll=4)

    tab_copy.wait()
    ordered = lax.dot_general(
        order_of[...], held_scale[...].astype(BF16), (((0,), (0,)), ((), ())), preferred_element_type=F32
    )
    send_scale[...] = ordered.astype(BF16).reshape(send_scale.shape)

    def scale_copy(u):
        return remote(
            send_scale.at[plan.peer(me_j, u)], got_scale.at[me_j], scale_send.at[u], scale_recv.at[u], at_peer(u)
        )

    def one_copy(t, u):
        return remote(
            send1.at[pl.ds((t * group + plan.peer(me_j, u)) * cap, cap)],
            recv1[t].at[pl.ds(me_j * cap, cap)],
            one_send.at[t, u],
            one_recv.at[t, u],
            at_peer(u),
        )

    def one_local(t):
        return pltpu.make_async_copy(
            send1.at[pl.ds((t * group + me_j) * cap, cap)], recv1[t].at[pl.ds(me_j * cap, cap)], local_sem.at[t]
        )

    scale_local = pltpu.make_async_copy(send_scale.at[me_j], got_scale.at[me_j], local_sem.at[lines])
    scale_local.start()
    for u in range(1, group):
        scale_copy(u).start()

    for t in plan.order:

        def put(p, carry, t=t):
            send1[t * plan.each + p] = held[tab[0, t * plan.each + p]]
            return carry

        lax.fori_loop(0, plan.each, put, 0, unroll=32)
        for u in range(1, group):
            one_copy(t, u).start()
        one_local(t).start()

    loads[4].wait()
    loads[5].wait()

    def turn_row(j, carry):
        pair = jnp.concatenate([row[j], row[leaf_y + j]], axis=0)
        basis = pair.astype(F32).T.astype(BF16)
        turned[j] = jnp.concatenate([basis, basis], axis=1)
        return carry

    lax.fori_loop(0, leaf_y, turn_row, 0, unroll=2)

    def lift(p, carry):
        parts = []
        for i in range(leaf_x):
            for q in range(2):
                mat = down[i * leaf_y + 2 * p + q]
                parts.append(jnp.concatenate([mat[:half], mat[half:]], axis=1))
        lifts[p] = left_of(jnp.concatenate(parts, axis=0))
        return carry

    lax.fori_loop(0, uppers, lift, 0, unroll=2)

    def near_field(first, count):
        def pair(j, carry):
            sums = []
            for i in range(leaf_x):
                m = i * leaf_y + j
                total = None
                for k in range(tiles.shape[1]):
                    o = off_ref[k, i, j]
                    term = dot(tiles[m, k], grid[i + lax.div(o, 3), j + lax.rem(o, 3)])
                    total = term if total is None else total + term
                sums.append(total)
            near[j] = jnp.where(low, sums[0], sums[1])
            return carry

        lax.fori_loop(first, first + count, pair, 0)

    def near_rows():
        for side in range(2):
            keep = present(2 * side - 1, 0)
            wide[:, side * LS : (side + 1) * LS, :] = jnp.where(keep, halo[side].astype(F32), 0.0)

        def to_rows(x, carry):
            plane = wide[:, x, :]
            lines_of = jnp.concatenate([plane, plane], axis=0).T.astype(BF16).reshape(leaf_y, LS, lanes)
            at = pl.multiple_of(lax.rem(x, LS) * LS, LS)
            grid[lax.div(x, LS) * (leaf_x + 1), 1 : 1 + leaf_y, pl.ds(at, LS), :] = lines_of
            return carry

        lax.fori_loop(0, 2 * LS, to_rows, 0, unroll=4)

    def near_wait(first, end):
        for n in range(first, end):

            @pl.when(present(-steps[n][0], -steps[n][1]))
            def _():
                near_copy(n).wait_recv()

    def near_corners():
        near_wait(0, 2)
        near_rows()
        for end in range(2):
            for side in range(2):
                block = grid[end * (leaf_x + 1), leaf_y if side else 1].reshape(2, LS // 2, LS, lanes)
                corners[end, side] = jnp.where(low, block[0], block[1])
        near_start(4, 8)

    def near_edges():
        near_wait(2, 8)
        loads[6].wait()
        for side in range(2):
            dy = 1 if side else -1
            for i in range(leaf_x + 2):
                dx = -1 if i == 0 else (1 if i == leaf_x + 1 else 0)
                keep = present(dx, dy)
                value = jnp.where(keep, rim[side, i].astype(F32), 0.0).reshape(points // 2, lanes)
                other = swapped(value)
                y = leaf_y + 1 if side else 0
                grid[i, y, : points // 2, :] = jnp.where(low, value, other).astype(BF16)
                grid[i, y, points // 2 :, :] = jnp.where(low, other, value).astype(BF16)

    scale_local.wait()
    for u in range(1, group):
        scale_copy(u).wait_recv()
    scale_of[...] = got_scale[...].astype(F32).reshape(scale_of.shape) * (1.0 / STEP)

    some = clusters // pieces

    def two_copy(t, h):
        return remote(
            send2.at[t - 1, pl.ds(h * some, some)],
            recv2[t - 1].at[pl.ds(h * some, some)],
            two_send.at[t, h],
            two_recv.at[t, h],
            at_line(plan.hop(t)),
        )

    def twos_copy(t, h):
        return remote(
            send2_scale.at[t - 1, h], recv2_scale[t - 1].at[h], twos_send.at[t, h], twos_recv.at[t, h], at_line(plan.hop(t))
        )

    def collect_all(t):
        one_local(t).wait()
        for u in range(1, group):
            one_copy(t, u).wait_recv()

        def collect(i, total):
            at = t * plan.each + i
            block = decoded(recv1[t][tab[1, at]]) * scale_of[tab[2, at]]
            total = total * tab[3, at].astype(F32) + block
            run[i] = total
            return total

        lax.fori_loop(0, plan.each, collect, jnp.zeros((half, lanes), F32), unroll=8)

        def pick(n, carry):
            own[n] = run[tab[4, t * KEYS + n]] * tab[5, t * KEYS + n].astype(F32)
            return carry

        lax.fori_loop(0, clusters, pick, 0, unroll=10)

    def merge(t, h):
        two_copy(t, h).wait_recv()
        twos_copy(t, h).wait_recv()
        place_scale[...] = recv2_scale[t - 1][h].astype(F32) * (1.0 / STEP)

        def gather(n, carry):
            own[h * some + n] = own[h * some + n] + decoded(recv2[t - 1][h * some + n]) * place_scale[pl.ds(n, 1), :]
            return carry

        lax.fori_loop(0, some, gather, 0, unroll=5)

    def pass_on(t, h):
        group_of = 5 if some % 5 == 0 else 1

        def pack(g, carry):
            first = h * some + g * group_of
            whole, scale = coded(own[pl.ds(first, group_of)])
            send2[t - 1, pl.ds(first, group_of)] = whole
            for q in range(group_of):
                place_scale[pl.ds(g * group_of + q, 1), :] = scale[q : q + 1]
            return carry

        lax.fori_loop(0, some // group_of, pack, 0, unroll=2)
        send2_scale[t - 1, h] = place_scale[...].astype(BF16)
        twos_copy(t, h).start()
        two_copy(t, h).start()

    def descend(p, carry):
        top = own[leaves + p]
        extra = dot(lifts[p], right_of(spread(top, top))).reshape(2 * leaf_x, half, lanes)
        for i in range(leaf_x):
            for q in range(2):
                m = leaf_x * (2 * p + q) + i
                own[m] = own[m] + extra[2 * i + q]
        return carry

    def out_copy(j):
        return pltpu.make_async_copy(near.at[j], out_hbm.at[j], out_sem.at[j])

    def far_field(first, end):
        for j in range(first, end):
            high, rest = halves(spread(own[leaf_x * j], own[leaf_x * j + 1]))
            near[j] = near[j] + dot(turned[j], jnp.concatenate([high, rest], axis=0))
            out_copy(j).start()

    place_scale[...] = jnp.zeros_like(place_scale)
    done = 0
    for step, t in enumerate(plan.order):
        collect_all(t)
        if t == 0:
            if step <= 2:
                near_corners()
            if step <= 3:
                near_edges()
            near_field(done, leaf_y - done)
        incoming = [other for other in plan.order if other and plan.into(other) == t]
        for h in range(pieces - 1, -1, -1):
            for other in sorted(incoming):
                merge(other, h)
            if t:
                pass_on(t, h)
            else:
                if h == pieces - 1:
                    lax.fori_loop(0, uppers, descend, 0, unroll=4)
                    left = leaf_y
                whole = -(-h * some // leaf_x)
                far_field(whole, left)
                left = min(whole, left)
        if step == 2 and t:
            near_corners()
        if step == 3 and t:
            near_edges()
        if step >= 3 and t:
            count = min(-(-leaf_y // max(lines - 3, 1)), leaf_y - done)
            near_field(done, count)
            done += count

    for j in range(leaf_y):
        out_copy(j).wait()

    for n in range(8):

        @pl.when(present(*steps[n]))
        def _():
            near_copy(n).wait_send()

    for u in range(1, group):
        scale_copy(u).wait_send()
        for t in range(lines):
            one_copy(t, u).wait_send()
    for t in range(1, lines):
        for h in range(pieces):
            two_copy(t, h).wait_send()
            twos_copy(t, h).wait_send()


def turn_out(sum_ref, out_ref):
    vecs = out_ref.shape[0]
    for x in range(out_ref.shape[2]):
        line = sum_ref[:, x * LS : (x + 1) * LS, :].reshape(out_ref.shape[3], 2 * vecs).T
        out_ref[:, 0, x, :] = line[:vecs]
        out_ref[:, 1, x, :] = line[vecs:]


def body(
    vectors,
    near_tiles,
    near_offset,
    col_basis,
    row_basis,
    up_transfer,
    down_transfer,
    coupling,
    couple_dest,
    couple_target,
):
    vecs, rows_x, rows_y = vectors.shape
    leaf_x, leaf_y = rows_x // LS, rows_y // LS
    leaves = leaf_x * leaf_y
    uppers = leaf_y // 2
    clusters = leaves + uppers
    rank = coupling.shape[2]
    half = rank // 2
    slots = coupling.shape[1]
    near_count = near_tiles.shape[2]
    points = LS * LS
    lanes = 2 * vecs
    plan = Plan(lax.axis_size("qx"), lax.axis_size("qy"), slots)
    lines, group, cap = plan.lines, plan.group, plan.cap
    pieces = 2 if clusters % 2 == 0 else 1
    scale2 = -(-(clusters // pieces) // 16) * 16
    devices = couple_dest.shape[0]
    width = max(plan.total, lines * KEYS)
    vmem, dma = pltpu.VMEM, pltpu.SemaphoreType.DMA
    int16 = jnp.int16
    scratch = [
        vmem((vecs, rows_x, rows_y), BF16),
        vmem((leaves, near_count, points, points), BF16),
        vmem((leaves, rank, points), BF16),
        vmem((leaves, rank, points), BF16),
        vmem((leaves, rank, rank), F32),
        vmem((leaves, rank, rank), F32),
        vmem((rank, rank, slots), F32),
        vmem((vecs, rows_x, rows_y), F32),
        vmem((2, vecs, LS, rows_y), BF16),
        vmem((leaf_x + 2, leaf_y + 2, points, lanes), BF16),
        vmem((2, leaf_x, LS // 2, LS, lanes), BF16),
        vmem((2, 2, LS // 2, LS, lanes), BF16),
        vmem((2, leaf_x + 2, LS // 2, LS, lanes), BF16),
        vmem((slots, half, lanes), F32),
        vmem((clusters, rank, lanes), F32),
        vmem((slots, half, lanes), int16),
        vmem((slots, lanes), F32),
        vmem((scale2, lanes), F32),
        vmem((group, plan.scale_rows, lanes), BF16),
        vmem((group, plan.scale_rows, lanes), BF16),
        vmem((group * plan.scale_rows, 1, lanes), F32),
        vmem((plan.total, half, lanes), int16),
        vmem((devices, slots), I32),
        vmem((devices, slots), I32),
        vmem((group, slots), I32),
        vmem((group, slots), F32),
        vmem((8, width), I32),
        vmem((slots, group * plan.scale_rows), BF16),
        pltpu.SMEM((8, width), I32),
        vmem((plan.each, half, lanes), F32),
        vmem((clusters, half, lanes), F32),
        vmem((max(lines - 1, 1), clusters, half, lanes), int16),
        vmem((max(lines - 1, 1), pieces, scale2, lanes), BF16),
        vmem((leaf_y, points, lanes), F32),
        vmem((leaf_y, points, 4 * rank), BF16),
        vmem((uppers, 2 * leaf_x * half, 6 * rank), BF16),
        dma((9,)),
        dma(()),
        dma((8,)),
        dma((8,)),
        dma((group,)),
        dma((group,)),
        dma((lines, group)),
        dma((lines, group)),
        dma((lines, pieces)),
        dma((lines, pieces)),
        dma((lines, pieces)),
        dma((lines, pieces)),
        dma((lines + 1,)),
        dma((leaf_y,)),
    ]
    scratch += [vmem((plan.each, half, lanes), int16)] * lines
    scratch += [vmem((clusters, half, lanes), int16)] * (lines - 1)
    scratch += [vmem((pieces, scale2, lanes), BF16)] * (lines - 1)
    summed = pl.pallas_call(
        lambda *refs: kernel(plan, *refs),
        out_shape=jax.ShapeDtypeStruct((leaf_y, points, lanes), F32),
        in_specs=[ANY, ANY, SM, ANY, ANY, ANY, ANY, ANY, ANY, ANY],
        out_specs=ANY,
        scratch_shapes=scratch,
        compiler_params=pltpu.CompilerParams(collective_id=0, has_side_effects=True, vmem_limit_bytes=60 << 20),
        name="product",
    )(
        vectors,
        near_tiles.reshape(leaves, near_count, points, points),
        near_offset.transpose(2, 0, 1),
        col_basis.reshape(leaves, rank, points),
        row_basis.reshape(leaves, rank, points),
        up_transfer.reshape(leaves, rank, rank),
        down_transfer.reshape(leaves, rank, rank),
        coupling[0].transpose(1, 2, 0),
        couple_dest,
        couple_target,
    )
    cuts = 2
    part = LS // cuts
    turned = pl.pallas_call(
        turn_out,
        grid=(cuts,),
        out_shape=jax.ShapeDtypeStruct((vecs, leaf_x, LS, rows_y), F32),
        in_specs=[pl.BlockSpec((leaf_y, part * LS, lanes), lambda n: (0, n, 0))],
        out_specs=pl.BlockSpec((vecs, leaf_x, part, rows_y), lambda n: (0, 0, n, 0)),
        name="turn",
    )(summed)
    return turned.reshape(vecs, rows_x, rows_y)


def solution(mesh):
    return jax.shard_map(
        body,
        mesh=mesh,
        in_specs=(
            P(None, "qx", "qy"),
            P("qx", "qy", None, None, None),
            P("qx", "qy", None),
            P("qx", "qy", None, None),
            P("qx", "qy", None, None),
            P("qx", "qy", None, None),
            P("qx", "qy", None, None),
            P(("qx", "qy"), None, None, None),
            P(),
            P(),
        ),
        out_specs=P(None, "qx", "qy"),
        check_vma=False,
    )
```
